128 devices in a mesh: row: 8 (over x, core), col: 16 (over y, z).
Axes of the slice: x: 4, y: 4, z: 4, core: 2. Of those that a mesh axis runs over, the one named last changes fastest.
Arguments:
- centroid: float32 [3, 131072], P(None, ('row', 'col')), may hold values from -6 to 6
- normals: float32 [3, 131072], P(None, ('row', 'col')), may hold values from -3 to 3
- tangent: float32 [3, 131072], P(None, ('row', 'col')), may hold values from -3 to 3
- element_area: float32 [131072], P(('row', 'col')), may hold values from 0.01 to 0.04
- forward_field: float32 [2, 131072], P(None, ('row', 'col')), may hold values from -6 to 6
- adjoint_field: float32 [2, 131072], P(None, ('row', 'col')), may hold values from -6 to 6
- corners: int32 [3, 131072], P(None, ('row', 'col')), may hold values from 0 to 65535, as said below
- slot_map: int32 [65536], replicated, may hold values from 0 to 65535, as said below
- quad_order: int32 [128, 8, 16, 8], P('row', None, 'col'), may hold values from 0 to 2
- morph_modes: float32 [300, 6, 65536], P(None, None, ('row', 'col')), may hold values from -0.3 to 0.3
Outputs:
- vertex_partial: float32 [6, 65536], P(None, ('row', 'col'))
- mode_gradient: float32 [300], replicated
The draws below stay inside these ranges and needn't reach their ends.
Inputs may be any that keep to these rules, and one draw needn't show every extreme that they name: slot_map is a permutation of 0 to 65535. `corners`: for each shard of elements (elements b * 1024 to (b + 1) * 1024 - 1), its 3072 corner references map through slot_map onto the slots of any one patch at most 24 times, and exactly 24 times for some patch.
All inputs are finite; a program needn't handle non-finite values.
Results may differ from the reference program's by a relative error of at most 0.0003.
Values sent between devices are 32-bit elements; how exact they have to be, the bound alone decides.
A program may use at most 128 MiB of HBM per device.

```python
import math
import jax
import jax.numpy as jnp
from jax import lax

E = 131072
V = 65536
MODES = 300
TC = 128
SLAB_DEV = 8
EL = 1024
SLAB = 1024
TILES = 8
N_ROW = 8
N_COL = 16
DEVICES = 128


def joint_layout(key):
    base_key = jax.random.fold_in(key, 7331)
    slot_key = jax.random.fold_in(base_key, 1)
    owner_key = jax.random.fold_in(base_key, 2)
    inside_key = jax.random.fold_in(base_key, 3)
    slot_table = jax.random.permutation(slot_key, V).astype(jnp.int32)
    shard_count = E // EL
    shard_keys = jax.random.split(owner_key, shard_count)

    def shard_owners(shard_key):
        order = jax.random.permutation(shard_key, shard_count).astype(jnp.int32)
        return order[jnp.arange(3 * EL, dtype=jnp.int32) % shard_count]
    owner_ids = jax.vmap(shard_owners)(shard_keys)
    inside_ids = jax.random.randint(inside_key, (shard_count, 3 * EL), 0, V // shard_count, dtype=jnp.int32)
    wanted_slot = owner_ids * (V // shard_count) + inside_ids
    inverse_table = jnp.argsort(slot_table, stable=True).astype(jnp.int32)
    vertex_ids = inverse_table[wanted_slot]
    corner_table = jnp.transpose(vertex_ids.reshape(shard_count, 3, EL), (1, 0, 2)).reshape(3, E)
    return (corner_table.astype(jnp.int32), slot_table)


def draw_corners(key, part):
    corner_table, slot_table = joint_layout(key)
    return corner_table


def draw_slot_map(key, part):
    corner_table, slot_table = joint_layout(key)
    return slot_table


def touch_ends(entries, stream_key, least, largest):
    index_at = [jax.random.randint(jax.random.fold_in(stream_key, axis), (), 0, length) for axis, length in enumerate(entries.shape)]
    main_axis = entries.shape.index(max(entries.shape))
    beside = index_at[:main_axis] + [(index_at[main_axis] + 1) % entries.shape[main_axis]] + index_at[main_axis + 1:]
    return entries.at[tuple(index_at)].set(least).at[tuple(beside)].set(largest)


def block_scale(rng, extent, shards, low, top_value):
    loudness, own = 1.0, jax.random.fold_in(rng, 6)
    for dim, parts in shards:
        draws = jnp.exp(jax.random.uniform(jax.random.fold_in(own, dim), (parts,), jnp.float32, low / len(shards), top_value / len(shards)))
        loudness = loudness * jnp.repeat(draws, extent[dim] // parts).reshape([-1 if axis == dim else 1 for axis in range(len(extent))])
    return loudness


def scatter_about(key, extent, width, most, pieces=(), kind=jnp.bfloat16):
    level = block_scale(key, extent, pieces, -0.22, 0.18) if pieces else 1.0
    values = jax.random.normal(key, extent, jnp.float32) * width * level
    return jnp.minimum(jnp.maximum(values, -most), most).astype(kind)


def setup_inputs(seed: int = 0) -> dict:
    seeds = jax.random.split(jax.random.key(seed), 11)
    return {
        "centroid": scatter_about(seeds[0], (3, E), 1.0, 6.0, ((1, 128),), jnp.float32),
        "normals": scatter_about(seeds[1], (3, E), 0.577, 3.0, ((1, 128),), jnp.float32),
        "tangent": scatter_about(seeds[2], (3, E), 0.577, 3.0, ((1, 128),), jnp.float32),
        "element_area": jnp.clip(jnp.exp(math.log(0.04) - 1.3862944 * jax.random.uniform(seeds[3], (E,), jnp.float32) ** block_scale(seeds[3], (E,), ((0, 128),), -0.2, 0.2)), 0.01, 0.04),
        "forward_field": scatter_about(seeds[4], (2, E), 1.0, 6.0, ((1, 128),), jnp.float32),
        "adjoint_field": scatter_about(seeds[5], (2, E), 1.0, 6.0, ((1, 128),), jnp.float32),
        "corners": draw_corners(jax.random.fold_in(seeds[10], 71), 0),
        "slot_map": draw_slot_map(jax.random.fold_in(seeds[10], 71), 0),
        "quad_order": touch_ends(jax.random.randint(seeds[8], (DEVICES, N_ROW, N_COL, TILES), 0, 3), jax.random.fold_in(seeds[8], 1), 0, 2).astype(jnp.int32),
        "morph_modes": scatter_about(seeds[9], (MODES, 6, V), 0.05, 0.3, ((2, 128),), jnp.float32),
    }


wavenumber = 4.0
quad_offsets = (-0.6, 0.0, 0.6)
quad_table = ((0.0, 1.0, 0.0), (0.5, 0.0, 0.5), (1.0 / 3.0, 1.0 / 3.0, 1.0 / 3.0))

def point_weights(pair_flags, point_index):
    weight_sum = jnp.zeros(pair_flags.shape, jnp.float32)
    for flag_level in range(3):
        chosen = jnp.where(pair_flags == flag_level, quad_table[flag_level][point_index], 0.0)
        weight_sum = weight_sum + chosen.astype(jnp.float32)
    return weight_sum

def pair_terms(row_point, row_adjoint, col_point, col_normal, col_tangent, col_area, col_forward, pair_flags):
    row_count = row_point.shape[1]
    col_count = col_point.shape[1]
    row_total = jnp.zeros((3, row_count), jnp.float32)
    col_total = jnp.zeros((3, col_count), jnp.float32)
    normal_total = jnp.zeros((3, col_count), jnp.float32)
    real_coupling = row_adjoint[0][:, None] * col_forward[0][None, :] + row_adjoint[1][:, None] * col_forward[1][None, :]
    imag_coupling = row_adjoint[0][:, None] * col_forward[1][None, :] - row_adjoint[1][:, None] * col_forward[0][None, :]
    spread = jnp.sqrt(col_area)
    for point_index in range(3):
        weight = point_weights(pair_flags, point_index) * col_area[None, :]
        source = col_point + quad_offsets[point_index] * spread[None, :] * col_tangent
        offset = row_point[:, :, None] - source[:, None, :]
        radius_sq = lax.optimization_barrier(jnp.sum(offset * offset, axis=0)) + col_area[None, :]
        radius = jnp.sqrt(radius_sq)
        phase_arg = wavenumber * radius
        cosine = jnp.cos(phase_arg)
        sine_part = jnp.sin(phase_arg)
        scale_three = 1.0 / (4.0 * math.pi * radius * radius_sq)
        scale_five = scale_three / radius_sq
        first_real = (-cosine - phase_arg * sine_part) * scale_three
        first_imag = (-sine_part + phase_arg * cosine) * scale_three
        poly_real = 3.0 - phase_arg * phase_arg
        poly_imag = -3.0 * phase_arg
        second_real = (cosine * poly_real - sine_part * poly_imag) * scale_five
        second_imag = (sine_part * poly_real + cosine * poly_imag) * scale_five
        along_normal = lax.optimization_barrier(jnp.sum(offset * col_normal[:, None, :], axis=0))
        combo_real = -first_imag / wavenumber - second_real * along_normal
        combo_imag = first_real / wavenumber - second_imag * along_normal
        coeff_first = (real_coupling * first_real - imag_coupling * first_imag) * weight
        coeff_second = (real_coupling * combo_real - imag_coupling * combo_imag) * weight
        position = coeff_second[None] * offset - coeff_first[None] * col_normal[:, None, :]
        row_total = row_total + lax.optimization_barrier(jnp.sum(position, axis=2))
        col_total = col_total - lax.optimization_barrier(jnp.sum(position, axis=1))
        normal_total = normal_total - lax.optimization_barrier(jnp.sum(coeff_first[None] * offset, axis=1))
    return (row_total, col_total, normal_total)

def reference(centroid, normals, tangent, element_area, forward_field, adjoint_field, corners, slot_map, quad_order, morph_modes):
    device_count = N_ROW * N_COL
    slab_index = (jnp.arange(device_count, dtype=jnp.int32)[:, None] * EL + jnp.arange(SLAB_DEV, dtype=jnp.int32)[None, :]).reshape(-1)
    row_point = centroid[:, slab_index]
    row_adjoint = adjoint_field[:, slab_index]

    def visit_block(row_carry, shard_index):
        col_start = (shard_index * EL).astype(jnp.int32)
        col_point = lax.dynamic_slice_in_dim(centroid, col_start, EL, 1)
        col_normal = lax.dynamic_slice_in_dim(normals, col_start, EL, 1)
        col_tangent = lax.dynamic_slice_in_dim(tangent, col_start, EL, 1)
        col_area = lax.dynamic_slice_in_dim(element_area, col_start, EL, 0)
        col_forward = lax.dynamic_slice_in_dim(forward_field, col_start, EL, 1)
        tile_flags = quad_order[:, shard_index // N_COL, shard_index % N_COL, :]
        pair_flags = jnp.repeat(jnp.repeat(tile_flags, SLAB_DEV, axis=0), TC, axis=1)
        row_total, col_total, normal_total = pair_terms(row_point, row_adjoint, col_point, col_normal, col_tangent, col_area, col_forward, pair_flags)
        return (row_carry + row_total, jnp.concatenate([col_total, normal_total], axis=0))
    row_sum, col_parts = lax.scan(visit_block, jnp.zeros((3, SLAB), jnp.float32), jnp.arange(device_count, dtype=jnp.int32))
    col_whole = jnp.transpose(col_parts, (1, 0, 2)).reshape(6, E)
    row_whole = jnp.pad(row_sum.reshape(3, device_count, SLAB_DEV), ((0, 3), (0, 0), (0, EL - SLAB_DEV))).reshape(6, E)
    element_part = col_whole + row_whole
    slot_ids = slot_map[corners].reshape(-1)
    values = jnp.concatenate([(element_part / 3.0).T] * 3, axis=0)
    vertex_partial = jax.ops.segment_sum(values, slot_ids, num_segments=V).T
    mode_gradient = jnp.dot(morph_modes.reshape(MODES, 6 * V), vertex_partial.reshape(6 * V), precision=lax.Precision.HIGHEST)
    return (vertex_partial, mode_gradient)
```

```python
import math, functools
import jax, jax.numpy as jnp
from jax import lax
from jax.experimental import pallas as pl
from jax.experimental.pallas import tpu as pltpu

F32 = jnp.float32
MAGIC = 12582912.0
INV_TURN = 1.0 / (2.0 * math.pi)
SIN_C = (4.442883014678955, -7.308245658874512, 3.6063544750213623, -0.8461129069328308, 0.10982698947191238)
COS_C = (1.4142135381698608, -6.978850841522217, 5.7394609451293945, -1.8835630416870117, 0.31069818139076233)


def horner(coeffs, z):
    total = z * coeffs[-1] + coeffs[-2]
    for value in coeffs[-3::-1]:
        total = total * z + value
    return total


def green(r2, cr, ci):
    inv = lax.rsqrt(r2)
    phi = r2 * inv
    turn = phi * INV_TURN
    frac = turn - ((turn + MAGIC) - MAGIC)
    z = frac * frac
    hs = frac * horner(SIN_C, z)
    hc = horner(COS_C, z)
    cosine = 1.0 - hs * hs
    sine = hs * hc
    er = cr * cosine - ci * sine
    ei = cr * sine + ci * cosine
    i2 = inv * inv
    i3 = i2 * inv
    g = er + phi * ei
    h = ei - phi * er
    k = g * (3.0 * i2) - er
    return g, h, k, i3


def tile_terms(kind, row, col, cr_scale, ci_scale):
    x, y, z, ar, ai = row
    dx, dy, dz = x - col["y"][0], y - col["y"][1], z - col["y"][2]
    d = (dx, dy, dz)
    nx, ny, nz = col["n"]
    mn = dx * nx + dy * ny + dz * nz
    sq = dx * dx + dy * dy + dz * dz
    cr = ar * cr_scale + ai * ci_scale
    ci = ar * ci_scale - ai * cr_scale
    out = {}
    sa = sb = None
    if kind != 0:
        ex, ey, ez = col["t2"]
        e = dx * ex + dy * ey + dz * ez
        b = sq + col["at"]
        pts = []
        for sign in (-1, 1):
            if sign > 0:
                r2, m = b - e, mn - col["tn"]
            else:
                r2, m = b + e, mn + col["tn"]
            g, h, k, i3 = green(r2, cr, ci)
            pts.append((i3 * g, i3 * (h - m * k)))
        (a0, b0), (a2, b2) = pts
        sa, sb, da, db = a0 + a2, b0 + b2, a2 - a0, b2 - b0
    if kind != 1:
        g, h, k, i3 = green(sq + col["a"], cr, ci)
        a1, b1 = i3 * g, i3 * (h - mn * k)
        sa, sb = (a1, b1) if sa is None else (sa + a1, sb + b1)
    bd = [sb * v for v in d]
    ad = [sa * v for v in d]
    an = [sa * v for v in (nx, ny, nz)]
    pos = [p + q for p, q in zip(bd, an)]
    if kind == 0:
        return pos, pos, ad, None
    ts = col["ts"]
    pos = [p - db * t for p, t in zip(pos, ts)]
    return pos, pos, ad, da


def pair_kernel(batches, groups, lists_ref, rows_ref, cen_ref, nor_ref, tan_ref, area_ref, fwd_ref, col_out, row_out, table, racc, ctab):
    tiles = lists_ref.shape[0]
    rt = jnp.transpose(rows_ref[...])
    for g in range(groups):
        for q in range(5):
            v = jnp.broadcast_to(rt[q * 8:(q + 1) * 8, g:g + 1], (8, 128))
            table[g, q] = v * 4.0 if q < 3 else v
    table[groups] = jnp.concatenate([jnp.full((3, 8, 128), 1.0, F32), jnp.zeros((2, 8, 128), F32)], axis=0)
    racc[...] = jnp.zeros(racc.shape, F32)
    area = area_ref[...]
    spread = jnp.sqrt(area) * 2.4
    ysc = 4.0 * cen_ref[...]
    n16 = 16.0 * nor_ref[...]
    ts = spread * tan_ref[...]
    a16 = 16.0 * area
    at = a16 + jnp.sum(ts * ts, axis=0, keepdims=True)
    tn = jnp.sum(ts * n16, axis=0, keepdims=True)
    fw = fwd_ref[...] * (area * (1.0 / math.pi))
    rows = [ysc, n16, ts, 2.0 * ts, a16, at, tn, fw]
    pos = 0
    for r in rows:
        ctab[pos:pos + r.shape[0], :] = r
        pos += r.shape[0]

    def tile_body(t, _):
        lanes = pl.ds(pl.multiple_of(t * 128, 128), 128)

        def bc(i):
            return jnp.broadcast_to(ctab[i:i + 1, lanes], (8, 128))

        def getcol():
            return dict(y=[bc(0), bc(1), bc(2)], n=[bc(3), bc(4), bc(5)], ts=[bc(6), bc(7), bc(8)],
                        t2=[bc(9), bc(10), bc(11)], a=bc(12), at=bc(13), tn=bc(14))
        zero = jnp.zeros((8, 128), F32)
        n0, n1, n2 = lists_ref[t, 253], lists_ref[t, 254], lists_ref[t, 255]
        b0, b1, b2 = batches
        s0 = 0
        s1 = n0 * b0
        s2 = s1 + n1 * b1
        carry = (zero,) * 7

        def make(kind, size, start, weight):
            def body(it, acc):
                col = getcol()
                frs, fis = bc(15) * weight, bc(16) * weight
                acc = list(acc)
                ids, news = [], []
                for j in range(size):
                    g = lists_ref[t, start + it * size + j]
                    row = [table[g, q] for q in range(5)]
                    pos, cpos, ad, da = tile_terms(kind, row, col, frs, fis)
                    for q in range(3):
                        acc[q] = acc[q] + pos[q]
                        acc[3 + q] = acc[3 + q] + ad[q]
                    if da is not None:
                        acc[6] = acc[6] + da
                    ids.append(g)
                    news.append(pos)
                olds = [[racc[g, q] for q in range(3)] for g in ids]
                for g, old, new in zip(ids, olds, news):
                    for q in range(3):
                        racc[g, q] = old[q] + new[q]
                return tuple(acc)
            return body
        carry = lax.fori_loop(0, n0, make(0, b0, s0, 1.0), carry)
        carry = lax.fori_loop(0, n1, make(1, b1, s1, 0.5), carry)
        carry = lax.fori_loop(0, n2, make(2, b2, s2, 1.0 / 3.0), carry)
        sums = [jnp.sum(v, axis=0, keepdims=True) for v in carry]
        for q in range(3):
            col_out[q:q + 1, lanes] = -sums[q]
            tsr = ctab[6 + q:7 + q, lanes]
            col_out[3 + q:4 + q, lanes] = 4.0 * (sums[3 + q] - sums[6] * tsr)
        return 0

    lax.fori_loop(0, tiles, tile_body, 0)
    lane = lax.broadcasted_iota(jnp.int32, (8, 128), 1)
    outs = [jnp.zeros((8, 128), F32) for _ in range(3)]
    for g in range(groups):
        for q in range(3):
            s = jnp.sum(racc[g, q], axis=1, keepdims=True)
            outs[q] = jnp.where(lane == g, s, outs[q])
    full = jnp.concatenate(outs + [jnp.zeros((104, 128), F32)], axis=0)
    row_out[...] = jnp.transpose(full)


def pair_call(lists, rows, cen, nor, tan, area, fwd, batches=(8, 4, 4)):
    el = cen.shape[1]
    groups = rows.shape[0]
    vm = pl.BlockSpec(memory_space=pltpu.VMEM)
    return pl.pallas_call(
        functools.partial(pair_kernel, batches, groups),
        out_shape=(jax.ShapeDtypeStruct((6, el), F32), jax.ShapeDtypeStruct((128, 128), F32)),
        in_specs=[pl.BlockSpec(memory_space=pltpu.SMEM)] + [vm] * 6,
        out_specs=(vm, vm),
        scratch_shapes=[pltpu.VMEM((groups + 1, 5, 8, 128), F32), pltpu.VMEM((groups + 1, 3, 8, 128), F32),
                        pltpu.VMEM((24, el), F32)],
        name="pairs",
    )(lists, rows, cen, nor, tan, area, fwd)


def dot_nn(a, b):
    return lax.dot_general(a, b, (((1,), (0,)), ((), ())), preferred_element_type=F32)


def dot_nt(a, b):
    return lax.dot_general(a, b, (((1,), (1,)), ((), ())), preferred_element_type=F32)


def iota(shape, dim):
    return lax.broadcasted_iota(jnp.int32, shape, dim)


BF16 = jnp.bfloat16


def split3(v):
    hi = v.astype(BF16)
    rest = v - hi.astype(F32)
    mid = rest.astype(BF16)
    low = (rest - mid.astype(F32)).astype(BF16)
    return hi, mid, low


def ones_where(mask):
    return jnp.where(mask, 1.0, 0.0)


def make_lists(flags, batches):
    l0, l1 = iota((128, 128), 0), iota((128, 128), 1)
    same = (l0 & 7) == (l1 & 7)
    before = ones_where(same & (l0 < l1)).astype(BF16)
    same = ones_where(same).astype(BF16)
    lower = ones_where(iota((8, 8), 0) > iota((8, 8), 1)).astype(BF16)
    lane = iota((8, 128), 1)
    tile = iota((8, 128), 0)
    pick = ones_where(lane == tile).astype(BF16)
    pos = jnp.zeros((8, 128), F32)
    base = jnp.zeros((8, 128), F32)
    counts = []
    for kind in range(3):
        mask = ones_where(flags == float(kind))
        mb = mask.astype(BF16)
        rowtot = dot_nn(mb, same)
        inside = dot_nn(mb, before) + dot_nn(lower, rowtot.astype(BF16))
        total = jnp.sum(rowtot, axis=0, keepdims=True) + jnp.zeros((8, 128), F32)
        pos = pos + mask * (inside + base)
        nb = jnp.floor((total + float(batches[kind] - 1)) * (1.0 / batches[kind]))
        base = base + nb * float(batches[kind])
        counts.append(dot_nt(pick, nb.astype(BF16))[:, 0:1])
    posi = pos.astype(jnp.int32)
    slot = iota((256, 128), 0)
    out = jnp.zeros((8, 256), F32)
    for r in range(8):
        hit = ones_where(slot == posi[r:r + 1, :]).astype(BF16)
        value = jnp.where((lane & 7) == tile, ((lane >> 3) * 8 + (r - 128)).astype(F32), 0.0).astype(BF16)
        out = out + dot_nt(value, hit)
    out = out + 128.0
    wide = iota((8, 256), 1)
    for kind in range(3):
        out = jnp.where(wide == 253 + kind, counts[kind], out)
    return out.astype(jnp.int32)


def lookup_slots(table, corners):
    parts = jnp.concatenate([(table >> 8).astype(F32).astype(BF16), (table & 255).astype(F32).astype(BF16)], axis=1)
    width = 256
    lo_iota = iota((128, width), 0)
    hi_iota = iota((512, width), 0)
    rows = []
    for n in range(corners.shape[0]):
        pieces = []
        for cb in range(corners.shape[1] // width):
            v = corners[n:n + 1, cb * width:(cb + 1) * width]
            hit = lo_iota == (v & 127)
            rhs = jnp.concatenate([jnp.where(hit, 256.0, 0.0), jnp.where(hit, 1.0, 0.0)], axis=0).astype(BF16)
            sel = dot_nn(parts, rhs)
            pieces.append(jnp.sum(jnp.where(hi_iota == (v >> 7), sel, 0.0), axis=0, keepdims=True))
        rows.append(jnp.concatenate(pieces, axis=1))
    return jnp.concatenate(rows, axis=0).astype(jnp.int32)


def patch_ranks(patches):
    width = 256
    before = ones_where(iota((width, width), 0) < iota((width, width), 1)).astype(BF16)
    sub = iota((128, width), 0)
    carry = jnp.zeros((128, 1), F32)
    rows = []
    for n in range(patches.shape[0]):
        pieces = []
        for cb in range(patches.shape[1] // width):
            hit = ones_where(sub == patches[n:n + 1, cb * width:(cb + 1) * width])
            earlier = dot_nn(hit.astype(BF16), before) + carry
            pieces.append(jnp.sum(hit * earlier, axis=0, keepdims=True))
            carry = carry + jnp.sum(hit, axis=1, keepdims=True)
        rows.append(jnp.concatenate(pieces, axis=1))
    return jnp.concatenate(rows, axis=0)


def fill_buckets(values, slots, ranks):
    width = 256
    sub = iota((128, width), 0)
    rank_of_row = iota((192, width), 0) >> 3
    send = jnp.zeros((128, 192), F32)
    for n in range(slots.shape[0]):
        for cb in range(slots.shape[1] // width):
            cols = slice(cb * width, (cb + 1) * width)
            s = slots[n:n + 1, cols]
            hit = ones_where(sub == (s >> 9)).astype(BF16)
            eight = jnp.concatenate([values[:, cols], (s & 511).astype(F32), jnp.zeros((1, width), F32)], axis=0)
            mine = rank_of_row == ranks[n:n + 1, cols].astype(jnp.int32)
            for part in split3(eight):
                rhs = jnp.where(mine, jnp.concatenate([part.astype(F32)] * 24, axis=0), 0.0).astype(BF16)
                send = send + dot_nt(hit, rhs)
    return jnp.concatenate([send, jnp.zeros((128, 64), F32)], axis=1)


def add_up(recv):
    turned = jnp.transpose(recv)
    sub = iota((512, 128), 0).astype(F32)
    total = jnp.zeros((24, 512), F32)
    for pair in range(12):
        parts, hits = [], []
        for q in (2 * pair, 2 * pair + 1):
            eight = turned[q * 8:(q + 1) * 8, :]
            hits.append(ones_where(sub == eight[6:7, :]).astype(BF16))
            parts.append(jnp.concatenate([p.astype(F32) for p in split3(eight)], axis=0))
        lhs = jnp.concatenate(parts, axis=1).astype(BF16)
        total = total + dot_nt(lhs, jnp.concatenate(hits, axis=1))
    return total[0:8] + total[8:16] + total[16:24]


def lists_kernel(flags_ref, out_ref):
    out_ref[...] = make_lists(flags_ref[...], BATCHES)


def slots_kernel(table_ref, corners_ref, slots_ref, ranks_ref):
    slots = lookup_slots(table_ref[...], corners_ref[...])
    slots_ref[...] = slots
    ranks_ref[...] = patch_ranks(slots >> 9)


def bucket_kernel(values_ref, slots_ref, ranks_ref, out_ref):
    out_ref[...] = fill_buckets(values_ref[...], slots_ref[...], ranks_ref[...])


def project(modes_ref, vertex, acc_ref):
    count = modes_ref.shape[0]
    step = 10

    def visit(i, _):
        block = pl.ds(i * step, step)
        s = sum(modes_ref[block, :, k * 128:(k + 1) * 128] * vertex[None, 0:6, k * 128:(k + 1) * 128] for k in range(4))
        folded = jnp.sum(s, axis=1)
        acc_ref[block, :] = folded
        return 0
    lax.fori_loop(0, count // step, visit, 0, unroll=False)
    ones = jnp.ones((8, 128), BF16)
    return sum(dot_nt(ones, p) for p in split3(acc_ref[...]))


def vertex_kernel(recv_ref, modes_ref, vertex_ref, grad_ref, acc_ref):
    vertex = add_up(recv_ref[...])
    vertex_ref[...] = vertex[0:6]
    grad_ref[...] = project(modes_ref, vertex, acc_ref)[0:1]


VM = pl.BlockSpec(memory_space=pltpu.VMEM)
SLAB_DEV = 8
BATCHES = (8, 4, 4)


def simple(kernel, shapes, name, *args, scratch=()):
    return pl.pallas_call(kernel, out_shape=shapes, in_specs=[VM] * len(args),
                          out_specs=jax.tree.map(lambda _: VM, shapes), scratch_shapes=scratch, name=name)(*args)


S = jax.ShapeDtypeStruct
I32 = jnp.int32


def body(centroid, normals, tangent, element_area, forward_field, adjoint_field, corners, slot_map, quad_order, morph_modes):
    el = centroid.shape[1]
    slab = jnp.concatenate([centroid[:, :8], adjoint_field[:, :8]], axis=0).reshape(1, 40)
    slab = jnp.pad(slab, ((0, 0), (0, 88)))
    rows = lax.all_gather(slab, ("row", "col"), axis=0, tiled=True)
    rows = rows.reshape(8, 16, 128).transpose(1, 0, 2).reshape(128, 128)
    flags = quad_order[:, :, 0, :].transpose(1, 0, 2).reshape(8, 128).astype(F32)
    flags = lax.all_to_all(flags, "row", 0, 0, tiled=True)
    lists = simple(lists_kernel, S((8, 256), I32), "lists", flags)
    col_part, row_part = pair_call(lists, rows, centroid, normals, tangent, element_area[None, :], forward_field, BATCHES)
    row_part = row_part.reshape(16, 8, 128).transpose(1, 0, 2).reshape(128, 128)
    own = jnp.sum(lax.all_to_all(row_part, ("row", "col"), 0, 0, tiled=True), axis=0)[:24].reshape(3, 8)
    element_part = col_part + jnp.pad(own, ((0, 3), (0, el - 8)))
    slots, ranks = simple(slots_kernel, (S((3, el), I32), S((3, el), F32)), "slots", slot_map.reshape(512, 128), corners)
    send = simple(bucket_kernel, S((128, 256), F32), "buckets", element_part / 3.0, slots, ranks)
    recv = lax.all_to_all(send, ("row", "col"), 0, 0, tiled=True)
    vertex, grad = simple(vertex_kernel, (S((6, 512), F32), S((1, 300), F32)), "vertex", recv, morph_modes,
                          scratch=[pltpu.VMEM((300, 128), F32)])
    return vertex, lax.psum(grad[0], ("row", "col"))


def solution(mesh):
    from jax.sharding import PartitionSpec as P
    every = ("row", "col")
    return jax.shard_map(
        body, mesh=mesh,
        in_specs=(P(None, every), P(None, every), P(None, every), P(every), P(None, every), P(None, every), P(None, every),
                  P(), P("row", None, "col", None), P(None, None, every)),
        out_specs=(P(None, every), P()), check_vma=False)
```

```python
import math, functools
import jax, jax.numpy as jnp
from jax import lax
from jax.experimental import pallas as pl
from jax.experimental.pallas import tpu as pltpu

F32 = jnp.float32
MAGIC = 12582912.0
INV_TURN = 1.0 / (2.0 * math.pi)
SIN_C = (4.442883014678955, -7.308245658874512, 3.6063544750213623, -0.8461129069328308, 0.10982698947191238)
COS_C = (1.4142135381698608, -6.978850841522217, 5.7394609451293945, -1.8835630416870117, 0.31069818139076233)


def horner(coeffs, z):
    total = z * coeffs[-1] + coeffs[-2]
    for value in coeffs[-3::-1]:
        total = total * z + value
    return total


def green(r2, cr, ci):
    inv = lax.rsqrt(r2)
    phi = r2 * inv
    turn = phi * INV_TURN
    frac = turn - ((turn + MAGIC) - MAGIC)
    z = frac * frac
    hs = frac * horner(SIN_C, z)
    hc = horner(COS_C, z)
    cosine = 1.0 - hs * hs
    sine = hs * hc
    er = cr * cosine - ci * sine
    ei = cr * sine + ci * cosine
    i2 = inv * inv
    i3 = i2 * inv
    g = er + phi * ei
    h = ei - phi * er
    k = g * (3.0 * i2) - er
    return g, h, k, i3


def tile_terms(kind, row, col, cr_scale, ci_scale):
    x, y, z, ar, ai = row
    dx, dy, dz = x - col["y"][0], y - col["y"][1], z - col["y"][2]
    d = (dx, dy, dz)
    nx, ny, nz = col["n"]
    mn = dx * nx + dy * ny + dz * nz
    sq = dx * dx + dy * dy + dz * dz
    cr = ar * cr_scale + ai * ci_scale
    ci = ar * ci_scale - ai * cr_scale
    out = {}
    sa = sb = None
    if kind != 0:
        ex, ey, ez = col["t2"]
        e = dx * ex + dy * ey + dz * ez
        b = sq + col["at"]
        pts = []
        for sign in (-1, 1):
            if sign > 0:
                r2, m = b - e, mn - col["tn"]
            else:
                r2, m = b + e, mn + col["tn"]
            g, h, k, i3 = green(r2, cr, ci)
            pts.append((i3 * g, i3 * (h - m * k)))
        (a0, b0), (a2, b2) = pts
        sa, sb, da, db = a0 + a2, b0 + b2, a2 - a0, b2 - b0
    if kind != 1:
        g, h, k, i3 = green(sq + col["a"], cr, ci)
        a1, b1 = i3 * g, i3 * (h - mn * k)
        sa, sb = (a1, b1) if sa is None else (sa + a1, sb + b1)
    bd = [sb * v for v in d]
    ad = [sa * v for v in d]
    an = [sa * v for v in (nx, ny, nz)]
    pos = [p + q for p, q in zip(bd, an)]
    if kind == 0:
        return pos, pos, ad, None
    ts = col["ts"]
    pos = [p - db * t for p, t in zip(pos, ts)]
    return pos, pos, ad, da


def pair_kernel(batches, groups, lists_ref, rows_ref, cen_ref, nor_ref, tan_ref, area_ref, fwd_ref, col_out, row_out, table, racc, ctab):
    tiles = lists_ref.shape[0]
    rt = jnp.transpose(rows_ref[...])
    for g in range(groups):
        for q in range(5):
            v = jnp.broadcast_to(rt[q * 8:(q + 1) * 8, g:g + 1], (8, 128))
            table[g, q] = v * 4.0 if q < 3 else v
    table[groups] = jnp.concatenate([jnp.full((3, 8, 128), 1.0, F32), jnp.zeros((2, 8, 128), F32)], axis=0)
    racc[...] = jnp.zeros(racc.shape, F32)
    area = area_ref[...]
    spread = jnp.sqrt(area) * 2.4
    ysc = 4.0 * cen_ref[...]
    n16 = 16.0 * nor_ref[...]
    ts = spread * tan_ref[...]
    a16 = 16.0 * area
    at = a16 + jnp.sum(ts * ts, axis=0, keepdims=True)
    tn = jnp.sum(ts * n16, axis=0, keepdims=True)
    fw = fwd_ref[...] * (area * (1.0 / math.pi))
    rows = [ysc, n16, ts, 2.0 * ts, a16, at, tn, fw]
    pos = 0
    for r in rows:
        ctab[pos:pos + r.shape[0], :] = r
        pos += r.shape[0]

    def tile_body(t, _):
        lanes = pl.ds(pl.multiple_of(t * 128, 128), 128)

        def bc(i):
            return jnp.broadcast_to(ctab[i:i + 1, lanes], (8, 128))

        def getcol():
            return dict(y=[bc(0), bc(1), bc(2)], n=[bc(3), bc(4), bc(5)], ts=[bc(6), bc(7), bc(8)],
                        t2=[bc(9), bc(10), bc(11)], a=bc(12), at=bc(13), tn=bc(14))
        zero = jnp.zeros((8, 128), F32)
        n0, n1, n2 = lists_ref[t, 253], lists_ref[t, 254], lists_ref[t, 255]
        b0, b1, b2 = batches
        s0 = 0
        s1 = n0 * b0
        s2 = s1 + n1 * b1
        carry = (zero,) * 7

        def make(kind, size, start, weight):
            def body(it, acc):
                col = getcol()
                frs, fis = bc(15) * weight, bc(16) * weight
                acc = list(acc)
                ids, news = [], []
                for j in range(size):
                    g = lists_ref[t, start + it * size + j]
                    row = [table[g, q] for q in range(5)]
                    pos, cpos, ad, da = tile_terms(kind, row, col, frs, fis)
                    for q in range(3):
                        acc[q] = acc[q] + pos[q]
                        acc[3 + q] = acc[3 + q] + ad[q]
                    if da is not None:
                        acc[6] = acc[6] + da
                    ids.append(g)
                    news.append(pos)
                olds = [[racc[g, q] for q in range(3)] for g in ids]
                for g, old, new in zip(ids, olds, news):
                    for q in range(3):
                        racc[g, q] = old[q] + new[q]
                return tuple(acc)
            return body
        carry = lax.fori_loop(0, n0, make(0, b0, s0, 1.0), carry)
        carry = lax.fori_loop(0, n1, make(1, b1, s1, 0.5), carry)
        carry = lax.fori_loop(0, n2, make(2, b2, s2, 1.0 / 3.0), carry)
        sums = [jnp.sum(v, axis=0, keepdims=True) for v in carry]
        for q in range(3):
            col_out[q:q + 1, lanes] = -sums[q]
            tsr = ctab[6 + q:7 + q, lanes]
            col_out[3 + q:4 + q, lanes] = 4.0 * (sums[3 + q] - sums[6] * tsr)
        return 0

    lax.fori_loop(0, tiles, tile_body, 0)
    lane = lax.broadcasted_iota(jnp.int32, (8, 128), 1)
    outs = [jnp.zeros((8, 128), F32) for _ in range(3)]
    for g in range(groups):
        for q in range(3):
            s = jnp.sum(racc[g, q], axis=1, keepdims=True)
            outs[q] = jnp.where(lane == g, s, outs[q])
    full = jnp.concatenate(outs + [jnp.zeros((104, 128), F32)], axis=0)
    row_out[...] = jnp.transpose(full)


def pair_call(lists, rows, cen, nor, tan, area, fwd, batches=(8, 4, 4)):
    el = cen.shape[1]
    groups = rows.shape[0]
    vm = pl.BlockSpec(memory_space=pltpu.VMEM)
    return pl.pallas_call(
        functools.partial(pair_kernel, batches, groups),
        out_shape=(jax.ShapeDtypeStruct((6, el), F32), jax.ShapeDtypeStruct((128, 128), F32)),
        in_specs=[pl.BlockSpec(memory_space=pltpu.SMEM)] + [vm] * 6,
        out_specs=(vm, vm),
        scratch_shapes=[pltpu.VMEM((groups + 1, 5, 8, 128), F32), pltpu.VMEM((groups + 1, 3, 8, 128), F32),
                        pltpu.VMEM((24, el), F32)],
        name="pairs",
    )(lists, rows, cen, nor, tan, area, fwd)


def dot_nn(a, b):
    return lax.dot_general(a, b, (((1,), (0,)), ((), ())), preferred_element_type=F32)


def dot_nt(a, b):
    return lax.dot_general(a, b, (((1,), (1,)), ((), ())), preferred_element_type=F32)


def iota(shape, dim):
    return lax.broadcasted_iota(jnp.int32, shape, dim)


BF16 = jnp.bfloat16


def split3(v):
    hi = v.astype(BF16)
    rest = v - hi.astype(F32)
    mid = rest.astype(BF16)
    low = (rest - mid.astype(F32)).astype(BF16)
    return hi, mid, low


def ones_where(mask):
    return jnp.where(mask, 1.0, 0.0)


def make_lists(flags, batches):
    before = ones_where(iota((128, 128), 0) < iota((128, 128), 1)).astype(BF16)
    tile = iota((8, 128), 0)
    lane = iota((8, 128), 1)
    pos = jnp.zeros((8, 128), F32)
    base = jnp.zeros((8, 1), F32)
    counts = []
    for kind in range(3):
        mask = ones_where(flags == float(kind))
        inside = dot_nn(mask.astype(BF16), before)
        total = jnp.sum(mask, axis=1, keepdims=True)
        pos = pos + mask * (inside + base)
        nb = jnp.floor((total + float(batches[kind] - 1)) * (1.0 / batches[kind]))
        base = base + nb * float(batches[kind])
        counts.append(nb)
    posi = pos.astype(jnp.int32)
    slot = iota((256, 128), 0)
    out = jnp.zeros((8, 256), F32)
    for t in range(8):
        hit = ones_where(slot == posi[t:t + 1, :]).astype(BF16)
        value = jnp.where(tile == t, (lane - 128).astype(F32), 0.0).astype(BF16)
        out = out + dot_nt(value, hit)
    out = out + 128.0
    wide = iota((8, 256), 1)
    for kind in range(3):
        out = jnp.where(wide == 253 + kind, counts[kind], out)
    return out.astype(jnp.int32)


def lookup_slots(table, corners):
    parts = jnp.concatenate([(table >> 8).astype(F32).astype(BF16), (table & 255).astype(F32).astype(BF16)], axis=1)
    width = 256
    lo_iota = iota((128, width), 0)
    hi_iota = iota((512, width), 0)
    rows = []
    for n in range(corners.shape[0]):
        pieces = []
        for cb in range(corners.shape[1] // width):
            v = corners[n:n + 1, cb * width:(cb + 1) * width]
            hit = lo_iota == (v & 127)
            rhs = jnp.concatenate([jnp.where(hit, 256.0, 0.0), jnp.where(hit, 1.0, 0.0)], axis=0).astype(BF16)
            sel = dot_nn(parts, rhs)
            pieces.append(jnp.sum(jnp.where(hi_iota == (v >> 7), sel, 0.0), axis=0, keepdims=True))
        rows.append(jnp.concatenate(pieces, axis=1))
    return jnp.concatenate(rows, axis=0).astype(jnp.int32)


def patch_ranks(patches):
    width = 256
    before = ones_where(iota((width, width), 0) < iota((width, width), 1)).astype(BF16)
    sub = iota((128, width), 0)
    carry = jnp.zeros((128, 1), F32)
    rows = []
    for n in range(patches.shape[0]):
        pieces = []
        for cb in range(patches.shape[1] // width):
            hit = ones_where(sub == patches[n:n + 1, cb * width:(cb + 1) * width])
            earlier = dot_nn(hit.astype(BF16), before) + carry
            pieces.append(jnp.sum(hit * earlier, axis=0, keepdims=True))
            carry = carry + jnp.sum(hit, axis=1, keepdims=True)
        rows.append(jnp.concatenate(pieces, axis=1))
    return jnp.concatenate(rows, axis=0)


def bucket_terms(values, slots, ranks):
    width = values.shape[1]
    hit = ones_where(iota((128, width), 0) == (slots >> 9)).astype(BF16)
    mine = (iota((192, width), 0) >> 3) == ranks
    total = None
    for part in split3(values):
        rhs = jnp.where(mine, jnp.concatenate([part.astype(F32)] * 24, axis=0), 0.0).astype(BF16)
        term = dot_nt(hit, rhs)
        total = term if total is None else total + term
    return total


def add_up(recv):
    turned = jnp.transpose(recv)
    sub = iota((512, 128), 0).astype(F32)
    total = jnp.zeros((24, 512), F32)
    for pair in range(12):
        parts, hits = [], []
        for q in (2 * pair, 2 * pair + 1):
            eight = turned[q * 8:(q + 1) * 8, :]
            hits.append(ones_where(sub == eight[6:7, :]).astype(BF16))
            parts.append(jnp.concatenate([p.astype(F32) for p in split3(eight)], axis=0))
        lhs = jnp.concatenate(parts, axis=1).astype(BF16)
        total = total + dot_nt(lhs, jnp.concatenate(hits, axis=1))
    return total[0:8] + total[8:16] + total[16:24]


VM = pl.BlockSpec(memory_space=pltpu.VMEM)
SLAB_DEV = 8
BATCHES = (8, 4, 4)
N_ROW, N_COL = 8, 16
S = jax.ShapeDtypeStruct
I32 = jnp.int32
DMA = pltpu.SemaphoreType.DMA
MESH = pl.DeviceIdType.MESH


def greet(me):
    barrier = pltpu.get_barrier_semaphore()
    for axis, count in (("row", N_ROW), ("col", N_COL)):
        def signal(k, _, axis=axis, count=count):
            pl.semaphore_signal(barrier, inc=1, device_id={axis: lax.rem(me[axis] + k, count)}, device_id_type=MESH)
            return 0
        lax.fori_loop(1, count, signal, 0)
    return barrier


class Swap:
    def __init__(self, me, axis, count, piece, slot, sems):
        self.me, self.count, self.axis = me[axis], count, axis
        self.piece, self.slot = piece, slot
        self.send_sem, self.recv_sem = sems

    def copy(self, peer, slot):
        return pltpu.make_async_remote_copy(
            src_ref=self.piece(peer), dst_ref=self.slot(slot), send_sem=self.send_sem.at[peer], recv_sem=self.recv_sem.at[slot],
            device_id={self.axis: peer}, device_id_type=MESH)

    def each(self, act):
        def visit(k, _):
            act(lax.rem(self.me + k, self.count))
            return 0
        lax.fori_loop(1, self.count, visit, 0)

    def start(self):
        self.each(lambda peer: self.copy(peer, self.me).start())

    def receive(self):
        self.each(lambda peer: self.copy(peer, peer).wait_recv())

    def drain(self):
        self.each(lambda peer: self.copy(peer, peer).wait_send())


def swap_sems(n):
    return [DMA((n,)), DMA((n,))]


def gather_kernel(cen_ref, adj_ref, flags_ref, table_ref, corners_ref, rows_out, lists_out, slots_out, ranks_out,
                  own, rowblk, rowall, flagall, fs, fr, cs, cr, rs, rr):
    me = {"row": lax.axis_index("row"), "col": lax.axis_index("col")}
    barrier = greet(me)
    lane = iota((1, 128), 1)
    packed = jnp.zeros((1, 128), F32)
    for q in range(5):
        line = cen_ref[q:q + 1, 0:128] if q < 3 else adj_ref[q - 3:q - 2, 0:128]
        if q:
            line = pltpu.roll(line, 8 * q, 1)
        packed = jnp.where((lane >> 3) == q, line, packed)
    own[...] = packed
    rowblk[pl.ds(me["col"], 1), :] = packed
    flagall[me["row"]] = flags_ref[me["row"]]
    pl.semaphore_wait(barrier, N_ROW + N_COL - 2)
    flag_swap = Swap(me, "row", N_ROW, lambda peer: flags_ref.at[peer], lambda slot: flagall.at[slot], (fs, fr))
    col_swap = Swap(me, "col", N_COL, lambda peer: own, lambda slot: rowblk.at[pl.ds(slot, 1), :], (cs, cr))
    row_swap = Swap(me, "row", N_ROW, lambda peer: rowblk, lambda slot: rowall.at[slot], (rs, rr))
    col_swap.start()
    flag_swap.start()
    slots = lookup_slots(table_ref[...], corners_ref[...])
    slots_out[...] = slots
    col_swap.receive()
    row_swap.start()
    rowall[me["row"]] = rowblk[...]
    ranks_out[...] = patch_ranks(slots >> 9).astype(I32)
    flag_swap.receive()
    flags = jnp.concatenate([flagall[r] for r in range(N_ROW)], axis=1).astype(F32)
    lists_out[...] = make_lists(flags, BATCHES)
    row_swap.receive()
    for r in range(N_ROW):
        rows_out[r * N_COL:(r + 1) * N_COL, :] = rowall[r]
    for swap in (col_swap, flag_swap, row_swap):
        swap.drain()


def project(modes_ref, vertex, acc_ref):
    total = None
    for comp in range(6):
        for k in range(4):
            lanes = slice(k * 128, (k + 1) * 128)
            term = modes_ref[comp, :, lanes] * vertex[comp:comp + 1, lanes]
            total = term if total is None else total + term
    acc_ref[...] = jnp.zeros(acc_ref.shape, F32)
    acc_ref[0:total.shape[0], :] = total
    ones = jnp.ones((8, 128), BF16)
    return sum(dot_nt(ones, p) for p in split3(acc_ref[...]))


def finish_kernel(col_ref, row_ref, slots_ref, ranks_ref, modes_hbm, vertex_out, grad_out,
                  modes, part16, sum16, own16, send, mid, stage, recv, acc, grad, grad8, mid_grad, grad16,
                  msem, a0, a1, b0, b1, c0, c1, d0, d1, e0, e1, f0, f1):
    me = {"row": lax.axis_index("row"), "col": lax.axis_index("col")}
    r, c = me["row"], me["col"]
    barrier = greet(me)
    fetch = pltpu.make_async_copy(modes_hbm, modes, msem)
    fetch.start()
    pl.semaphore_wait(barrier, N_ROW + N_COL - 2)

    def block(ref, i):
        return ref.at[pl.ds(pl.multiple_of(i * N_COL, N_COL), N_COL), :]

    def halves(ref, i):
        return ref.at[:, pl.ds(pl.multiple_of(i * N_COL, N_COL), N_COL), :]

    swap_a = Swap(me, "row", N_ROW, lambda peer: block(row_ref, peer), lambda slot: part16.at[slot], (a0, a1))
    swap_b = Swap(me, "col", N_COL, lambda peer: sum16.at[pl.ds(peer, 1), :], lambda slot: own16.at[pl.ds(slot, 1), :], (b0, b1))
    swap_c = Swap(me, "row", N_ROW, lambda peer: halves(send, peer), lambda slot: halves(mid, slot), (c0, c1))
    swap_d = Swap(me, "col", N_COL, lambda peer: stage.at[peer], lambda slot: recv.at[slot], (d0, d1))
    swap_e = Swap(me, "row", N_ROW, lambda peer: grad, lambda slot: grad8.at[slot], (e0, e1))
    swap_f = Swap(me, "col", N_COL, lambda peer: mid_grad, lambda slot: grad16.at[slot], (f0, f1))

    swap_a.start()
    part16[r] = block(row_ref, r)[...]
    width = 256
    third = 1.0 / 3.0
    total = jnp.zeros((128, 192), F32)
    for n in range(3):
        for cb in range(col_ref.shape[1] // width):
            cols = slice(cb * width, (cb + 1) * width)
            s = slots_ref[n:n + 1, cols]
            eight = jnp.concatenate([col_ref[:, cols] * third, (s & 511).astype(F32), jnp.zeros((1, width), F32)], axis=0)
            total = total + bucket_terms(eight, s, ranks_ref[n:n + 1, cols])
        if n == 0:
            swap_a.receive()
            sum16[...] = sum(part16[i] for i in range(N_ROW))
            swap_b.start()
            own16[pl.ds(c, 1), :] = sum16[pl.ds(c, 1), :]
    swap_b.receive()
    own = jnp.sum(own16[...], axis=0, keepdims=True) * third
    lane = iota((1, 128), 1)
    lines = [jnp.where(lane < 8, own if q == 0 else pltpu.roll(own, 128 - 8 * q, 1), 0.0) for q in range(3)]
    extra = jnp.concatenate(lines + [jnp.zeros((5, 128), F32)], axis=0)
    for n in range(3):
        total = total + bucket_terms(extra, slots_ref[n:n + 1, 0:128], ranks_ref[n:n + 1, 0:128])
    send[0] = total[:, 0:128]
    send[1] = jnp.concatenate([total[:, 128:192], jnp.zeros((128, 64), F32)], axis=1)
    swap_c.start()
    halves(mid, r)[...] = halves(send, r)[...]
    swap_c.receive()
    for i in range(N_COL):
        for half in range(2):
            stage[i, :, half * 128:(half + 1) * 128] = mid[half, pl.ds(i, N_ROW, stride=N_COL), :]
    swap_d.start()
    recv[c] = stage[c]
    swap_d.receive()
    vertex = add_up(recv[...].reshape(128, 256))
    vertex_out[...] = vertex[0:6]
    fetch.wait()
    grad[...] = project(modes, vertex, acc)[0:1]
    swap_e.start()
    grad8[r] = grad[...]
    swap_e.receive()
    mid_grad[...] = sum(grad8[i] for i in range(N_ROW))
    swap_f.start()
    grad16[c] = mid_grad[...]
    swap_f.receive()
    grad_out[...] = sum(grad16[i] for i in range(N_COL))[:, 0:grad_out.shape[1]]
    for swap in (swap_a, swap_b, swap_c, swap_d, swap_e, swap_f):
        swap.drain()


def body(centroid, normals, tangent, element_area, forward_field, adjoint_field, corners, slot_map, quad_order, morph_modes):
    el = centroid.shape[1]
    modes_t = jnp.transpose(morph_modes, (1, 0, 2))
    flags = jnp.transpose(quad_order[:, :, 0, :], (1, 2, 0))
    whole = pl.BlockSpec(memory_space=pltpu.VMEM)
    rows, lists, slots, ranks = pl.pallas_call(
        gather_kernel,
        out_shape=(S((128, 128), F32), S((8, 256), I32), S((3, el), I32), S((3, el), I32)),
        in_specs=[whole] * 5, out_specs=(whole,) * 4,
        scratch_shapes=[pltpu.VMEM((1, 128), F32), pltpu.VMEM((16, 128), F32), pltpu.VMEM((8, 16, 128), F32),
                        pltpu.VMEM((8, 8, 16), I32)] + swap_sems(8) + swap_sems(16) + swap_sems(8),
        compiler_params=pltpu.CompilerParams(collective_id=0, has_side_effects=True), name="gather",
    )(centroid, adjoint_field, flags, slot_map.reshape(512, 128), corners)
    col_part, row_part = pair_call(lists, rows, centroid, normals, tangent, element_area[None, :], forward_field, BATCHES)
    vertex, grad = pl.pallas_call(
        finish_kernel,
        out_shape=(S((6, 512), F32), S((1, 300), F32)),
        in_specs=[whole] * 4 + [pl.BlockSpec(memory_space=pl.ANY)], out_specs=(whole, whole),
        scratch_shapes=[pltpu.VMEM((6, 300, 512), F32), pltpu.VMEM((8, 16, 128), F32), pltpu.VMEM((16, 128), F32),
                        pltpu.VMEM((16, 128), F32), pltpu.VMEM((2, 128, 128), F32), pltpu.VMEM((2, 128, 128), F32),
                        pltpu.VMEM((16, 8, 256), F32), pltpu.VMEM((16, 8, 256), F32), pltpu.VMEM((384, 128), F32),
                        pltpu.VMEM((1, 384), F32), pltpu.VMEM((8, 1, 384), F32), pltpu.VMEM((1, 384), F32),
                        pltpu.VMEM((16, 1, 384), F32), DMA] + (swap_sems(8) + swap_sems(16)) * 3,
        compiler_params=pltpu.CompilerParams(collective_id=1, has_side_effects=True), name="finish",
    )(col_part, row_part, slots, ranks, modes_t)
    return vertex, grad[0]


def solution(mesh):
    from jax.sharding import PartitionSpec as P
    every = ("row", "col")
    return jax.shard_map(
        body, mesh=mesh,
        in_specs=(P(None, every), P(None, every), P(None, every), P(every), P(None, every), P(None, every), P(None, every),
                  P(), P("row", None, "col", None), P(None, None, every)),
        out_specs=(P(None, every), P()), check_vma=False)
```

```python
import math, functools
import jax, jax.numpy as jnp
from jax import lax
from jax.experimental import pallas as pl
from jax.experimental.pallas import tpu as pltpu

F32 = jnp.float32
MAGIC = 12582912.0
INV_TURN = 1.0 / (2.0 * math.pi)
SIN_C = (4.442883014678955, -7.308245658874512, 3.6063544750213623, -0.8461129069328308, 0.10982698947191238)
COS_C = (1.4142135381698608, -6.978850841522217, 5.7394609451293945, -1.8835630416870117, 0.31069818139076233)


def horner(coeffs, z):
    total = z * coeffs[-1] + coeffs[-2]
    for value in coeffs[-3::-1]:
        total = total * z + value
    return total


def green(r2, cr, ci):
    inv = lax.rsqrt(r2)
    phi = r2 * inv
    turn = phi * INV_TURN
    frac = turn - ((turn + MAGIC) - MAGIC)
    z = frac * frac
    hs = frac * horner(SIN_C, z)
    hc = horner(COS_C, z)
    cosine = 1.0 - hs * hs
    sine = hs * hc
    er = cr * cosine - ci * sine
    ei = cr * sine + ci * cosine
    i2 = inv * inv
    i3 = i2 * inv
    g = er + phi * ei
    h = ei - phi * er
    k = g * (3.0 * i2) - er
    return g, h, k, i3


def tile_terms(kind, row, col, cr_scale, ci_scale):
    x, y, z, ar, ai = row
    dx, dy, dz = x - col["y"][0], y - col["y"][1], z - col["y"][2]
    d = (dx, dy, dz)
    nx, ny, nz = col["n"]
    mn = dx * nx + dy * ny + dz * nz
    sq = dx * dx + dy * dy + dz * dz
    cr = ar * cr_scale + ai * ci_scale
    ci = ar * ci_scale - ai * cr_scale
    out = {}
    sa = sb = None
    if kind != 0:
        ex, ey, ez = col["t2"]
        e = dx * ex + dy * ey + dz * ez
        b = sq + col["at"]
        pts = []
        for sign in (-1, 1):
            if sign > 0:
                r2, m = b - e, mn - col["tn"]
            else:
                r2, m = b + e, mn + col["tn"]
            g, h, k, i3 = green(r2, cr, ci)
            pts.append((i3 * g, i3 * (h - m * k)))
        (a0, b0), (a2, b2) = pts
        sa, sb, da, db = a0 + a2, b0 + b2, a2 - a0, b2 - b0
    if kind != 1:
        g, h, k, i3 = green(sq + col["a"], cr, ci)
        a1, b1 = i3 * g, i3 * (h - mn * k)
        sa, sb = (a1, b1) if sa is None else (sa + a1, sb + b1)
    bd = [sb * v for v in d]
    ad = [sa * v for v in d]
    an = [sa * v for v in (nx, ny, nz)]
    pos = [p + q for p, q in zip(bd, an)]
    if kind == 0:
        return pos, pos, ad, None
    ts = col["ts"]
    pos = [p - db * t for p, t in zip(pos, ts)]
    return pos, pos, ad, da


def pair_kernel(batches, groups, lists_ref, rows_ref, cen_ref, nor_ref, tan_ref, area_ref, fwd_ref, col_out, row_out, table, racc, ctab):
    tiles = lists_ref.shape[0]
    rt = jnp.transpose(rows_ref[...])
    for g in range(groups):
        for q in range(5):
            v = jnp.broadcast_to(rt[q * 8:(q + 1) * 8, g:g + 1], (8, 128))
            table[g, q] = v * 4.0 if q < 3 else v
    table[groups] = jnp.concatenate([jnp.full((3, 8, 128), 1.0, F32), jnp.zeros((2, 8, 128), F32)], axis=0)
    racc[...] = jnp.zeros(racc.shape, F32)
    area = area_ref[...]
    spread = jnp.sqrt(area) * 2.4
    ysc = 4.0 * cen_ref[...]
    n16 = 16.0 * nor_ref[...]
    ts = spread * tan_ref[...]
    a16 = 16.0 * area
    at = a16 + jnp.sum(ts * ts, axis=0, keepdims=True)
    tn = jnp.sum(ts * n16, axis=0, keepdims=True)
    fw = fwd_ref[...] * (area * (1.0 / math.pi))
    rows = [ysc, n16, ts, 2.0 * ts, a16, at, tn, fw]
    pos = 0
    for r in rows:
        ctab[pos:pos + r.shape[0], :] = r
        pos += r.shape[0]

    def tile_body(t, _):
        lanes = pl.ds(pl.multiple_of(t * 128, 128), 128)

        def bc(i):
            return jnp.broadcast_to(ctab[i:i + 1, lanes], (8, 128))

        def getcol():
            return dict(y=[bc(0), bc(1), bc(2)], n=[bc(3), bc(4), bc(5)], ts=[bc(6), bc(7), bc(8)],
                        t2=[bc(9), bc(10), bc(11)], a=bc(12), at=bc(13), tn=bc(14))
        zero = jnp.zeros((8, 128), F32)
        n0, n1, n2 = lists_ref[t, 253], lists_ref[t, 254], lists_ref[t, 255]
        b0, b1, b2 = batches
        s0 = 0
        s1 = n0 * b0
        s2 = s1 + n1 * b1
        carry = (zero,) * 7

        def make(kind, size, start, weight):
            def body(it, acc):
                col = getcol()
                frs, fis = bc(15) * weight, bc(16) * weight
                acc = list(acc)
                ids, news = [], []
                for j in range(size):
                    g = lists_ref[t, start + it * size + j]
                    row = [table[g, q] for q in range(5)]
                    pos, cpos, ad, da = tile_terms(kind, row, col, frs, fis)
                    for q in range(3):
                        acc[q] = acc[q] + pos[q]
                        acc[3 + q] = acc[3 + q] + ad[q]
                    if da is not None:
                        acc[6] = acc[6] + da
                    ids.append(g)
                    news.append(pos)
                olds = [[racc[g, q] for q in range(3)] for g in ids]
                for g, old, new in zip(ids, olds, news):
                    for q in range(3):
                        racc[g, q] = old[q] + new[q]
                return tuple(acc)
            return body
        carry = lax.fori_loop(0, n0, make(0, b0, s0, 1.0), carry)
        carry = lax.fori_loop(0, n1, make(1, b1, s1, 0.5), carry)
        carry = lax.fori_loop(0, n2, make(2, b2, s2, 1.0 / 3.0), carry)
        sums = [jnp.sum(v, axis=0, keepdims=True) for v in carry]
        for q in range(3):
            col_out[q:q + 1, lanes] = -sums[q]
            tsr = ctab[6 + q:7 + q, lanes]
            col_out[3 + q:4 + q, lanes] = 4.0 * (sums[3 + q] - sums[6] * tsr)
        return 0

    lax.fori_loop(0, tiles, tile_body, 0)
    lane = lax.broadcasted_iota(jnp.int32, (8, 128), 1)
    outs = [jnp.zeros((8, 128), F32) for _ in range(3)]
    for g in range(groups):
        for q in range(3):
            s = jnp.sum(racc[g, q], axis=1, keepdims=True)
            outs[q] = jnp.where(lane == g, s, outs[q])
    for q in range(3):
        row_out[q * 8:(q + 1) * 8, :] = outs[q]


def pair_call(lists, rows, cen, nor, tan, area, fwd, batches=(8, 4, 4)):
    el = cen.shape[1]
    groups = rows.shape[0]
    vm = pl.BlockSpec(memory_space=pltpu.VMEM)
    return pl.pallas_call(
        functools.partial(pair_kernel, batches, groups),
        out_shape=(jax.ShapeDtypeStruct((6, el), F32), jax.ShapeDtypeStruct((24, 128), F32)),
        in_specs=[pl.BlockSpec(memory_space=pltpu.SMEM)] + [vm] * 6,
        out_specs=(vm, vm),
        scratch_shapes=[pltpu.VMEM((groups + 1, 5, 8, 128), F32), pltpu.VMEM((groups + 1, 3, 8, 128), F32),
                        pltpu.VMEM((24, el), F32)],
        name="pairs",
    )(lists, rows, cen, nor, tan, area, fwd)


def dot_nn(a, b):
    return lax.dot_general(a, b, (((1,), (0,)), ((), ())), preferred_element_type=F32)


def dot_nt(a, b):
    return lax.dot_general(a, b, (((1,), (1,)), ((), ())), preferred_element_type=F32)


def iota(shape, dim):
    return lax.broadcasted_iota(jnp.int32, shape, dim)


BF16 = jnp.bfloat16


def split3(v):
    hi = v.astype(BF16)
    rest = v - hi.astype(F32)
    mid = rest.astype(BF16)
    low = (rest - mid.astype(F32)).astype(BF16)
    return hi, mid, low


def ones_where(mask):
    return jnp.where(mask, 1.0, 0.0)


def make_lists(flags, batches):
    before = ones_where(iota((128, 128), 0) < iota((128, 128), 1)).astype(BF16)
    tile = iota((8, 128), 0)
    lane = iota((8, 128), 1)
    pos = jnp.zeros((8, 128), F32)
    base = jnp.zeros((8, 1), F32)
    counts = []
    for kind in range(3):
        mask = ones_where(flags == float(kind))
        inside = dot_nn(mask.astype(BF16), before)
        total = jnp.sum(mask, axis=1, keepdims=True)
        pos = pos + mask * (inside + base)
        nb = jnp.floor((total + float(batches[kind] - 1)) * (1.0 / batches[kind]))
        base = base + nb * float(batches[kind])
        counts.append(nb)
    posi = pos.astype(jnp.int32)
    slot = iota((256, 128), 0)
    out = jnp.zeros((8, 256), F32)
    for t in range(8):
        hit = ones_where(slot == posi[t:t + 1, :]).astype(BF16)
        value = jnp.where(tile == t, (((lane & 15) << 3) + (lane >> 4) - 128).astype(F32), 0.0).astype(BF16)
        out = out + dot_nt(value, hit)
    out = out + 128.0
    wide = iota((8, 256), 1)
    for kind in range(3):
        out = jnp.where(wide == 253 + kind, counts[kind], out)
    return out.astype(jnp.int32)


def lookup_slots(table, corners):
    parts = jnp.concatenate([(table >> 8).astype(F32).astype(BF16), (table & 255).astype(F32).astype(BF16)], axis=1)
    width = 256
    lo_iota = iota((128, width), 0)
    hi_iota = iota((512, width), 0)
    rows = []
    for n in range(corners.shape[0]):
        pieces = []
        for cb in range(corners.shape[1] // width):
            v = corners[n:n + 1, cb * width:(cb + 1) * width]
            hit = lo_iota == (v & 127)
            rhs = jnp.concatenate([jnp.where(hit, 256.0, 0.0), jnp.where(hit, 1.0, 0.0)], axis=0).astype(BF16)
            sel = dot_nn(parts, rhs)
            pieces.append(jnp.sum(jnp.where(hi_iota == (v >> 7), sel, 0.0), axis=0, keepdims=True))
        rows.append(jnp.concatenate(pieces, axis=1))
    return jnp.concatenate(rows, axis=0).astype(jnp.int32)


def patch_ranks(patches):
    width = 256
    before = ones_where(iota((width, width), 0) < iota((width, width), 1)).astype(BF16)
    sub = iota((128, width), 0)
    carry = jnp.zeros((128, 1), F32)
    rows = []
    for n in range(patches.shape[0]):
        pieces = []
        for cb in range(patches.shape[1] // width):
            hit = ones_where(sub == patches[n:n + 1, cb * width:(cb + 1) * width])
            earlier = dot_nn(hit.astype(BF16), before) + carry
            pieces.append(jnp.sum(hit * earlier, axis=0, keepdims=True))
            carry = carry + jnp.sum(hit, axis=1, keepdims=True)
        rows.append(jnp.concatenate(pieces, axis=1))
    return jnp.concatenate(rows, axis=0)


def bucket_terms(values, slots, ranks):
    width = values.shape[1]
    hit = ones_where(iota((128, width), 0) == (slots >> 9)).astype(BF16)
    mine = (iota((192, width), 0) >> 3) == ranks
    total = None
    for part in split3(values):
        rhs = jnp.where(mine, jnp.concatenate([part.astype(F32)] * 24, axis=0), 0.0).astype(BF16)
        term = dot_nt(hit, rhs)
        total = term if total is None else total + term
    return total


def add_up(recv, rows):
    turned = jnp.transpose(recv)
    sub = iota((512, 128), 0).astype(F32)
    row8 = iota((8, 128), 0)
    row8f = row8.astype(F32)
    total = jnp.zeros((24, 512), F32)
    for pair in range(12):
        parts, hits = [], []
        for q in (2 * pair, 2 * pair + 1):
            eight = turned[q * 8:(q + 1) * 8, :]
            mine = ones_where(row8f == eight[7:8, :])
            for comp in range(3):
                gain = jnp.sum(mine * rows[comp * 8:(comp + 1) * 8], axis=0, keepdims=True)
                eight = eight + jnp.where(row8 == comp, gain, 0.0)
            hits.append(ones_where(sub == eight[6:7, :]).astype(BF16))
            parts.append(jnp.concatenate([p.astype(F32) for p in split3(eight)], axis=0))
        lhs = jnp.concatenate(parts, axis=1).astype(BF16)
        total = total + dot_nt(lhs, jnp.concatenate(hits, axis=1))
    return total[0:8] + total[8:16] + total[16:24]


VM = pl.BlockSpec(memory_space=pltpu.VMEM)
SLAB_DEV = 8
BATCHES = (8, 4, 4)
N_ROW, N_COL = 8, 16
S = jax.ShapeDtypeStruct
I32 = jnp.int32
DMA = pltpu.SemaphoreType.DMA
MESH = pl.DeviceIdType.MESH


def greet(me):
    barrier = pltpu.get_barrier_semaphore()
    for axis, count in (("row", N_ROW), ("col", N_COL)):
        def signal(k, _, axis=axis, count=count):
            pl.semaphore_signal(barrier, inc=1, device_id={axis: lax.rem(me[axis] + k, count)}, device_id_type=MESH)
            return 0
        lax.fori_loop(1, count, signal, 0)
    return barrier


class Swap:
    def __init__(self, me, axis, count, piece, slot, sems):
        self.me, self.count, self.axis = me[axis], count, axis
        self.piece, self.slot = piece, slot
        self.send_sem, self.recv_sem = sems

    def copy(self, peer, slot):
        return pltpu.make_async_remote_copy(
            src_ref=self.piece(peer), dst_ref=self.slot(slot), send_sem=self.send_sem.at[peer], recv_sem=self.recv_sem.at[slot],
            device_id={self.axis: peer}, device_id_type=MESH)

    def each(self, act):
        def visit(k, _):
            act(lax.rem(self.me + k, self.count))
            return 0
        lax.fori_loop(1, self.count, visit, 0)

    def start(self):
        self.each(lambda peer: self.copy(peer, self.me).start())

    def receive(self):
        self.each(lambda peer: self.copy(peer, peer).wait_recv())

    def drain(self):
        self.each(lambda peer: self.copy(peer, peer).wait_send())


def swap_sems(n):
    return [DMA((n,)), DMA((n,))]


def gather_kernel(cen_ref, adj_ref, flags_ref, table_ref, corners_ref, rows_out, lists_out, codes_out,
                  own, rowblk, rowall, flagall, fs, fr, cs, cr, rs, rr):
    me = {"row": lax.axis_index("row"), "col": lax.axis_index("col")}
    barrier = greet(me)
    lane = iota((1, 128), 1)
    packed = jnp.zeros((1, 128), F32)
    for q in range(5):
        line = cen_ref[q:q + 1, 0:128] if q < 3 else adj_ref[q - 3:q - 2, 0:128]
        if q:
            line = pltpu.roll(line, 8 * q, 1)
        packed = jnp.where((lane >> 3) == q, line, packed)
    own[...] = packed
    rowblk[pl.ds(me["col"], 1), :] = packed
    flagall[me["row"]] = flags_ref[me["row"]]
    slots = lookup_slots(table_ref[...], corners_ref[...])
    codes_out[...] = slots * 32 + patch_ranks(slots >> 9).astype(I32)
    pl.semaphore_wait(barrier, N_ROW + N_COL - 2)
    flag_swap = Swap(me, "row", N_ROW, lambda peer: flags_ref.at[peer], lambda slot: flagall.at[slot], (fs, fr))
    col_swap = Swap(me, "col", N_COL, lambda peer: own, lambda slot: rowblk.at[pl.ds(slot, 1), :], (cs, cr))
    row_swap = Swap(me, "row", N_ROW, lambda peer: rowblk,
                    lambda slot: rowall.at[pl.ds(pl.multiple_of(slot * N_COL, N_COL), N_COL), :], (rs, rr))
    col_swap.start()
    flag_swap.start()
    flag_swap.receive()
    flags = jnp.concatenate([flagall[r] for r in range(N_ROW)], axis=1).astype(F32)
    lists_out[...] = make_lists(flags, BATCHES)
    col_swap.receive()
    row_swap.start()
    rowall[pl.ds(pl.multiple_of(me["row"] * N_COL, N_COL), N_COL), :] = rowblk[...]
    row_swap.receive()
    for c in range(N_COL):
        rows_out[c * N_ROW:(c + 1) * N_ROW, :] = rowall[pl.ds(c, N_ROW, stride=N_COL), :]
    for swap in (col_swap, flag_swap, row_swap):
        swap.drain()


def project(modes_ref, vertex, acc_ref):
    total = None
    for comp in range(6):
        for k in range(4):
            lanes = slice(k * 128, (k + 1) * 128)
            term = modes_ref[comp, :, lanes] * vertex[comp:comp + 1, lanes]
            total = term if total is None else total + term
    acc_ref[...] = jnp.zeros(acc_ref.shape, F32)
    acc_ref[0:total.shape[0], :] = total
    ones = jnp.ones((8, 128), BF16)
    return sum(dot_nt(ones, p) for p in split3(acc_ref[...]))


def finish_kernel(col_ref, row_ref, codes_ref, modes_hbm, vertex_out, grad_out,
                  modes, part8, sumrow, part16, send, mid, stage, recv, acc, grad, grad8, mid_grad, grad16,
                  msem, a0, a1, b0, b1, c0, c1, d0, d1, e0, e1, f0, f1):
    me = {"row": lax.axis_index("row"), "col": lax.axis_index("col")}
    r, c = me["row"], me["col"]
    barrier = greet(me)
    fetch = pltpu.make_async_copy(modes_hbm, modes, msem)
    fetch.start()

    def halves(ref, i):
        return ref.at[:, pl.ds(pl.multiple_of(i * N_COL, N_COL), N_COL), :]

    swap_a = Swap(me, "row", N_ROW, lambda peer: row_ref, lambda slot: part8.at[slot], (a0, a1))
    swap_b = Swap(me, "col", N_COL, lambda peer: sumrow, lambda slot: part16.at[slot], (b0, b1))
    swap_c = Swap(me, "row", N_ROW, lambda peer: halves(send, peer), lambda slot: halves(mid, slot), (c0, c1))
    swap_d = Swap(me, "col", N_COL, lambda peer: stage.at[peer], lambda slot: recv.at[slot], (d0, d1))
    swap_e = Swap(me, "row", N_ROW, lambda peer: grad, lambda slot: grad8.at[slot], (e0, e1))
    swap_f = Swap(me, "col", N_COL, lambda peer: mid_grad, lambda slot: grad16.at[slot], (f0, f1))

    width = 256
    third = 1.0 / 3.0
    total = jnp.zeros((128, 192), F32)
    for n in range(3):
        for cb in range(col_ref.shape[1] // width):
            cols = slice(cb * width, (cb + 1) * width)
            code = codes_ref[n:n + 1, cols]
            slots = code >> 5
            element = jnp.minimum(iota((1, width), 1) + cb * width, SLAB_DEV).astype(F32)
            eight = jnp.concatenate([col_ref[:, cols] * third, (slots & 511).astype(F32), element], axis=0)
            total = total + bucket_terms(eight, slots, code & 31)
    send[0] = total[:, 0:128]
    send[1] = jnp.concatenate([total[:, 128:192], jnp.zeros((128, 64), F32)], axis=1)
    pl.semaphore_wait(barrier, N_ROW + N_COL - 2)
    swap_a.start()
    swap_c.start()
    part8[r] = row_ref[...]
    halves(mid, r)[...] = halves(send, r)[...]
    swap_a.receive()
    sumrow[...] = sum(part8[i] for i in range(N_ROW)) * third
    swap_b.start()
    part16[c] = sumrow[...]
    swap_c.receive()
    for i in range(N_COL):
        for half in range(2):
            stage[i, :, half * 128:(half + 1) * 128] = mid[half, pl.ds(i, N_ROW, stride=N_COL), :]
    swap_d.start()
    recv[c] = stage[c]
    swap_b.receive()
    rows = sum(part16[i] for i in range(N_COL))
    swap_d.receive()
    vertex = add_up(recv[...].reshape(128, 256), rows)
    vertex_out[...] = vertex[0:6]
    fetch.wait()
    grad[...] = project(modes, vertex, acc)[0:1]
    swap_e.start()
    grad8[r] = grad[...]
    swap_e.receive()
    mid_grad[...] = sum(grad8[i] for i in range(N_ROW))
    swap_f.start()
    grad16[c] = mid_grad[...]
    swap_f.receive()
    grad_out[...] = sum(grad16[i] for i in range(N_COL))
    for swap in (swap_a, swap_b, swap_c, swap_d, swap_e, swap_f):
        swap.drain()


def emit_kernel(vertex_ref, grad_ref, vertex_out, grad_out):
    vertex_out[...] = vertex_ref[...]
    grad_out[...] = grad_ref[...].reshape(grad_ref.shape[1])[0:grad_out.shape[0]]


def body(centroid, normals, tangent, element_area, forward_field, adjoint_field, corners, slot_map, quad_order, morph_modes):
    el = centroid.shape[1]
    modes_t = jnp.transpose(morph_modes, (1, 0, 2))
    flags = jnp.transpose(quad_order[:, :, 0, :], (1, 2, 0))
    rows, lists, codes = pl.pallas_call(
        gather_kernel,
        out_shape=(S((128, 128), F32), S((8, 256), I32), S((3, el), I32)),
        in_specs=[VM] * 5, out_specs=(VM,) * 3,
        scratch_shapes=[pltpu.VMEM((1, 128), F32), pltpu.VMEM((16, 128), F32), pltpu.VMEM((128, 128), F32),
                        pltpu.VMEM((8, 8, 16), I32)] + swap_sems(8) + swap_sems(16) + swap_sems(8),
        compiler_params=pltpu.CompilerParams(collective_id=0, has_side_effects=True), name="gather",
    )(centroid, adjoint_field, flags, slot_map.reshape(512, 128), corners)
    col_part, row_part = pair_call(lists, rows, centroid, normals, tangent, element_area[None, :], forward_field, BATCHES)
    vertex, grad = pl.pallas_call(
        finish_kernel,
        out_shape=(S((6, 512), F32), S((1, 384), F32)),
        in_specs=[VM] * 3 + [pl.BlockSpec(memory_space=pl.ANY)], out_specs=(VM, VM),
        scratch_shapes=[pltpu.VMEM((6, 300, 512), F32), pltpu.VMEM((8, 24, 128), F32), pltpu.VMEM((24, 128), F32),
                        pltpu.VMEM((16, 24, 128), F32), pltpu.VMEM((2, 128, 128), F32), pltpu.VMEM((2, 128, 128), F32),
                        pltpu.VMEM((16, 8, 256), F32), pltpu.VMEM((16, 8, 256), F32), pltpu.VMEM((384, 128), F32),
                        pltpu.VMEM((1, 384), F32), pltpu.VMEM((8, 1, 384), F32), pltpu.VMEM((1, 384), F32),
                        pltpu.VMEM((16, 1, 384), F32), DMA] + (swap_sems(8) + swap_sems(16)) * 3,
        compiler_params=pltpu.CompilerParams(collective_id=1, has_side_effects=True), name="finish",
    )(col_part, row_part, codes, modes_t)
    return pl.pallas_call(emit_kernel, out_shape=(S((6, 512), F32), S((300,), F32)), in_specs=[VM] * 2, out_specs=(VM, VM),
                          name="emit")(vertex, grad)


def solution(mesh):
    from jax.sharding import PartitionSpec as P
    every = ("row", "col")
    return jax.shard_map(
        body, mesh=mesh,
        in_specs=(P(None, every), P(None, every), P(None, every), P(every), P(None, every), P(None, every), P(None, every),
                  P(), P("row", None, "col", None), P(None, None, every)),
        out_specs=(P(None, every), P()), check_vma=False)
```

```python
import math, functools
import jax, jax.numpy as jnp
from jax import lax
from jax.experimental import pallas as pl
from jax.experimental.pallas import tpu as pltpu

F32 = jnp.float32
MAGIC = 12582912.0
INV_TURN = 1.0 / (2.0 * math.pi)
SIN_C = (4.442883014678955, -7.308245658874512, 3.6063544750213623, -0.8461129069328308, 0.10982698947191238)
COS_C = (1.4142135381698608, -6.978850841522217, 5.7394609451293945, -1.8835630416870117, 0.31069818139076233)


def horner(coeffs, z):
    total = z * coeffs[-1] + coeffs[-2]
    for value in coeffs[-3::-1]:
        total = total * z + value
    return total


def green(r2, cr, ci):
    inv = lax.rsqrt(r2)
    phi = r2 * inv
    turn = phi * INV_TURN
    frac = turn - jnp.round(turn)
    z = frac * frac
    hs = frac * horner(SIN_C, z)
    hc = horner(COS_C, z)
    cosine = 1.0 - hs * hs
    sine = hs * hc
    er = cr * cosine - ci * sine
    ei = cr * sine + ci * cosine
    i2 = inv * inv
    i3 = i2 * inv
    g = er + phi * ei
    h = ei - phi * er
    k = g * (3.0 * i2) - er
    return g, h, k, i3


def tile_terms(kind, row, col, cr_scale, ci_scale):
    x, y, z, ar, ai = row
    dx, dy, dz = x - col["y"][0], y - col["y"][1], z - col["y"][2]
    d = (dx, dy, dz)
    nx, ny, nz = col["n"]
    mn = dx * nx + dy * ny + dz * nz
    sq = dx * dx + dy * dy + dz * dz
    cr = ar * cr_scale + ai * ci_scale
    ci = ar * ci_scale - ai * cr_scale
    out = {}
    sa = sb = None
    if kind != 0:
        ex, ey, ez = col["t2"]
        e = dx * ex + dy * ey + dz * ez
        b = sq + col["at"]
        pts = []
        for sign in (-1, 1):
            if sign > 0:
                r2, m = b - e, mn - col["tn"]
            else:
                r2, m = b + e, mn + col["tn"]
            g, h, k, i3 = green(r2, cr, ci)
            pts.append((i3 * g, i3 * (h - m * k)))
        (a0, b0), (a2, b2) = pts
        sa, sb, da, db = a0 + a2, b0 + b2, a2 - a0, b2 - b0
    if kind != 1:
        g, h, k, i3 = green(sq + col["a"], cr, ci)
        a1, b1 = i3 * g, i3 * (h - mn * k)
        sa, sb = (a1, b1) if sa is None else (sa + a1, sb + b1)
    bd = [sb * v for v in d]
    ad = [sa * v for v in d]
    an = [sa * v for v in (nx, ny, nz)]
    pos = [p + q for p, q in zip(bd, an)]
    if kind == 0:
        return pos, pos, ad, None
    ts = col["ts"]
    pos = [p - db * t for p, t in zip(pos, ts)]
    return pos, pos, ad, da


def pair_kernel(batches, groups, lists_ref, rows_ref, cen_ref, nor_ref, tan_ref, area_ref, fwd_ref, col_out, row_out, table, racc, ctab, colv):
    tiles = lists_ref.shape[0] // 256
    rt = jnp.transpose(rows_ref[...])
    for g in range(groups):
        for q in range(5):
            v = jnp.broadcast_to(rt[q * 8:(q + 1) * 8, g:g + 1], (8, 128))
            table[g, q] = v * 4.0 if q < 3 else v
    table[groups] = jnp.concatenate([jnp.full((3, 8, 128), 1.0, F32), jnp.zeros((2, 8, 128), F32)], axis=0)
    racc[...] = jnp.zeros(racc.shape, F32)
    area = area_ref[...]
    spread = jnp.sqrt(area) * 2.4
    ysc = 4.0 * cen_ref[...]
    n16 = 16.0 * nor_ref[...]
    ts = spread * tan_ref[...]
    a16 = 16.0 * area
    at = a16 + jnp.sum(ts * ts, axis=0, keepdims=True)
    tn = jnp.sum(ts * n16, axis=0, keepdims=True)
    fw = fwd_ref[...] * (area * (1.0 / math.pi))
    rows = [ysc, n16, ts, 2.0 * ts, a16, at, tn, fw]
    pos = 0
    for r in rows:
        ctab[pos:pos + r.shape[0], :] = r
        pos += r.shape[0]

    def tile_body(t, _):
        lanes = pl.ds(pl.multiple_of(t * 128, 128), 128)
        for i in range(15):
            colv[i] = jnp.broadcast_to(ctab[i:i + 1, lanes], (8, 128))
        for kind, weight in enumerate((1.0, 0.5, 1.0 / 3.0)):
            for part in range(2):
                colv[15 + 2 * kind + part] = jnp.broadcast_to(ctab[15 + part:16 + part, lanes] * weight, (8, 128))

        def getcol():
            return dict(y=[colv[0], colv[1], colv[2]], n=[colv[3], colv[4], colv[5]], ts=[colv[6], colv[7], colv[8]],
                        t2=[colv[9], colv[10], colv[11]], a=colv[12], at=colv[13], tn=colv[14])
        zero = jnp.zeros((8, 128), F32)

        def make(kind, size):
            def body(it, state):
                pos, ids, acc = state
                col = getcol()
                frs, fis = colv[15 + 2 * kind], colv[16 + 2 * kind]
                acc = list(acc)
                news = []
                for j in range(size):
                    row = [table[ids[j], q] for q in range(5)]
                    gain, _, ad, da = tile_terms(kind, row, col, frs, fis)
                    for q in range(3):
                        acc[q] = acc[q] + gain[q]
                        acc[3 + q] = acc[3 + q] + ad[q]
                    if da is not None:
                        acc[6] = acc[6] + da
                    news.append(gain)
                olds = [[racc[ids[j], q] for q in range(3)] for j in range(size)]
                for j in range(size):
                    for q in range(3):
                        racc[ids[j], q] = olds[j][q] + news[j][q]
                pos = pos + size
                return pos, tuple(lists_ref[pos + j] for j in range(most)), tuple(acc)
            return body
        most = max(batches)
        start = t * 256
        state = (start, tuple(lists_ref[start + j] for j in range(most)), (zero,) * 7)
        for kind in range(3):
            state = lax.fori_loop(0, lists_ref[start + 253 + kind], make(kind, batches[kind]), state)
        sums = [jnp.sum(v, axis=0, keepdims=True) for v in state[2]]
        for q in range(3):
            col_out[q:q + 1, lanes] = -sums[q]
            tsr = ctab[6 + q:7 + q, lanes]
            col_out[3 + q:4 + q, lanes] = 4.0 * (sums[3 + q] - sums[6] * tsr)
        return 0

    lax.fori_loop(0, tiles, tile_body, 0)
    lane = lax.broadcasted_iota(jnp.int32, (8, 128), 1)
    outs = [jnp.zeros((8, 128), F32) for _ in range(3)]
    for g in range(groups):
        for q in range(3):
            s = jnp.sum(racc[g, q], axis=1, keepdims=True)
            outs[q] = jnp.where(lane == g, s, outs[q])
    for q in range(3):
        row_out[q * 8:(q + 1) * 8, :] = outs[q]


def pair_call(lists, rows, cen, nor, tan, area, fwd, batches=(8, 4, 4)):
    el = cen.shape[1]
    groups = rows.shape[0]
    vm = pl.BlockSpec(memory_space=pltpu.VMEM)
    return pl.pallas_call(
        functools.partial(pair_kernel, batches, groups),
        out_shape=(jax.ShapeDtypeStruct((6, el), F32), jax.ShapeDtypeStruct((24, 128), F32)),
        in_specs=[pl.BlockSpec(memory_space=pltpu.SMEM)] + [vm] * 6,
        out_specs=(vm, vm),
        scratch_shapes=[pltpu.VMEM((groups + 1, 5, 8, 128), F32), pltpu.VMEM((groups + 1, 3, 8, 128), F32),
                        pltpu.VMEM((24, el), F32), pltpu.VMEM((21, 8, 128), F32)],
        compiler_params=pltpu.CompilerParams(vmem_limit_bytes=16 << 20), name="pairs",
    )(lists, rows, cen, nor, tan, area, fwd)


def dot_nn(a, b):
    return lax.dot_general(a, b, (((1,), (0,)), ((), ())), preferred_element_type=F32)


def dot_nt(a, b):
    return lax.dot_general(a, b, (((1,), (1,)), ((), ())), preferred_element_type=F32)


def iota(shape, dim):
    return lax.broadcasted_iota(jnp.int32, shape, dim)


BF16 = jnp.bfloat16


def split3(v):
    hi = v.astype(BF16)
    rest = v - hi.astype(F32)
    mid = rest.astype(BF16)
    low = (rest - mid.astype(F32)).astype(BF16)
    return hi, mid, low


def ones_where(mask):
    return jnp.where(mask, 1.0, 0.0)


def make_lists(flags, batches):
    before = ones_where(iota((128, 128), 0) < iota((128, 128), 1)).astype(BF16)
    tile = iota((8, 128), 0)
    lane = iota((8, 128), 1)
    pos = jnp.zeros((8, 128), F32)
    base = jnp.zeros((8, 1), F32)
    counts = []
    for kind in range(3):
        mask = ones_where(flags == float(kind))
        inside = dot_nn(mask.astype(BF16), before)
        total = jnp.sum(mask, axis=1, keepdims=True)
        pos = pos + mask * (inside + base)
        nb = jnp.floor((total + float(batches[kind] - 1)) * (1.0 / batches[kind]))
        base = base + nb * float(batches[kind])
        counts.append(nb)
    posi = pos.astype(jnp.int32)
    slot = iota((256, 128), 0)
    out = jnp.zeros((8, 256), F32)
    for t in range(8):
        hit = ones_where(slot == posi[t:t + 1, :]).astype(BF16)
        value = jnp.where(tile == t, (((lane & 15) << 3) + (lane >> 4) - 128).astype(F32), 0.0).astype(BF16)
        out = out + dot_nt(value, hit)
    out = out + 128.0
    wide = iota((8, 256), 1)
    for kind in range(3):
        out = jnp.where(wide == 253 + kind, counts[kind], out)
    return out.astype(jnp.int32)


def lookup_slots(table, corners):
    parts = jnp.concatenate([(table >> 8).astype(F32).astype(BF16), (table & 255).astype(F32).astype(BF16)], axis=1)
    width = 256
    lo_iota = iota((128, width), 0)
    hi_iota = iota((512, width), 0)
    rows = []
    for n in range(corners.shape[0]):
        pieces = []
        for cb in range(corners.shape[1] // width):
            v = corners[n:n + 1, cb * width:(cb + 1) * width]
            hit = lo_iota == (v & 127)
            rhs = jnp.concatenate([jnp.where(hit, 256.0, 0.0), jnp.where(hit, 1.0, 0.0)], axis=0).astype(BF16)
            sel = dot_nn(parts, rhs)
            pieces.append(jnp.sum(jnp.where(hi_iota == (v >> 7), sel, 0.0), axis=0, keepdims=True))
        rows.append(jnp.concatenate(pieces, axis=1))
    return jnp.concatenate(rows, axis=0).astype(jnp.int32)


def patch_ranks(patches):
    width = 256
    before = ones_where(iota((width, width), 0) < iota((width, width), 1)).astype(BF16)
    sub = iota((128, width), 0)
    carry = jnp.zeros((128, 1), F32)
    rows = []
    for n in range(patches.shape[0]):
        pieces = []
        for cb in range(patches.shape[1] // width):
            hit = ones_where(sub == patches[n:n + 1, cb * width:(cb + 1) * width])
            earlier = dot_nn(hit.astype(BF16), before) + carry
            pieces.append(jnp.sum(hit * earlier, axis=0, keepdims=True))
            carry = carry + jnp.sum(hit, axis=1, keepdims=True)
        rows.append(jnp.concatenate(pieces, axis=1))
    return jnp.concatenate(rows, axis=0)


def bucket_terms(values, slots, ranks):
    width = values.shape[1]
    hit = ones_where(iota((128, width), 0) == (slots >> 9)).astype(BF16)
    mine = (iota((192, width), 0) >> 3) == ranks
    total = None
    for part in split3(values):
        rhs = jnp.where(mine, jnp.concatenate([part.astype(F32)] * 24, axis=0), 0.0).astype(BF16)
        term = dot_nt(hit, rhs)
        total = term if total is None else total + term
    return total


def add_up(recv, rows):
    turned = jnp.transpose(recv)
    sub = iota((512, 128), 0).astype(F32)
    row8 = iota((8, 128), 0)
    row8f = row8.astype(F32)
    total = jnp.zeros((24, 512), F32)
    for pair in range(12):
        parts, hits = [], []
        for q in (2 * pair, 2 * pair + 1):
            eight = turned[q * 8:(q + 1) * 8, :]
            mine = ones_where(row8f == eight[7:8, :])
            for comp in range(3):
                gain = jnp.sum(mine * rows[comp * 8:(comp + 1) * 8], axis=0, keepdims=True)
                eight = eight + jnp.where(row8 == comp, gain, 0.0)
            hits.append(ones_where(sub == eight[6:7, :]).astype(BF16))
            parts.append(jnp.concatenate([p.astype(F32) for p in split3(eight)], axis=0))
        lhs = jnp.concatenate(parts, axis=1).astype(BF16)
        total = total + dot_nt(lhs, jnp.concatenate(hits, axis=1))
    return total[0:8] + total[8:16] + total[16:24]


VM = pl.BlockSpec(memory_space=pltpu.VMEM)
SLAB_DEV = 8
BATCHES = (8, 4, 4)
N_ROW, N_COL = 8, 16
S = jax.ShapeDtypeStruct
I32 = jnp.int32
DMA = pltpu.SemaphoreType.DMA
MESH = pl.DeviceIdType.MESH


def greet(me):
    barrier = pltpu.get_barrier_semaphore()
    for axis, count in (("row", N_ROW), ("col", N_COL)):
        def signal(k, _, axis=axis, count=count):
            pl.semaphore_signal(barrier, inc=1, device_id={axis: lax.rem(me[axis] + k, count)}, device_id_type=MESH)
            return 0
        lax.fori_loop(1, count, signal, 0)
    return barrier


class Swap:
    def __init__(self, me, axis, count, piece, slot, sems):
        self.me, self.count, self.axis = me[axis], count, axis
        self.piece, self.slot = piece, slot
        self.send_sem, self.recv_sem = sems

    def copy(self, peer, slot):
        return pltpu.make_async_remote_copy(
            src_ref=self.piece(peer), dst_ref=self.slot(slot), send_sem=self.send_sem.at[peer], recv_sem=self.recv_sem.at[slot],
            device_id={self.axis: peer}, device_id_type=MESH)

    def each(self, act):
        def visit(k, _):
            act(lax.rem(self.me + k, self.count))
            return 0
        lax.fori_loop(1, self.count, visit, 0)

    def start(self):
        self.each(lambda peer: self.copy(peer, self.me).start())

    def receive(self):
        self.each(lambda peer: self.copy(peer, peer).wait_recv())

    def drain(self):
        self.each(lambda peer: self.copy(peer, peer).wait_send())


def swap_sems(n):
    return [DMA((n,)), DMA((n,))]


def gather_kernel(cen_ref, adj_ref, flags_ref, table_ref, corners_ref, rows_out, lists_out, codes_out,
                  own, rowblk, rowall, flagall, fs, fr, cs, cr, rs, rr):
    me = {"row": lax.axis_index("row"), "col": lax.axis_index("col")}
    barrier = greet(me)
    lane = iota((1, 128), 1)
    packed = jnp.zeros((1, 128), F32)
    for q in range(5):
        line = cen_ref[q:q + 1, 0:128] if q < 3 else adj_ref[q - 3:q - 2, 0:128]
        if q:
            line = pltpu.roll(line, 8 * q, 1)
        packed = jnp.where((lane >> 3) == q, line, packed)
    own[...] = packed
    rowblk[pl.ds(me["col"], 1), :] = packed
    flagall[me["row"]] = flags_ref[me["row"]]
    slots = lookup_slots(table_ref[...], corners_ref[...])
    codes_out[...] = slots * 32 + patch_ranks(slots >> 9).astype(I32)
    pl.semaphore_wait(barrier, N_ROW + N_COL - 2)
    flag_swap = Swap(me, "row", N_ROW, lambda peer: flags_ref.at[peer], lambda slot: flagall.at[slot], (fs, fr))
    col_swap = Swap(me, "col", N_COL, lambda peer: own, lambda slot: rowblk.at[pl.ds(slot, 1), :], (cs, cr))
    row_swap = Swap(me, "row", N_ROW, lambda peer: rowblk,
                    lambda slot: rowall.at[pl.ds(pl.multiple_of(slot * N_COL, N_COL), N_COL), :], (rs, rr))
    col_swap.start()
    flag_swap.start()
    flag_swap.receive()
    flags = jnp.concatenate([flagall[r] for r in range(N_ROW)], axis=1).astype(F32)
    lists = make_lists(flags, BATCHES)
    for t in range(8):
        for half in range(2):
            lists_out[2 * t + half:2 * t + half + 1, :] = lists[t:t + 1, half * 128:(half + 1) * 128]
    col_swap.receive()
    row_swap.start()
    rowall[pl.ds(pl.multiple_of(me["row"] * N_COL, N_COL), N_COL), :] = rowblk[...]
    row_swap.receive()
    for c in range(N_COL):
        rows_out[c * N_ROW:(c + 1) * N_ROW, :] = rowall[pl.ds(c, N_ROW, stride=N_COL), :]
    for swap in (col_swap, flag_swap, row_swap):
        swap.drain()


def project(modes_ref, vertex, acc_ref):
    total = None
    for comp in range(6):
        for k in range(4):
            lanes = slice(k * 128, (k + 1) * 128)
            term = modes_ref[comp, :, lanes] * vertex[comp:comp + 1, lanes]
            total = term if total is None else total + term
    acc_ref[...] = jnp.zeros(acc_ref.shape, F32)
    acc_ref[0:total.shape[0], :] = total
    ones = jnp.ones((8, 128), BF16)
    return sum(dot_nt(ones, p) for p in split3(acc_ref[...]))


def finish_kernel(col_ref, row_ref, codes_ref, modes_hbm, vertex_out, grad_out,
                  modes, part8, sumrow, part16, send, mid, stage, recv, acc, grad, grad8, mid_grad, grad16,
                  msem, a0, a1, b0, b1, c0, c1, d0, d1, e0, e1, f0, f1):
    me = {"row": lax.axis_index("row"), "col": lax.axis_index("col")}
    r, c = me["row"], me["col"]
    barrier = greet(me)
    fetch = pltpu.make_async_copy(modes_hbm, modes, msem)
    fetch.start()

    def halves(ref, i):
        return ref.at[:, pl.ds(pl.multiple_of(i * N_COL, N_COL), N_COL), :]

    swap_a = Swap(me, "row", N_ROW, lambda peer: row_ref, lambda slot: part8.at[slot], (a0, a1))
    swap_b = Swap(me, "col", N_COL, lambda peer: sumrow, lambda slot: part16.at[slot], (b0, b1))
    swap_c = Swap(me, "row", N_ROW, lambda peer: halves(send, peer), lambda slot: halves(mid, slot), (c0, c1))
    swap_d = Swap(me, "col", N_COL, lambda peer: stage.at[peer], lambda slot: recv.at[slot], (d0, d1))
    swap_e = Swap(me, "row", N_ROW, lambda peer: grad, lambda slot: grad8.at[slot], (e0, e1))
    swap_f = Swap(me, "col", N_COL, lambda peer: mid_grad, lambda slot: grad16.at[slot], (f0, f1))

    width = 256
    third = 1.0 / 3.0
    total = jnp.zeros((128, 192), F32)
    for n in range(3):
        for cb in range(col_ref.shape[1] // width):
            cols = slice(cb * width, (cb + 1) * width)
            code = codes_ref[n:n + 1, cols]
            slots = code >> 5
            element = jnp.minimum(iota((1, width), 1) + cb * width, SLAB_DEV).astype(F32)
            eight = jnp.concatenate([col_ref[:, cols] * third, (slots & 511).astype(F32), element], axis=0)
            total = total + bucket_terms(eight, slots, code & 31)
    send[0] = total[:, 0:128]
    send[1] = jnp.concatenate([total[:, 128:192], jnp.zeros((128, 64), F32)], axis=1)
    pl.semaphore_wait(barrier, N_ROW + N_COL - 2)
    swap_a.start()
    swap_c.start()
    part8[r] = row_ref[...]
    halves(mid, r)[...] = halves(send, r)[...]
    swap_a.receive()
    sumrow[...] = sum(part8[i] for i in range(N_ROW)) * third
    swap_b.start()
    part16[c] = sumrow[...]
    swap_c.receive()
    for i in range(N_COL):
        for half in range(2):
            stage[i, :, half * 128:(half + 1) * 128] = mid[half, pl.ds(i, N_ROW, stride=N_COL), :]
    swap_d.start()
    recv[c] = stage[c]
    swap_b.receive()
    rows = sum(part16[i] for i in range(N_COL))
    swap_d.receive()
    vertex = add_up(recv[...].reshape(128, 256), rows)
    vertex_out[...] = vertex[0:6]
    fetch.wait()
    grad[...] = project(modes, vertex, acc)[0:1]
    swap_e.start()
    grad8[r] = grad[...]
    swap_e.receive()
    mid_grad[...] = sum(grad8[i] for i in range(N_ROW))
    swap_f.start()
    grad16[c] = mid_grad[...]
    swap_f.receive()
    grad_out[...] = sum(grad16[i] for i in range(N_COL))
    for swap in (swap_a, swap_b, swap_c, swap_d, swap_e, swap_f):
        swap.drain()


def emit_kernel(vertex_ref, grad_ref, vertex_out, grad_out):
    vertex_out[...] = vertex_ref[...]
    grad_out[...] = grad_ref[...].reshape(grad_ref.shape[1])[0:grad_out.shape[0]]


def body(centroid, normals, tangent, element_area, forward_field, adjoint_field, corners, slot_map, quad_order, morph_modes):
    el = centroid.shape[1]
    modes_t = jnp.transpose(morph_modes, (1, 0, 2))
    flags = jnp.transpose(quad_order[:, :, 0, :], (1, 2, 0))
    rows, lists, codes = pl.pallas_call(
        gather_kernel,
        out_shape=(S((128, 128), F32), S((16, 128), I32), S((3, el), I32)),
        in_specs=[VM] * 5, out_specs=(VM,) * 3,
        scratch_shapes=[pltpu.VMEM((1, 128), F32), pltpu.VMEM((16, 128), F32), pltpu.VMEM((128, 128), F32),
                        pltpu.VMEM((8, 8, 16), I32)] + swap_sems(8) + swap_sems(16) + swap_sems(8),
        compiler_params=pltpu.CompilerParams(collective_id=0, has_side_effects=True, vmem_limit_bytes=16 << 20), name="gather",
    )(centroid, adjoint_field, flags, slot_map.reshape(512, 128), corners)
    col_part, row_part = pair_call(lists.reshape(2048), rows, centroid, normals, tangent, element_area[None, :], forward_field, BATCHES)
    vertex, grad = pl.pallas_call(
        finish_kernel,
        out_shape=(S((6, 512), F32), S((1, 384), F32)),
        in_specs=[VM] * 3 + [pl.BlockSpec(memory_space=pl.ANY)], out_specs=(VM, VM),
        scratch_shapes=[pltpu.VMEM((6, 300, 512), F32), pltpu.VMEM((8, 24, 128), F32), pltpu.VMEM((24, 128), F32),
                        pltpu.VMEM((16, 24, 128), F32), pltpu.VMEM((2, 128, 128), F32), pltpu.VMEM((2, 128, 128), F32),
                        pltpu.VMEM((16, 8, 256), F32), pltpu.VMEM((16, 8, 256), F32), pltpu.VMEM((384, 128), F32),
                        pltpu.VMEM((1, 384), F32), pltpu.VMEM((8, 1, 384), F32), pltpu.VMEM((1, 384), F32),
                        pltpu.VMEM((16, 1, 384), F32), DMA] + (swap_sems(8) + swap_sems(16)) * 3,
        compiler_params=pltpu.CompilerParams(collective_id=1, has_side_effects=True, vmem_limit_bytes=16 << 20), name="finish",
    )(col_part, row_part, codes, modes_t)
    return pl.pallas_call(emit_kernel, out_shape=(S((6, 512), F32), S((300,), F32)), in_specs=[VM] * 2, out_specs=(VM, VM),
                          compiler_params=pltpu.CompilerParams(vmem_limit_bytes=16 << 20), name="emit")(vertex, grad)


def solution(mesh):
    from jax.sharding import PartitionSpec as P
    every = ("row", "col")
    return jax.shard_map(
        body, mesh=mesh,
        in_specs=(P(None, every), P(None, every), P(None, every), P(every), P(None, every), P(None, every), P(None, every),
                  P(), P("row", None, "col", None), P(None, None, every)),
        out_specs=(P(None, every), P()), check_vma=False)
```

```python
import math, functools
import jax, jax.numpy as jnp
from jax import lax
from jax.experimental import pallas as pl
from jax.experimental.pallas import tpu as pltpu

F32 = jnp.float32
MAGIC = 12582912.0
INV_TURN = 1.0 / (2.0 * math.pi)
SIN_C = (4.442883014678955, -7.308245658874512, 3.6063544750213623, -0.8461129069328308, 0.10982698947191238)
COS_C = (1.4142135381698608, -6.978850841522217, 5.7394609451293945, -1.8835630416870117, 0.31069818139076233)


def horner(coeffs, z):
    total = z * coeffs[-1] + coeffs[-2]
    for value in coeffs[-3::-1]:
        total = total * z + value
    return total


def green(r2, cr, ci):
    inv = lax.rsqrt(r2)
    phi = r2 * inv
    turn = phi * INV_TURN
    frac = turn - jnp.round(turn)
    z = frac * frac
    hs = frac * horner(SIN_C, z)
    hc = horner(COS_C, z)
    cosine = 1.0 - hs * hs
    sine = hs * hc
    er = cr * cosine - ci * sine
    ei = cr * sine + ci * cosine
    i2 = inv * inv
    i3 = i2 * inv
    g = er + phi * ei
    h = ei - phi * er
    k = g * (3.0 * i2) - er
    return g, h, k, i3


def tile_terms(kind, row, col, cr_scale, ci_scale):
    x, y, z, ar, ai = row
    dx, dy, dz = x - col["y"][0], y - col["y"][1], z - col["y"][2]
    d = (dx, dy, dz)
    nx, ny, nz = col["n"]
    mn = dx * nx + dy * ny + dz * nz
    sq = dx * dx + dy * dy + dz * dz
    cr = ar * cr_scale + ai * ci_scale
    ci = ar * ci_scale - ai * cr_scale
    out = {}
    sa = sb = None
    if kind != 0:
        ex, ey, ez = col["t2"]
        e = dx * ex + dy * ey + dz * ez
        b = sq + col["at"]
        pts = []
        for sign in (-1, 1):
            if sign > 0:
                r2, m = b - e, mn - col["tn"]
            else:
                r2, m = b + e, mn + col["tn"]
            g, h, k, i3 = green(r2, cr, ci)
            pts.append((i3 * g, i3 * (h - m * k)))
        (a0, b0), (a2, b2) = pts
        sa, sb, da, db = a0 + a2, b0 + b2, a2 - a0, b2 - b0
    if kind != 1:
        g, h, k, i3 = green(sq + col["a"], cr, ci)
        a1, b1 = i3 * g, i3 * (h - mn * k)
        sa, sb = (a1, b1) if sa is None else (sa + a1, sb + b1)
    bd = [sb * v for v in d]
    ad = [sa * v for v in d]
    an = [sa * v for v in (nx, ny, nz)]
    pos = [p + q for p, q in zip(bd, an)]
    if kind == 0:
        return pos, pos, ad, None
    ts = col["ts"]
    pos = [p - db * t for p, t in zip(pos, ts)]
    return pos, pos, ad, da


def pair_kernel(batches, groups, lists_ref, rows_ref, cen_hbm, nor_hbm, tan_hbm, area_hbm, fwd_hbm, col_out, row_out,
                table, racc, ctab, colv, cen_ref, nor_ref, tan_ref, area_ref, fwd_ref, insem):
    copies = fetch_all((cen_hbm, nor_hbm, tan_hbm, area_hbm, fwd_hbm), (cen_ref, nor_ref, tan_ref, area_ref, fwd_ref), insem)
    tiles = lists_ref.shape[0] // 256
    rt = jnp.transpose(rows_ref[...])
    for g in range(groups):
        for q in range(5):
            v = jnp.broadcast_to(rt[q * 8:(q + 1) * 8, g:g + 1], (8, 128))
            table[g, q] = v * 4.0 if q < 3 else v
    table[groups] = jnp.concatenate([jnp.full((3, 8, 128), 1.0, F32), jnp.zeros((2, 8, 128), F32)], axis=0)
    racc[...] = jnp.zeros(racc.shape, F32)
    for copy in copies:
        copy.wait()
    area = area_ref[...]
    spread = jnp.sqrt(area) * 2.4
    ysc = 4.0 * cen_ref[...]
    n16 = 16.0 * nor_ref[...]
    ts = spread * tan_ref[...]
    a16 = 16.0 * area
    at = a16 + jnp.sum(ts * ts, axis=0, keepdims=True)
    tn = jnp.sum(ts * n16, axis=0, keepdims=True)
    fw = fwd_ref[...] * (area * (1.0 / math.pi))
    rows = [ysc, n16, ts, 2.0 * ts, a16, at, tn, fw]
    pos = 0
    for r in rows:
        ctab[pos:pos + r.shape[0], :] = r
        pos += r.shape[0]

    def tile_body(t, _):
        lanes = pl.ds(pl.multiple_of(t * 128, 128), 128)
        for i in range(15):
            colv[i] = jnp.broadcast_to(ctab[i:i + 1, lanes], (8, 128))
        for kind, weight in enumerate((1.0, 0.5, 1.0 / 3.0)):
            for part in range(2):
                colv[15 + 2 * kind + part] = jnp.broadcast_to(ctab[15 + part:16 + part, lanes] * weight, (8, 128))

        def getcol():
            return dict(y=[colv[0], colv[1], colv[2]], n=[colv[3], colv[4], colv[5]], ts=[colv[6], colv[7], colv[8]],
                        t2=[colv[9], colv[10], colv[11]], a=colv[12], at=colv[13], tn=colv[14])
        zero = jnp.zeros((8, 128), F32)

        def make(kind, size):
            def body(it, state):
                pos, ids, acc = state
                col = getcol()
                frs, fis = colv[15 + 2 * kind], colv[16 + 2 * kind]
                acc = list(acc)
                news = []
                for j in range(size):
                    row = [table[ids[j], q] for q in range(5)]
                    gain, _, ad, da = tile_terms(kind, row, col, frs, fis)
                    for q in range(3):
                        acc[q] = acc[q] + gain[q]
                        acc[3 + q] = acc[3 + q] + ad[q]
                    if da is not None:
                        acc[6] = acc[6] + da
                    news.append(gain)
                olds = [[racc[ids[j], q] for q in range(3)] for j in range(size)]
                for j in range(size):
                    for q in range(3):
                        racc[ids[j], q] = olds[j][q] + news[j][q]
                pos = pos + size
                return pos, tuple(lists_ref[pos + j] for j in range(most)), tuple(acc)
            return body
        most = max(batches)
        start = t * 256
        state = (start, tuple(lists_ref[start + j] for j in range(most)), (zero,) * 7)
        for kind in range(3):
            state = lax.fori_loop(0, lists_ref[start + 253 + kind], make(kind, batches[kind]), state)
        sums = [jnp.sum(v, axis=0, keepdims=True) for v in state[2]]
        for q in range(3):
            col_out[q:q + 1, lanes] = -sums[q]
            tsr = ctab[6 + q:7 + q, lanes]
            col_out[3 + q:4 + q, lanes] = 4.0 * (sums[3 + q] - sums[6] * tsr)
        return 0

    lax.fori_loop(0, tiles, tile_body, 0)
    lane = lax.broadcasted_iota(jnp.int32, (8, 128), 1)
    outs = [jnp.zeros((8, 128), F32) for _ in range(3)]
    for g in range(groups):
        for q in range(3):
            s = jnp.sum(racc[g, q], axis=1, keepdims=True)
            outs[q] = jnp.where(lane == g, s, outs[q])
    for q in range(3):
        row_out[q * 8:(q + 1) * 8, :] = outs[q]


def pair_call(lists, rows, cen, nor, tan, area, fwd, batches=(8, 4, 4)):
    el = cen.shape[1]
    groups = rows.shape[0]
    vm = pl.BlockSpec(memory_space=pltpu.VMEM)
    return pl.pallas_call(
        functools.partial(pair_kernel, batches, groups),
        out_shape=(jax.ShapeDtypeStruct((6, el), F32), jax.ShapeDtypeStruct((24, 128), F32)),
        in_specs=[pl.BlockSpec(memory_space=pltpu.SMEM), vm] + [pl.BlockSpec(memory_space=pltpu.HBM)] * 5,
        out_specs=(vm, vm),
        scratch_shapes=[pltpu.VMEM((groups + 1, 5, 8, 128), F32), pltpu.VMEM((groups + 1, 3, 8, 128), F32),
                        pltpu.VMEM((24, el), F32), pltpu.VMEM((21, 8, 128), F32), pltpu.VMEM((3, el), F32),
                        pltpu.VMEM((3, el), F32), pltpu.VMEM((3, el), F32), pltpu.VMEM((1, el), F32), pltpu.VMEM((2, el), F32),
                        pltpu.SemaphoreType.DMA((5,))],
        compiler_params=pltpu.CompilerParams(vmem_limit_bytes=16 << 20), name="pairs",
    )(lists, rows, cen, nor, tan, area, fwd)


def dot_nn(a, b):
    return lax.dot_general(a, b, (((1,), (0,)), ((), ())), preferred_element_type=F32)


def dot_nt(a, b):
    return lax.dot_general(a, b, (((1,), (1,)), ((), ())), preferred_element_type=F32)


def iota(shape, dim):
    return lax.broadcasted_iota(jnp.int32, shape, dim)


BF16 = jnp.bfloat16


def split3(v):
    hi = v.astype(BF16)
    rest = v - hi.astype(F32)
    mid = rest.astype(BF16)
    low = (rest - mid.astype(F32)).astype(BF16)
    return hi, mid, low


def ones_where(mask):
    return jnp.where(mask, 1.0, 0.0)


def make_lists(flags, batches):
    before = ones_where(iota((128, 128), 0) < iota((128, 128), 1)).astype(BF16)
    tile = iota((8, 128), 0)
    lane = iota((8, 128), 1)
    pos = jnp.zeros((8, 128), F32)
    base = jnp.zeros((8, 1), F32)
    counts = []
    for kind in range(3):
        mask = ones_where(flags == float(kind))
        inside = dot_nn(mask.astype(BF16), before)
        total = jnp.sum(mask, axis=1, keepdims=True)
        pos = pos + mask * (inside + base)
        nb = jnp.floor((total + float(batches[kind] - 1)) * (1.0 / batches[kind]))
        base = base + nb * float(batches[kind])
        counts.append(nb)
    posi = pos.astype(jnp.int32)
    slot = iota((256, 128), 0)
    out = jnp.zeros((8, 256), F32)
    for t in range(8):
        hit = ones_where(slot == posi[t:t + 1, :]).astype(BF16)
        value = jnp.where(tile == t, (((lane & 15) << 3) + (lane >> 4) - 128).astype(F32), 0.0).astype(BF16)
        out = out + dot_nt(value, hit)
    out = out + 128.0
    wide = iota((8, 256), 1)
    for kind in range(3):
        out = jnp.where(wide == 253 + kind, counts[kind], out)
    return out.astype(jnp.int32)


def lookup_slots(table, corners):
    parts = jnp.concatenate([(table >> 8).astype(F32).astype(BF16), (table & 255).astype(F32).astype(BF16)], axis=1)
    width = 256
    lo_iota = iota((128, width), 0)
    hi_iota = iota((512, width), 0)
    rows = []
    for n in range(corners.shape[0]):
        pieces = []
        for cb in range(corners.shape[1] // width):
            v = corners[n:n + 1, cb * width:(cb + 1) * width]
            hit = lo_iota == (v & 127)
            rhs = jnp.concatenate([jnp.where(hit, 256.0, 0.0), jnp.where(hit, 1.0, 0.0)], axis=0).astype(BF16)
            sel = dot_nn(parts, rhs)
            pieces.append(jnp.sum(jnp.where(hi_iota == (v >> 7), sel, 0.0), axis=0, keepdims=True))
        rows.append(jnp.concatenate(pieces, axis=1))
    return jnp.concatenate(rows, axis=0).astype(jnp.int32)


def patch_ranks(patches):
    width = 256
    before = ones_where(iota((width, width), 0) < iota((width, width), 1)).astype(BF16)
    sub = iota((128, width), 0)
    carry = jnp.zeros((128, 1), F32)
    rows = []
    for n in range(patches.shape[0]):
        pieces = []
        for cb in range(patches.shape[1] // width):
            hit = ones_where(sub == patches[n:n + 1, cb * width:(cb + 1) * width])
            earlier = dot_nn(hit.astype(BF16), before) + carry
            pieces.append(jnp.sum(hit * earlier, axis=0, keepdims=True))
            carry = carry + jnp.sum(hit, axis=1, keepdims=True)
        rows.append(jnp.concatenate(pieces, axis=1))
    return jnp.concatenate(rows, axis=0)


def bucket_terms(values, slots, ranks):
    width = values.shape[1]
    hit = ones_where(iota((128, width), 0) == (slots >> 9)).astype(BF16)
    mine = (iota((192, width), 0) >> 3) == ranks
    total = None
    for part in split3(values):
        rhs = jnp.where(mine, jnp.concatenate([part.astype(F32)] * 24, axis=0), 0.0).astype(BF16)
        term = dot_nt(hit, rhs)
        total = term if total is None else total + term
    return total


def add_up(recv, rows):
    turned = jnp.transpose(recv)
    sub = iota((512, 128), 0).astype(F32)
    row8 = iota((8, 128), 0)
    row8f = row8.astype(F32)
    total = jnp.zeros((24, 512), F32)
    for pair in range(12):
        parts, hits = [], []
        for q in (2 * pair, 2 * pair + 1):
            eight = turned[q * 8:(q + 1) * 8, :]
            mine = ones_where(row8f == eight[7:8, :])
            for comp in range(3):
                gain = jnp.sum(mine * rows[comp * 8:(comp + 1) * 8], axis=0, keepdims=True)
                eight = eight + jnp.where(row8 == comp, gain, 0.0)
            hits.append(ones_where(sub == eight[6:7, :]).astype(BF16))
            parts.append(jnp.concatenate([p.astype(F32) for p in split3(eight)], axis=0))
        lhs = jnp.concatenate(parts, axis=1).astype(BF16)
        total = total + dot_nt(lhs, jnp.concatenate(hits, axis=1))
    return total[0:8] + total[8:16] + total[16:24]


VM = pl.BlockSpec(memory_space=pltpu.VMEM)
HB = pl.BlockSpec(memory_space=pltpu.HBM)
SLAB_DEV = 8
BATCHES = (8, 4, 4)
N_ROW, N_COL = 8, 16
S = jax.ShapeDtypeStruct
I32 = jnp.int32
DMA = pltpu.SemaphoreType.DMA
MESH = pl.DeviceIdType.MESH


def greet(me):
    barrier = pltpu.get_barrier_semaphore()
    for axis, count in (("row", N_ROW), ("col", N_COL)):
        def signal(k, _, axis=axis, count=count):
            pl.semaphore_signal(barrier, inc=1, device_id={axis: lax.rem(me[axis] + k, count)}, device_id_type=MESH)
            return 0
        lax.fori_loop(1, count, signal, 0)
    return barrier


class Swap:
    def __init__(self, me, axis, count, piece, slot, sems):
        self.me, self.count, self.axis = me[axis], count, axis
        self.piece, self.slot = piece, slot
        self.send_sem, self.recv_sem = sems

    def copy(self, peer, slot):
        return pltpu.make_async_remote_copy(
            src_ref=self.piece(peer), dst_ref=self.slot(slot), send_sem=self.send_sem.at[peer], recv_sem=self.recv_sem.at[slot],
            device_id={self.axis: peer}, device_id_type=MESH)

    def each(self, act):
        def visit(k, _):
            act(lax.rem(self.me + k, self.count))
            return 0
        lax.fori_loop(1, self.count, visit, 0)

    def start(self):
        self.each(lambda peer: self.copy(peer, self.me).start())

    def receive(self):
        self.each(lambda peer: self.copy(peer, peer).wait_recv())

    def drain(self):
        self.each(lambda peer: self.copy(peer, peer).wait_send())


def swap_sems(n):
    return [DMA((n,)), DMA((n,))]


def fetch_all(sources, targets, sems):
    copies = [pltpu.make_async_copy(src, dst, sems.at[i]) for i, (src, dst) in enumerate(zip(sources, targets))]
    for copy in copies:
        copy.start()
    return copies


def gather_kernel(cen_hbm, adj_hbm, flags_hbm, table_hbm, corners_hbm, rows_out, lists_out, codes_out,
                  cen_ref, adj_ref, flags_ref, table_ref, corners_ref, insem, own, rowblk, rowall, flagall, fs, fr, cs, cr, rs, rr):
    me = {"row": lax.axis_index("row"), "col": lax.axis_index("col")}
    copies = fetch_all((cen_hbm, adj_hbm, flags_hbm, table_hbm, corners_hbm),
                       (cen_ref, adj_ref, flags_ref, table_ref, corners_ref), insem)
    barrier = greet(me)
    lane = iota((1, 128), 1)
    packed = jnp.zeros((1, 128), F32)
    copies[0].wait()
    copies[1].wait()
    for q in range(5):
        line = cen_ref[q:q + 1, 0:128] if q < 3 else adj_ref[q - 3:q - 2, 0:128]
        if q:
            line = pltpu.roll(line, 8 * q, 1)
        packed = jnp.where((lane >> 3) == q, line, packed)
    own[...] = packed
    rowblk[pl.ds(me["col"], 1), :] = packed
    copies[2].wait()
    flagall[me["row"]] = flags_ref[me["row"]]
    copies[3].wait()
    copies[4].wait()
    slots = lookup_slots(table_ref[...], corners_ref[...])
    codes_out[...] = slots * 32 + patch_ranks(slots >> 9).astype(I32)
    pl.semaphore_wait(barrier, N_ROW + N_COL - 2)
    flag_swap = Swap(me, "row", N_ROW, lambda peer: flags_ref.at[peer], lambda slot: flagall.at[slot], (fs, fr))
    col_swap = Swap(me, "col", N_COL, lambda peer: own, lambda slot: rowblk.at[pl.ds(slot, 1), :], (cs, cr))
    row_swap = Swap(me, "row", N_ROW, lambda peer: rowblk,
                    lambda slot: rowall.at[pl.ds(pl.multiple_of(slot * N_COL, N_COL), N_COL), :], (rs, rr))
    col_swap.start()
    flag_swap.start()
    flag_swap.receive()
    flags = jnp.concatenate([flagall[r] for r in range(N_ROW)], axis=1).astype(F32)
    lists = make_lists(flags, BATCHES)
    for t in range(8):
        for half in range(2):
            lists_out[2 * t + half:2 * t + half + 1, :] = lists[t:t + 1, half * 128:(half + 1) * 128]
    col_swap.receive()
    row_swap.start()
    rowall[pl.ds(pl.multiple_of(me["row"] * N_COL, N_COL), N_COL), :] = rowblk[...]
    row_swap.receive()
    for c in range(N_COL):
        rows_out[c * N_ROW:(c + 1) * N_ROW, :] = rowall[pl.ds(c, N_ROW, stride=N_COL), :]
    for swap in (col_swap, flag_swap, row_swap):
        swap.drain()


def project(modes_ref, vertex, acc_ref):
    total = None
    for comp in range(6):
        for k in range(4):
            lanes = slice(k * 128, (k + 1) * 128)
            term = modes_ref[comp, :, lanes] * vertex[comp:comp + 1, lanes]
            total = term if total is None else total + term
    acc_ref[...] = jnp.zeros(acc_ref.shape, F32)
    acc_ref[0:total.shape[0], :] = total
    ones = jnp.ones((8, 128), BF16)
    return sum(dot_nt(ones, p) for p in split3(acc_ref[...]))


def finish_kernel(col_ref, row_ref, codes_ref, modes_hbm, vertex_out, grad_out,
                  modes, part8, sumrow, part16, send, mid, stage, recv, acc, grad, grad8, mid_grad, grad16,
                  msem, a0, a1, b0, b1, c0, c1, d0, d1, e0, e1, f0, f1):
    me = {"row": lax.axis_index("row"), "col": lax.axis_index("col")}
    r, c = me["row"], me["col"]
    barrier = greet(me)
    fetch = pltpu.make_async_copy(modes_hbm, modes, msem)
    fetch.start()

    def halves(ref, i):
        return ref.at[:, pl.ds(pl.multiple_of(i * N_COL, N_COL), N_COL), :]

    swap_a = Swap(me, "row", N_ROW, lambda peer: row_ref, lambda slot: part8.at[slot], (a0, a1))
    swap_b = Swap(me, "col", N_COL, lambda peer: sumrow, lambda slot: part16.at[slot], (b0, b1))
    swap_c = Swap(me, "row", N_ROW, lambda peer: halves(send, peer), lambda slot: halves(mid, slot), (c0, c1))
    swap_d = Swap(me, "col", N_COL, lambda peer: stage.at[peer], lambda slot: recv.at[slot], (d0, d1))
    swap_e = Swap(me, "row", N_ROW, lambda peer: grad, lambda slot: grad8.at[slot], (e0, e1))
    swap_f = Swap(me, "col", N_COL, lambda peer: mid_grad, lambda slot: grad16.at[slot], (f0, f1))

    width = 256
    third = 1.0 / 3.0
    total = jnp.zeros((128, 192), F32)
    for n in range(3):
        for cb in range(col_ref.shape[1] // width):
            cols = slice(cb * width, (cb + 1) * width)
            code = codes_ref[n:n + 1, cols]
            slots = code >> 5
            element = jnp.minimum(iota((1, width), 1) + cb * width, SLAB_DEV).astype(F32)
            eight = jnp.concatenate([col_ref[:, cols] * third, (slots & 511).astype(F32), element], axis=0)
            total = total + bucket_terms(eight, slots, code & 31)
    send[0] = total[:, 0:128]
    send[1] = jnp.concatenate([total[:, 128:192], jnp.zeros((128, 64), F32)], axis=1)
    pl.semaphore_wait(barrier, N_ROW + N_COL - 2)
    swap_a.start()
    swap_c.start()
    part8[r] = row_ref[...]
    halves(mid, r)[...] = halves(send, r)[...]
    swap_a.receive()
    sumrow[...] = sum(part8[i] for i in range(N_ROW)) * third
    swap_b.start()
    part16[c] = sumrow[...]
    swap_c.receive()
    for i in range(N_COL):
        for half in range(2):
            stage[i, :, half * 128:(half + 1) * 128] = mid[half, pl.ds(i, N_ROW, stride=N_COL), :]
    swap_d.start()
    recv[c] = stage[c]
    swap_b.receive()
    rows = sum(part16[i] for i in range(N_COL))
    swap_d.receive()
    vertex = add_up(recv[...].reshape(128, 256), rows)
    vertex_out[...] = vertex[0:6]
    fetch.wait()
    grad[...] = project(modes, vertex, acc)[0:1]
    swap_e.start()
    grad8[r] = grad[...]
    swap_e.receive()
    mid_grad[...] = sum(grad8[i] for i in range(N_ROW))
    swap_f.start()
    grad16[c] = mid_grad[...]
    swap_f.receive()
    grad_out[...] = sum(grad16[i] for i in range(N_COL))
    for swap in (swap_a, swap_b, swap_c, swap_d, swap_e, swap_f):
        swap.drain()


def emit_kernel(vertex_ref, grad_ref, vertex_out, grad_out):
    vertex_out[...] = vertex_ref[...]
    grad_out[...] = grad_ref[...].reshape(grad_ref.shape[1])[0:grad_out.shape[0]]


def body(centroid, normals, tangent, element_area, forward_field, adjoint_field, corners, slot_map, quad_order, morph_modes):
    el = centroid.shape[1]
    modes_t = jnp.transpose(morph_modes, (1, 0, 2))
    flags = jnp.transpose(quad_order[:, :, 0, :], (1, 2, 0))
    table = slot_map.reshape(512, 128)
    area = element_area[None, :]
    centroid, normals, tangent, area, forward_field, adjoint_field, corners, table, flags, modes_t = [
        pltpu.with_memory_space_constraint(x, pltpu.HBM)
        for x in (centroid, normals, tangent, area, forward_field, adjoint_field, corners, table, flags, modes_t)]
    rows, lists, codes = pl.pallas_call(
        gather_kernel,
        out_shape=(S((128, 128), F32), S((16, 128), I32), S((3, el), I32)),
        in_specs=[HB] * 5, out_specs=(VM,) * 3,
        scratch_shapes=[pltpu.VMEM((3, el), F32), pltpu.VMEM((2, el), F32), pltpu.VMEM((8, 8, 16), I32),
                        pltpu.VMEM((512, 128), I32), pltpu.VMEM((3, el), I32), DMA((5,)), pltpu.VMEM((1, 128), F32), pltpu.VMEM((16, 128), F32), pltpu.VMEM((128, 128), F32),
                        pltpu.VMEM((8, 8, 16), I32)] + swap_sems(8) + swap_sems(16) + swap_sems(8),
        compiler_params=pltpu.CompilerParams(collective_id=0, has_side_effects=True, vmem_limit_bytes=16 << 20), name="gather",
    )(centroid, adjoint_field, flags, table, corners)
    col_part, row_part = pair_call(lists.reshape(2048), rows, centroid, normals, tangent, area, forward_field, BATCHES)
    vertex, grad = pl.pallas_call(
        finish_kernel,
        out_shape=(S((6, 512), F32), S((1, 384), F32)),
        in_specs=[VM] * 3 + [HB], out_specs=(VM, VM),
        scratch_shapes=[pltpu.VMEM((6, 300, 512), F32), pltpu.VMEM((8, 24, 128), F32), pltpu.VMEM((24, 128), F32),
                        pltpu.VMEM((16, 24, 128), F32), pltpu.VMEM((2, 128, 128), F32), pltpu.VMEM((2, 128, 128), F32),
                        pltpu.VMEM((16, 8, 256), F32), pltpu.VMEM((16, 8, 256), F32), pltpu.VMEM((384, 128), F32),
                        pltpu.VMEM((1, 384), F32), pltpu.VMEM((8, 1, 384), F32), pltpu.VMEM((1, 384), F32),
                        pltpu.VMEM((16, 1, 384), F32), DMA] + (swap_sems(8) + swap_sems(16)) * 3,
        compiler_params=pltpu.CompilerParams(collective_id=1, has_side_effects=True, vmem_limit_bytes=16 << 20), name="finish",
    )(col_part, row_part, codes, modes_t)
    return pl.pallas_call(emit_kernel, out_shape=(S((6, 512), F32), S((300,), F32)), in_specs=[VM] * 2, out_specs=(VM, VM),
                          compiler_params=pltpu.CompilerParams(vmem_limit_bytes=16 << 20), name="emit")(vertex, grad)


def solution(mesh):
    from jax.sharding import PartitionSpec as P
    every = ("row", "col")
    return jax.shard_map(
        body, mesh=mesh,
        in_specs=(P(None, every), P(None, every), P(None, every), P(every), P(None, every), P(None, every), P(None, every),
                  P(), P("row", None, "col", None), P(None, None, every)),
        out_specs=(P(None, every), P()), check_vma=False)
```

```python
import math, functools
import jax, jax.numpy as jnp
from jax import lax
from jax.experimental import pallas as pl
from jax.experimental.pallas import tpu as pltpu

F32 = jnp.float32
MAGIC = 12582912.0
INV_TURN = 1.0 / (2.0 * math.pi)
SIN_C = (4.442883014678955, -7.308245658874512, 3.6063544750213623, -0.8461129069328308, 0.10982698947191238)
COS_C = (1.4142135381698608, -6.978850841522217, 5.7394609451293945, -1.8835630416870117, 0.31069818139076233)


def horner(coeffs, z):
    total = z * coeffs[-1] + coeffs[-2]
    for value in coeffs[-3::-1]:
        total = total * z + value
    return total


def green(r2, cr, ci):
    inv = lax.rsqrt(r2)
    phi = r2 * inv
    turn = phi * INV_TURN
    frac = turn - jnp.round(turn)
    z = frac * frac
    hs = frac * horner(SIN_C, z)
    hc = horner(COS_C, z)
    cosine = 1.0 - hs * hs
    sine = hs * hc
    er = cr * cosine - ci * sine
    ei = cr * sine + ci * cosine
    i2 = inv * inv
    i3 = i2 * inv
    g = er + phi * ei
    h = ei - phi * er
    k = g * (3.0 * i2) - er
    return g, h, k, i3


def tile_terms(kind, row, col, cr_scale, ci_scale):
    x, y, z, ar, ai = row
    dx, dy, dz = x - col["y"][0], y - col["y"][1], z - col["y"][2]
    d = (dx, dy, dz)
    nx, ny, nz = col["n"]
    mn = dx * nx + dy * ny + dz * nz
    sq = dx * dx + dy * dy + dz * dz
    cr = ar * cr_scale + ai * ci_scale
    ci = ar * ci_scale - ai * cr_scale
    out = {}
    sa = sb = None
    if kind != 0:
        ex, ey, ez = col["t2"]
        e = dx * ex + dy * ey + dz * ez
        b = sq + col["at"]
        pts = []
        for sign in (-1, 1):
            if sign > 0:
                r2, m = b - e, mn - col["tn"]
            else:
                r2, m = b + e, mn + col["tn"]
            g, h, k, i3 = green(r2, cr, ci)
            pts.append((i3 * g, i3 * (h - m * k)))
        (a0, b0), (a2, b2) = pts
        sa, sb, da, db = a0 + a2, b0 + b2, a2 - a0, b2 - b0
    if kind != 1:
        g, h, k, i3 = green(sq + col["a"], cr, ci)
        a1, b1 = i3 * g, i3 * (h - mn * k)
        sa, sb = (a1, b1) if sa is None else (sa + a1, sb + b1)
    bd = [sb * v for v in d]
    ad = [sa * v for v in d]
    an = [sa * v for v in (nx, ny, nz)]
    pos = [p + q for p, q in zip(bd, an)]
    if kind == 0:
        return pos, pos, ad, None
    ts = col["ts"]
    pos = [p - db * t for p, t in zip(pos, ts)]
    return pos, pos, ad, da


def pair_kernel(batches, lists_ref, table, ctab, col_out, racc, colv):
    tiles = lists_ref.shape[0] // 256
    racc[...] = jnp.zeros(racc.shape, F32)

    def tile_body(t, _):
        lanes = pl.ds(pl.multiple_of(t * 128, 128), 128)
        for i in range(15):
            colv[i] = jnp.broadcast_to(ctab[i:i + 1, lanes], (8, 128))
        for kind, weight in enumerate((1.0, 0.5, 1.0 / 3.0)):
            for part in range(2):
                colv[15 + 2 * kind + part] = jnp.broadcast_to(ctab[15 + part:16 + part, lanes] * weight, (8, 128))

        def getcol():
            return dict(y=[colv[0], colv[1], colv[2]], n=[colv[3], colv[4], colv[5]], ts=[colv[6], colv[7], colv[8]],
                        t2=[colv[9], colv[10], colv[11]], a=colv[12], at=colv[13], tn=colv[14])
        zero = jnp.zeros((8, 128), F32)

        def make(kind, size):
            def body(it, state):
                pos, ids, acc = state
                col = getcol()
                frs, fis = colv[15 + 2 * kind], colv[16 + 2 * kind]
                acc = list(acc)
                news = []
                for j in range(size):
                    row = [table[ids[j], q] for q in range(5)]
                    gain, _, ad, da = tile_terms(kind, row, col, frs, fis)
                    for q in range(3):
                        acc[q] = acc[q] + gain[q]
                        acc[3 + q] = acc[3 + q] + ad[q]
                    if da is not None:
                        acc[6] = acc[6] + da
                    news.append(gain)
                olds = [[racc[ids[j], q] for q in range(3)] for j in range(size)]
                for j in range(size):
                    for q in range(3):
                        racc[ids[j], q] = olds[j][q] + news[j][q]
                pos = pos + size
                return pos, tuple(lists_ref[pos + j] for j in range(most)), tuple(acc)
            return body
        most = max(batches)
        start = t * 256
        state = (start, tuple(lists_ref[start + j] for j in range(most)), (zero,) * 7)
        for kind in range(3):
            state = lax.fori_loop(0, lists_ref[start + 253 + kind], make(kind, batches[kind]), state)
        sums = [jnp.sum(v, axis=0, keepdims=True) for v in state[2]]
        for q in range(3):
            col_out[q:q + 1, lanes] = -sums[q]
            tsr = ctab[6 + q:7 + q, lanes]
            col_out[3 + q:4 + q, lanes] = 4.0 * (sums[3 + q] - sums[6] * tsr)
        return 0

    lax.fori_loop(0, tiles, tile_body, 0)

def pair_call(lists, table, ctab, batches):
    el = ctab.shape[1]
    vm = pl.BlockSpec(memory_space=pltpu.VMEM)
    return pl.pallas_call(
        functools.partial(pair_kernel, batches),
        out_shape=(jax.ShapeDtypeStruct((6, el), F32), jax.ShapeDtypeStruct((table.shape[0], 3, 8, 128), F32)),
        in_specs=[pl.BlockSpec(memory_space=pltpu.SMEM), vm, vm], out_specs=(vm, vm),
        scratch_shapes=[pltpu.VMEM((21, 8, 128), F32)],
        compiler_params=pltpu.CompilerParams(vmem_limit_bytes=16 << 20), name="pairs",
    )(lists, table, ctab)


def dot_nn(a, b):
    return lax.dot_general(a, b, (((1,), (0,)), ((), ())), preferred_element_type=F32)


def dot_nt(a, b):
    return lax.dot_general(a, b, (((1,), (1,)), ((), ())), preferred_element_type=F32)


def iota(shape, dim):
    return lax.broadcasted_iota(jnp.int32, shape, dim)


BF16 = jnp.bfloat16


def split3(v):
    hi = v.astype(BF16)
    rest = v - hi.astype(F32)
    mid = rest.astype(BF16)
    low = (rest - mid.astype(F32)).astype(BF16)
    return hi, mid, low


def ones_where(mask):
    return jnp.where(mask, 1.0, 0.0)


def make_lists(flags, batches):
    before = ones_where(iota((128, 128), 0) < iota((128, 128), 1)).astype(BF16)
    tile = iota((8, 128), 0)
    lane = iota((8, 128), 1)
    pos = jnp.zeros((8, 128), F32)
    base = jnp.zeros((8, 1), F32)
    counts = []
    for kind in range(3):
        mask = ones_where(flags == float(kind))
        inside = dot_nn(mask.astype(BF16), before)
        total = jnp.sum(mask, axis=1, keepdims=True)
        pos = pos + mask * (inside + base)
        nb = jnp.floor((total + float(batches[kind] - 1)) * (1.0 / batches[kind]))
        base = base + nb * float(batches[kind])
        counts.append(nb)
    posi = pos.astype(jnp.int32)
    slot = iota((256, 128), 0)
    out = jnp.zeros((8, 256), F32)
    for t in range(8):
        hit = ones_where(slot == posi[t:t + 1, :]).astype(BF16)
        value = jnp.where(tile == t, (((lane & 15) << 3) + (lane >> 4) - 128).astype(F32), 0.0).astype(BF16)
        out = out + dot_nt(value, hit)
    out = out + 128.0
    wide = iota((8, 256), 1)
    for kind in range(3):
        out = jnp.where(wide == 253 + kind, counts[kind], out)
    return out.astype(jnp.int32)


def lookup_slots(table, corners):
    parts = jnp.concatenate([(table >> 8).astype(F32).astype(BF16), (table & 255).astype(F32).astype(BF16)], axis=1)
    width = 256
    lo_iota = iota((128, width), 0)
    hi_iota = iota((512, width), 0)
    rows = []
    for n in range(corners.shape[0]):
        pieces = []
        for cb in range(corners.shape[1] // width):
            v = corners[n:n + 1, cb * width:(cb + 1) * width]
            hit = lo_iota == (v & 127)
            rhs = jnp.concatenate([jnp.where(hit, 256.0, 0.0), jnp.where(hit, 1.0, 0.0)], axis=0).astype(BF16)
            sel = dot_nn(parts, rhs)
            pieces.append(jnp.sum(jnp.where(hi_iota == (v >> 7), sel, 0.0), axis=0, keepdims=True))
        rows.append(jnp.concatenate(pieces, axis=1))
    return jnp.concatenate(rows, axis=0).astype(jnp.int32)


def patch_ranks(patches):
    width = 256
    before = ones_where(iota((width, width), 0) < iota((width, width), 1)).astype(BF16)
    sub = iota((128, width), 0)
    carry = jnp.zeros((128, 1), F32)
    rows = []
    for n in range(patches.shape[0]):
        pieces = []
        for cb in range(patches.shape[1] // width):
            hit = ones_where(sub == patches[n:n + 1, cb * width:(cb + 1) * width])
            earlier = dot_nn(hit.astype(BF16), before) + carry
            pieces.append(jnp.sum(hit * earlier, axis=0, keepdims=True))
            carry = carry + jnp.sum(hit, axis=1, keepdims=True)
        rows.append(jnp.concatenate(pieces, axis=1))
    return jnp.concatenate(rows, axis=0)


def bucket_terms(values, slots, ranks):
    width = values.shape[1]
    hit = ones_where(iota((128, width), 0) == (slots >> 9)).astype(BF16)
    mine = (iota((192, width), 0) >> 3) == ranks
    total = None
    for part in split3(values):
        rhs = jnp.where(mine, jnp.concatenate([part.astype(F32)] * 24, axis=0), 0.0).astype(BF16)
        term = dot_nt(hit, rhs)
        total = term if total is None else total + term
    return total


def add_up(recv, rows):
    turned = jnp.transpose(recv)
    sub = iota((512, 128), 0).astype(F32)
    row8 = iota((8, 128), 0)
    row8f = row8.astype(F32)
    total = jnp.zeros((24, 512), F32)
    for pair in range(12):
        parts, hits = [], []
        for q in (2 * pair, 2 * pair + 1):
            eight = turned[q * 8:(q + 1) * 8, :]
            mine = ones_where(row8f == eight[7:8, :])
            for comp in range(3):
                gain = jnp.sum(mine * rows[comp * 8:(comp + 1) * 8], axis=0, keepdims=True)
                eight = eight + jnp.where(row8 == comp, gain, 0.0)
            hits.append(ones_where(sub == eight[6:7, :]).astype(BF16))
            parts.append(jnp.concatenate([p.astype(F32) for p in split3(eight)], axis=0))
        lhs = jnp.concatenate(parts, axis=1).astype(BF16)
        total = total + dot_nt(lhs, jnp.concatenate(hits, axis=1))
    return total[0:8] + total[8:16] + total[16:24]


VM = pl.BlockSpec(memory_space=pltpu.VMEM)
HB = pl.BlockSpec(memory_space=pltpu.HBM)
SLAB_DEV = 8
BATCHES = (8, 4, 4)
N_ROW, N_COL = 8, 16
S = jax.ShapeDtypeStruct
I32 = jnp.int32
DMA = pltpu.SemaphoreType.DMA
MESH = pl.DeviceIdType.MESH


def greet(me):
    barrier = pltpu.get_barrier_semaphore()
    for axis, count in (("row", N_ROW), ("col", N_COL)):
        def signal(k, _, axis=axis, count=count):
            pl.semaphore_signal(barrier, inc=1, device_id={axis: lax.rem(me[axis] + k, count)}, device_id_type=MESH)
            return 0
        lax.fori_loop(1, count, signal, 0)
    return barrier


class Swap:
    def __init__(self, me, axis, count, piece, slot, sems):
        self.me, self.count, self.axis = me[axis], count, axis
        self.piece, self.slot = piece, slot
        self.send_sem, self.recv_sem = sems

    def copy(self, peer, slot):
        return pltpu.make_async_remote_copy(
            src_ref=self.piece(peer), dst_ref=self.slot(slot), send_sem=self.send_sem.at[peer], recv_sem=self.recv_sem.at[slot],
            device_id={self.axis: peer}, device_id_type=MESH)

    def each(self, act):
        def visit(k, _):
            act(lax.rem(self.me + k, self.count))
            return 0
        lax.fori_loop(1, self.count, visit, 0)

    def start(self):
        self.each(lambda peer: self.copy(peer, self.me).start())

    def receive(self):
        self.each(lambda peer: self.copy(peer, peer).wait_recv())

    def drain(self):
        self.each(lambda peer: self.copy(peer, peer).wait_send())


def swap_sems(n):
    return [DMA((n,)), DMA((n,))]


def fetch_all(sources, targets, sems):
    copies = [pltpu.make_async_copy(src, dst, sems.at[i]) for i, (src, dst) in enumerate(zip(sources, targets))]
    for copy in copies:
        copy.start()
    return copies


def column_rows(cen, nor, tan, area, fwd):
    ts = jnp.sqrt(area) * 2.4 * tan
    n16 = 16.0 * nor
    a16 = 16.0 * area
    at = a16 + jnp.sum(ts * ts, axis=0, keepdims=True)
    tn = jnp.sum(ts * n16, axis=0, keepdims=True)
    return [4.0 * cen, n16, ts, 2.0 * ts, a16, at, tn, fwd * (area * (1.0 / math.pi))]


def gather_kernel(cen_hbm, adj_hbm, flags_hbm, table_hbm, corners_hbm, nor_hbm, tan_hbm, area_hbm, fwd_hbm,
                  rowtab, lists_out, codes_out, ctab,
                  cen_ref, adj_ref, flags_ref, table_ref, corners_ref, nor_ref, tan_ref, area_ref, fwd_ref, insem,
                  own, rowblk, rowall, flagall, fs, fr, cs, cr, rs, rr):
    me = {"row": lax.axis_index("row"), "col": lax.axis_index("col")}
    copies = fetch_all((cen_hbm, adj_hbm, flags_hbm, table_hbm, corners_hbm, nor_hbm, tan_hbm, area_hbm, fwd_hbm),
                       (cen_ref, adj_ref, flags_ref, table_ref, corners_ref, nor_ref, tan_ref, area_ref, fwd_ref), insem)
    barrier = greet(me)
    lane = iota((1, 128), 1)
    packed = jnp.zeros((1, 128), F32)
    for copy in copies:
        copy.wait()
    for q in range(5):
        line = cen_ref[q:q + 1, 0:128] * 4.0 if q < 3 else adj_ref[q - 3:q - 2, 0:128]
        if q:
            line = pltpu.roll(line, 8 * q, 1)
        packed = jnp.where((lane >> 3) == q, line, packed)
    own[...] = packed
    rowblk[pl.ds(me["col"], 1), :] = packed
    flagall[me["row"]] = flags_ref[me["row"]]
    slots = lookup_slots(table_ref[...], corners_ref[...])
    codes_out[...] = slots * 32 + patch_ranks(slots >> 9).astype(I32)
    at = 0
    for line in column_rows(cen_ref[...], nor_ref[...], tan_ref[...], area_ref[...], fwd_ref[...]):
        ctab[at:at + line.shape[0], :] = line
        at += line.shape[0]
    ctab[at:, :] = jnp.zeros((ctab.shape[0] - at, ctab.shape[1]), F32)
    rowtab[128] = jnp.concatenate([jnp.full((3, 8, 128), 1.0, F32), jnp.zeros((2, 8, 128), F32)], axis=0)
    pl.semaphore_wait(barrier, N_ROW + N_COL - 2)

    def rows_of(slot):
        return pl.ds(pl.multiple_of(slot * N_COL, N_COL), N_COL)

    flag_swap = Swap(me, "row", N_ROW, lambda peer: flags_ref.at[peer], lambda slot: flagall.at[slot], (fs, fr))
    col_swap = Swap(me, "col", N_COL, lambda peer: own, lambda slot: rowblk.at[pl.ds(slot, 1), :], (cs, cr))
    row_swap = Swap(me, "row", N_ROW, lambda peer: rowblk, lambda slot: rowall.at[rows_of(slot), :], (rs, rr))

    def spread(block, slot):
        turned = jnp.transpose(block)[0:40]
        for c in range(N_COL):
            for q in range(5):
                rowtab[c * N_ROW + slot, q] = jnp.broadcast_to(turned[q * 8:(q + 1) * 8, c:c + 1], (8, 128))

    col_swap.start()
    flag_swap.start()
    col_swap.receive()
    row_swap.start()
    spread(rowblk[...], me["row"])
    flag_swap.receive()
    flags = jnp.concatenate([flagall[r] for r in range(N_ROW)], axis=1).astype(F32)
    lists = make_lists(flags, BATCHES)
    for t in range(8):
        for half in range(2):
            lists_out[2 * t + half:2 * t + half + 1, :] = lists[t:t + 1, half * 128:(half + 1) * 128]
    chip, core = me["row"] // 2, lax.rem(me["row"], 2)
    for away in (0, 1, 3, 2):
        for other in ((1,) if away == 0 else (0, 1)):
            peer = lax.rem(chip + away, N_ROW // 2) * 2 + lax.rem(core + other, 2)
            row_swap.copy(peer, peer).wait_recv()
            spread(rowall[rows_of(peer), :], peer)
    for swap in (col_swap, flag_swap, row_swap):
        swap.drain()


def project(modes_ref, vertex, acc_ref):
    total = None
    for comp in range(6):
        for k in range(4):
            lanes = slice(k * 128, (k + 1) * 128)
            term = modes_ref[comp, :, lanes] * vertex[comp:comp + 1, lanes]
            total = term if total is None else total + term
    acc_ref[...] = jnp.zeros(acc_ref.shape, F32)
    acc_ref[0:total.shape[0], :] = total
    ones = jnp.ones((8, 128), BF16)
    return sum(dot_nt(ones, p) for p in split3(acc_ref[...]))


def finish_kernel(col_ref, racc_ref, codes_ref, modes_hbm, vertex_out, grad_out,
                  modes, row_ref, part8, sumrow, part16, send, mid, stage, recv, acc, grad, grad8, mid_grad, grad16,
                  msem, a0, a1, b0, b1, c0, c1, d0, d1, e0, e1, f0, f1):
    me = {"row": lax.axis_index("row"), "col": lax.axis_index("col")}
    r, c = me["row"], me["col"]
    barrier = greet(me)
    fetch = pltpu.make_async_copy(modes_hbm, modes, msem)
    fetch.start()

    def halves(ref, i):
        return ref.at[:, pl.ds(pl.multiple_of(i * N_COL, N_COL), N_COL), :]

    swap_a = Swap(me, "row", N_ROW, lambda peer: row_ref, lambda slot: part8.at[slot], (a0, a1))
    swap_b = Swap(me, "col", N_COL, lambda peer: sumrow, lambda slot: part16.at[slot], (b0, b1))
    swap_c = Swap(me, "row", N_ROW, lambda peer: halves(send, peer), lambda slot: halves(mid, slot), (c0, c1))
    swap_d = Swap(me, "col", N_COL, lambda peer: stage.at[peer], lambda slot: recv.at[slot], (d0, d1))
    swap_e = Swap(me, "row", N_ROW, lambda peer: grad, lambda slot: grad8.at[slot], (e0, e1))
    swap_f = Swap(me, "col", N_COL, lambda peer: mid_grad, lambda slot: grad16.at[slot], (f0, f1))

    width = 256
    third = 1.0 / 3.0
    total = jnp.zeros((128, 192), F32)
    for n in range(3):
        for cb in range(col_ref.shape[1] // width):
            cols = slice(cb * width, (cb + 1) * width)
            code = codes_ref[n:n + 1, cols]
            slots = code >> 5
            element = jnp.minimum(iota((1, width), 1) + cb * width, SLAB_DEV).astype(F32)
            eight = jnp.concatenate([col_ref[:, cols] * third, (slots & 511).astype(F32), element], axis=0)
            total = total + bucket_terms(eight, slots, code & 31)
    lane = iota((8, 128), 1)
    outs = [jnp.zeros((8, 128), F32) for _ in range(3)]
    for g in range(128):
        for q in range(3):
            outs[q] = jnp.where(lane == g, jnp.sum(racc_ref[g, q], axis=1, keepdims=True), outs[q])
    for q in range(3):
        row_ref[q * 8:(q + 1) * 8, :] = outs[q]
    send[0] = total[:, 0:128]
    send[1] = jnp.concatenate([total[:, 128:192], jnp.zeros((128, 64), F32)], axis=1)
    pl.semaphore_wait(barrier, N_ROW + N_COL - 2)
    swap_a.start()
    swap_c.start()
    part8[r] = row_ref[...]
    halves(mid, r)[...] = halves(send, r)[...]
    swap_a.receive()
    sumrow[...] = sum(part8[i] for i in range(N_ROW)) * third
    swap_b.start()
    part16[c] = sumrow[...]
    swap_c.receive()
    for i in range(N_COL):
        for half in range(2):
            stage[i, :, half * 128:(half + 1) * 128] = mid[half, pl.ds(i, N_ROW, stride=N_COL), :]
    swap_d.start()
    recv[c] = stage[c]
    swap_b.receive()
    rows = sum(part16[i] for i in range(N_COL))
    swap_d.receive()
    vertex = add_up(recv[...].reshape(128, 256), rows)
    vertex_out[...] = vertex[0:6]
    fetch.wait()
    grad[...] = project(modes, vertex, acc)[0:1]
    swap_e.start()
    grad8[r] = grad[...]
    swap_e.receive()
    mid_grad[...] = sum(grad8[i] for i in range(N_ROW))
    swap_f.start()
    grad16[c] = mid_grad[...]
    swap_f.receive()
    grad_out[...] = sum(grad16[i] for i in range(N_COL))
    for swap in (swap_a, swap_b, swap_c, swap_d, swap_e, swap_f):
        swap.drain()


def emit_kernel(vertex_ref, grad_ref, vertex_out, grad_out):
    vertex_out[...] = vertex_ref[...]
    grad_out[...] = grad_ref[...].reshape(grad_ref.shape[1])[0:grad_out.shape[0]]


def body(centroid, normals, tangent, element_area, forward_field, adjoint_field, corners, slot_map, quad_order, morph_modes):
    el = centroid.shape[1]
    modes_t = jnp.transpose(morph_modes, (1, 0, 2))
    flags = jnp.transpose(quad_order[:, :, 0, :], (1, 2, 0))
    table = slot_map.reshape(512, 128)
    area = element_area[None, :]
    centroid, normals, tangent, area, forward_field, adjoint_field, corners, table, flags, modes_t = [
        pltpu.with_memory_space_constraint(x, pltpu.HBM)
        for x in (centroid, normals, tangent, area, forward_field, adjoint_field, corners, table, flags, modes_t)]
    rowtab, lists, codes, ctab = pl.pallas_call(
        gather_kernel,
        out_shape=(S((129, 5, 8, 128), F32), S((16, 128), I32), S((3, el), I32), S((24, el), F32)),
        in_specs=[HB] * 9, out_specs=(VM,) * 4,
        scratch_shapes=[pltpu.VMEM((3, el), F32), pltpu.VMEM((2, el), F32), pltpu.VMEM((8, 8, 16), I32),
                        pltpu.VMEM((512, 128), I32), pltpu.VMEM((3, el), I32), pltpu.VMEM((3, el), F32), pltpu.VMEM((3, el), F32),
                        pltpu.VMEM((1, el), F32), pltpu.VMEM((2, el), F32), DMA((9,)), pltpu.VMEM((1, 128), F32),
                        pltpu.VMEM((16, 128), F32), pltpu.VMEM((128, 128), F32),
                        pltpu.VMEM((8, 8, 16), I32)] + swap_sems(8) + swap_sems(16) + swap_sems(8),
        compiler_params=pltpu.CompilerParams(collective_id=0, has_side_effects=True, vmem_limit_bytes=16 << 20), name="gather",
    )(centroid, adjoint_field, flags, table, corners, normals, tangent, area, forward_field)
    col_part, row_part = pair_call(lists.reshape(2048), rowtab, ctab, BATCHES)
    vertex, grad = pl.pallas_call(
        finish_kernel,
        out_shape=(S((6, 512), F32), S((1, 384), F32)),
        in_specs=[VM] * 3 + [HB], out_specs=(VM, VM),
        scratch_shapes=[pltpu.VMEM((6, 300, 512), F32), pltpu.VMEM((24, 128), F32), pltpu.VMEM((8, 24, 128), F32), pltpu.VMEM((24, 128), F32),
                        pltpu.VMEM((16, 24, 128), F32), pltpu.VMEM((2, 128, 128), F32), pltpu.VMEM((2, 128, 128), F32),
                        pltpu.VMEM((16, 8, 256), F32), pltpu.VMEM((16, 8, 256), F32), pltpu.VMEM((384, 128), F32),
                        pltpu.VMEM((1, 384), F32), pltpu.VMEM((8, 1, 384), F32), pltpu.VMEM((1, 384), F32),
                        pltpu.VMEM((16, 1, 384), F32), DMA] + (swap_sems(8) + swap_sems(16)) * 3,
        compiler_params=pltpu.CompilerParams(collective_id=1, has_side_effects=True, vmem_limit_bytes=16 << 20), name="finish",
    )(col_part, row_part, codes, modes_t)
    return pl.pallas_call(emit_kernel, out_shape=(S((6, 512), F32), S((300,), F32)), in_specs=[VM] * 2, out_specs=(VM, VM),
                          compiler_params=pltpu.CompilerParams(vmem_limit_bytes=16 << 20), name="emit")(vertex, grad)


def solution(mesh):
    from jax.sharding import PartitionSpec as P
    every = ("row", "col")
    return jax.shard_map(
        body, mesh=mesh,
        in_specs=(P(None, every), P(None, every), P(None, every), P(every), P(None, every), P(None, every), P(None, every),
                  P(), P("row", None, "col", None), P(None, None, every)),
        out_specs=(P(None, every), P()), check_vma=False)
```

```python
import math, functools
import jax, jax.numpy as jnp
from jax import lax
from jax.experimental import pallas as pl
from jax.experimental.pallas import tpu as pltpu

F32 = jnp.float32
MAGIC = 12582912.0
INV_TURN = 1.0 / (2.0 * math.pi)
SIN_C = (4.442883014678955, -7.308245658874512, 3.6063544750213623, -0.8461129069328308, 0.10982698947191238)
COS_C = (1.4142135381698608, -6.978850841522217, 5.7394609451293945, -1.8835630416870117, 0.31069818139076233)


def horner(coeffs, z):
    total = z * coeffs[-1] + coeffs[-2]
    for value in coeffs[-3::-1]:
        total = total * z + value
    return total


def green(r2, cr, ci):
    inv = lax.rsqrt(r2)
    phi = r2 * inv
    turn = phi * INV_TURN
    frac = turn - jnp.round(turn)
    z = frac * frac
    hs = frac * horner(SIN_C, z)
    hc = horner(COS_C, z)
    cosine = 1.0 - hs * hs
    sine = hs * hc
    er = cr * cosine - ci * sine
    ei = cr * sine + ci * cosine
    i2 = inv * inv
    i3 = i2 * inv
    g = er + phi * ei
    h = ei - phi * er
    k = g * (3.0 * i2) - er
    return g, h, k, i3


def tile_terms(kind, row, col, cr_scale, ci_scale):
    x, y, z, ar, ai = row
    dx, dy, dz = x - col["y"][0], y - col["y"][1], z - col["y"][2]
    d = (dx, dy, dz)
    nx, ny, nz = col["n"]
    mn = dx * nx + dy * ny + dz * nz
    sq = dx * dx + dy * dy + dz * dz
    cr = ar * cr_scale + ai * ci_scale
    ci = ar * ci_scale - ai * cr_scale
    out = {}
    sa = sb = None
    if kind != 0:
        ex, ey, ez = col["t2"]
        e = dx * ex + dy * ey + dz * ez
        b = sq + col["at"]
        pts = []
        for sign in (-1, 1):
            if sign > 0:
                r2, m = b - e, mn - col["tn"]
            else:
                r2, m = b + e, mn + col["tn"]
            g, h, k, i3 = green(r2, cr, ci)
            pts.append((i3 * g, i3 * (h - m * k)))
        (a0, b0), (a2, b2) = pts
        sa, sb, da, db = a0 + a2, b0 + b2, a2 - a0, b2 - b0
    if kind != 1:
        g, h, k, i3 = green(sq + col["a"], cr, ci)
        a1, b1 = i3 * g, i3 * (h - mn * k)
        sa, sb = (a1, b1) if sa is None else (sa + a1, sb + b1)
    bd = [sb * v for v in d]
    ad = [sa * v for v in d]
    an = [sa * v for v in (nx, ny, nz)]
    pos = [p + q for p, q in zip(bd, an)]
    if kind == 0:
        return pos, pos, ad, None
    ts = col["ts"]
    pos = [p - db * t for p, t in zip(pos, ts)]
    return pos, pos, ad, da


def pair_kernel(batches, lists_ref, table, ctab, col_out, racc, colv, cacc):
    tiles = lists_ref.shape[0] // 256
    racc[...] = jnp.zeros(racc.shape, F32)

    def tile_body(t, _):
        lanes = pl.ds(pl.multiple_of(t * 128, 128), 128)
        for i in range(15):
            colv[i] = jnp.broadcast_to(ctab[i:i + 1, lanes], (8, 128))
        for kind, weight in enumerate((1.0, 0.5, 1.0 / 3.0)):
            for part in range(2):
                colv[15 + 2 * kind + part] = jnp.broadcast_to(ctab[15 + part:16 + part, lanes] * weight, (8, 128))

        def getcol():
            return dict(y=[colv[0], colv[1], colv[2]], n=[colv[3], colv[4], colv[5]], ts=[colv[6], colv[7], colv[8]],
                        t2=[colv[9], colv[10], colv[11]], a=colv[12], at=colv[13], tn=colv[14])
        zero = jnp.zeros((8, 128), F32)

        def make(kind, size):
            def body(it, state):
                pos, ids = state
                col = getcol()
                frs, fis = colv[15 + 2 * kind], colv[16 + 2 * kind]
                acc = [None] * 7
                news = []
                for j in range(size):
                    row = [table[ids[j], q] for q in range(5)]
                    gain, _, ad, da = tile_terms(kind, row, col, frs, fis)
                    for q, v in enumerate(gain + ad + [da]):
                        if v is not None:
                            acc[q] = v if acc[q] is None else acc[q] + v
                    news.append(gain)
                olds = [[racc[ids[j], q] for q in range(3)] for j in range(size)]
                for j in range(size):
                    for q in range(3):
                        racc[ids[j], q] = olds[j][q] + news[j][q]
                for q, v in enumerate(acc):
                    if v is not None:
                        cacc[q] = cacc[q] + v
                pos = pos + size
                return pos, tuple(lists_ref[pos + j] for j in range(most))
            return body
        most = max(batches)
        start = t * 256
        state = (start, tuple(lists_ref[start + j] for j in range(most)))
        cacc[...] = jnp.zeros(cacc.shape, F32)
        for kind in range(3):
            state = lax.fori_loop(0, lists_ref[start + 253 + kind], make(kind, batches[kind]), state)
        sums = [jnp.sum(cacc[q], axis=0, keepdims=True) for q in range(7)]
        for q in range(3):
            col_out[q:q + 1, lanes] = -sums[q]
            tsr = ctab[6 + q:7 + q, lanes]
            col_out[3 + q:4 + q, lanes] = 4.0 * (sums[3 + q] - sums[6] * tsr)
        return 0

    lax.fori_loop(0, tiles, tile_body, 0)

def pair_call(lists, table, ctab, batches):
    el = ctab.shape[1]
    vm = pl.BlockSpec(memory_space=pltpu.VMEM)
    return pl.pallas_call(
        functools.partial(pair_kernel, batches),
        out_shape=(jax.ShapeDtypeStruct((6, el), F32), jax.ShapeDtypeStruct((table.shape[0], 3, 8, 128), F32)),
        in_specs=[pl.BlockSpec(memory_space=pltpu.SMEM), vm, vm], out_specs=(vm, vm),
        scratch_shapes=[pltpu.VMEM((21, 8, 128), F32), pltpu.VMEM((7, 8, 128), F32)],
        compiler_params=pltpu.CompilerParams(vmem_limit_bytes=16 << 20), name="pairs",
    )(lists, table, ctab)


def dot_nn(a, b):
    return lax.dot_general(a, b, (((1,), (0,)), ((), ())), preferred_element_type=F32)


def dot_nt(a, b):
    return lax.dot_general(a, b, (((1,), (1,)), ((), ())), preferred_element_type=F32)


def iota(shape, dim):
    return lax.broadcasted_iota(jnp.int32, shape, dim)


BF16 = jnp.bfloat16


def split3(v):
    hi = v.astype(BF16)
    rest = v - hi.astype(F32)
    mid = rest.astype(BF16)
    low = (rest - mid.astype(F32)).astype(BF16)
    return hi, mid, low


def ones_where(mask):
    return jnp.where(mask, 1.0, 0.0)


def make_lists(flags, batches):
    before = ones_where(iota((128, 128), 0) < iota((128, 128), 1)).astype(BF16)
    tile = iota((8, 128), 0)
    lane = iota((8, 128), 1)
    pos = jnp.zeros((8, 128), F32)
    base = jnp.zeros((8, 1), F32)
    counts = []
    for kind in range(3):
        mask = ones_where(flags == float(kind))
        inside = dot_nn(mask.astype(BF16), before)
        total = jnp.sum(mask, axis=1, keepdims=True)
        pos = pos + mask * (inside + base)
        nb = jnp.floor((total + (batches[kind] - 0.5)) * (1.0 / batches[kind]))
        base = base + nb * float(batches[kind])
        counts.append(nb)
    posi = pos.astype(jnp.int32)
    slot = iota((256, 128), 0)
    out = jnp.zeros((8, 256), F32)
    for t in range(8):
        hit = ones_where(slot == posi[t:t + 1, :]).astype(BF16)
        value = jnp.where(tile == t, (((lane & 15) << 3) + (lane >> 4) - 128).astype(F32), 0.0).astype(BF16)
        out = out + dot_nt(value, hit)
    out = out + 128.0
    wide = iota((8, 256), 1)
    for kind in range(3):
        out = jnp.where(wide == 253 + kind, counts[kind], out)
    return out.astype(jnp.int32)


def lookup_slots(table, corners):
    parts = jnp.concatenate([(table >> 8).astype(F32).astype(BF16), (table & 255).astype(F32).astype(BF16)], axis=1)
    width = 256
    lo_iota = iota((128, width), 0)
    hi_iota = iota((512, width), 0)
    rows = []
    for n in range(corners.shape[0]):
        pieces = []
        for cb in range(corners.shape[1] // width):
            v = corners[n:n + 1, cb * width:(cb + 1) * width]
            hit = lo_iota == (v & 127)
            rhs = jnp.concatenate([jnp.where(hit, 256.0, 0.0), jnp.where(hit, 1.0, 0.0)], axis=0).astype(BF16)
            sel = dot_nn(parts, rhs)
            pieces.append(jnp.sum(jnp.where(hi_iota == (v >> 7), sel, 0.0), axis=0, keepdims=True))
        rows.append(jnp.concatenate(pieces, axis=1))
    return jnp.concatenate(rows, axis=0).astype(jnp.int32)


def patch_ranks(patches):
    width = 256
    before = ones_where(iota((width, width), 0) < iota((width, width), 1)).astype(BF16)
    sub = iota((128, width), 0)
    carry = jnp.zeros((128, 1), F32)
    rows = []
    for n in range(patches.shape[0]):
        pieces = []
        for cb in range(patches.shape[1] // width):
            hit = ones_where(sub == patches[n:n + 1, cb * width:(cb + 1) * width])
            earlier = dot_nn(hit.astype(BF16), before) + carry
            pieces.append(jnp.sum(hit * earlier, axis=0, keepdims=True))
            carry = carry + jnp.sum(hit, axis=1, keepdims=True)
        rows.append(jnp.concatenate(pieces, axis=1))
    return jnp.concatenate(rows, axis=0)


def bucket_terms(values, slots, ranks):
    width = values.shape[1]
    hit = ones_where(iota((128, width), 0) == (slots >> 9)).astype(BF16)
    mine = (iota((192, width), 0) >> 3) == ranks
    total = None
    for part in split3(values):
        rhs = jnp.where(mine, jnp.concatenate([part.astype(F32)] * 24, axis=0), 0.0).astype(BF16)
        term = dot_nt(hit, rhs)
        total = term if total is None else total + term
    return total


def add_up(recv, rows):
    turned = jnp.transpose(recv)
    sub = iota((512, 128), 0).astype(F32)
    row8 = iota((8, 128), 0)
    row8f = row8.astype(F32)
    total = jnp.zeros((24, 512), F32)
    for pair in range(12):
        parts, hits = [], []
        for q in (2 * pair, 2 * pair + 1):
            eight = turned[q * 8:(q + 1) * 8, :]
            mine = ones_where(row8f == eight[7:8, :])
            for comp in range(3):
                gain = jnp.sum(mine * rows[comp * 8:(comp + 1) * 8], axis=0, keepdims=True)
                eight = eight + jnp.where(row8 == comp, gain, 0.0)
            hits.append(ones_where(sub == eight[6:7, :]).astype(BF16))
            parts.append(jnp.concatenate([p.astype(F32) for p in split3(eight)], axis=0))
        lhs = jnp.concatenate(parts, axis=1).astype(BF16)
        total = total + dot_nt(lhs, jnp.concatenate(hits, axis=1))
    return total[0:8] + total[8:16] + total[16:24]


VM = pl.BlockSpec(memory_space=pltpu.VMEM)
HB = pl.BlockSpec(memory_space=pltpu.HBM)
SLAB_DEV = 8
BATCHES = (8, 5, 5)
N_ROW, N_COL = 8, 16
S = jax.ShapeDtypeStruct
I32 = jnp.int32
DMA = pltpu.SemaphoreType.DMA
MESH = pl.DeviceIdType.MESH


def greet(me):
    barrier = pltpu.get_barrier_semaphore()
    for axis, count in (("row", N_ROW), ("col", N_COL)):
        def signal(k, _, axis=axis, count=count):
            pl.semaphore_signal(barrier, inc=1, device_id={axis: lax.rem(me[axis] + k, count)}, device_id_type=MESH)
            return 0
        lax.fori_loop(1, count, signal, 0)
    return barrier


class Swap:
    def __init__(self, me, axis, count, piece, slot, sems):
        self.me, self.count, self.axis = me[axis], count, axis
        self.piece, self.slot = piece, slot
        self.send_sem, self.recv_sem = sems

    def copy(self, peer, slot):
        return pltpu.make_async_remote_copy(
            src_ref=self.piece(peer), dst_ref=self.slot(slot), send_sem=self.send_sem.at[peer], recv_sem=self.recv_sem.at[slot],
            device_id={self.axis: peer}, device_id_type=MESH)

    def each(self, act):
        def visit(k, _):
            act(lax.rem(self.me + k, self.count))
            return 0
        lax.fori_loop(1, self.count, visit, 0)

    def start(self):
        self.each(lambda peer: self.copy(peer, self.me).start())

    def receive(self):
        self.each(lambda peer: self.copy(peer, peer).wait_recv())

    def drain(self):
        self.each(lambda peer: self.copy(peer, peer).wait_send())


def swap_sems(n):
    return [DMA((n,)), DMA((n,))]


def fetch_all(sources, targets, sems):
    copies = [pltpu.make_async_copy(src, dst, sems.at[i]) for i, (src, dst) in enumerate(zip(sources, targets))]
    for copy in copies:
        copy.start()
    return copies


def column_rows(cen, nor, tan, area, fwd):
    ts = jnp.sqrt(area) * 2.4 * tan
    n16 = 16.0 * nor
    a16 = 16.0 * area
    at = a16 + jnp.sum(ts * ts, axis=0, keepdims=True)
    tn = jnp.sum(ts * n16, axis=0, keepdims=True)
    return [4.0 * cen, n16, ts, 2.0 * ts, a16, at, tn, fwd * (area * (1.0 / math.pi))]


def gather_kernel(cen_hbm, adj_hbm, flags_hbm, table_hbm, corners_hbm, nor_hbm, tan_hbm, area_hbm, fwd_hbm,
                  rowtab, lists_out, codes_out, ctab,
                  cen_ref, adj_ref, flags_ref, table_ref, corners_ref, nor_ref, tan_ref, area_ref, fwd_ref, insem,
                  own, rowblk, rowall, flagall, fs, fr, cs, cr, rs, rr):
    me = {"row": lax.axis_index("row"), "col": lax.axis_index("col")}
    copies = fetch_all((cen_hbm, adj_hbm, flags_hbm, table_hbm, corners_hbm, nor_hbm, tan_hbm, area_hbm, fwd_hbm),
                       (cen_ref, adj_ref, flags_ref, table_ref, corners_ref, nor_ref, tan_ref, area_ref, fwd_ref), insem)
    barrier = greet(me)
    lane = iota((1, 128), 1)
    packed = jnp.zeros((1, 128), F32)
    for copy in copies:
        copy.wait()
    for q in range(5):
        line = cen_ref[q:q + 1, 0:128] * 4.0 if q < 3 else adj_ref[q - 3:q - 2, 0:128]
        if q:
            line = pltpu.roll(line, 8 * q, 1)
        packed = jnp.where((lane >> 3) == q, line, packed)
    own[...] = packed
    rowblk[pl.ds(me["col"], 1), :] = packed
    flagall[me["row"]] = flags_ref[me["row"]]
    slots = lookup_slots(table_ref[...], corners_ref[...])
    codes_out[...] = slots * 32 + patch_ranks(slots >> 9).astype(I32)
    at = 0
    for line in column_rows(cen_ref[...], nor_ref[...], tan_ref[...], area_ref[...], fwd_ref[...]):
        ctab[at:at + line.shape[0], :] = line
        at += line.shape[0]
    ctab[at:, :] = jnp.zeros((ctab.shape[0] - at, ctab.shape[1]), F32)
    rowtab[128] = jnp.concatenate([jnp.full((3, 8, 128), 1.0, F32), jnp.zeros((2, 8, 128), F32)], axis=0)
    pl.semaphore_wait(barrier, N_ROW + N_COL - 2)

    def rows_of(slot):
        return pl.ds(pl.multiple_of(slot * N_COL, N_COL), N_COL)

    flag_swap = Swap(me, "row", N_ROW, lambda peer: flags_ref.at[peer], lambda slot: flagall.at[slot], (fs, fr))
    col_swap = Swap(me, "col", N_COL, lambda peer: own, lambda slot: rowblk.at[pl.ds(slot, 1), :], (cs, cr))
    row_swap = Swap(me, "row", N_ROW, lambda peer: rowblk, lambda slot: rowall.at[rows_of(slot), :], (rs, rr))

    def spread(block, slot):
        turned = jnp.transpose(block)[0:40]
        for c in range(N_COL):
            for q in range(5):
                rowtab[c * N_ROW + slot, q] = jnp.broadcast_to(turned[q * 8:(q + 1) * 8, c:c + 1], (8, 128))

    col_swap.start()
    flag_swap.start()
    col_swap.receive()
    row_swap.start()
    spread(rowblk[...], me["row"])
    flag_swap.receive()
    flags = jnp.concatenate([flagall[r] for r in range(N_ROW)], axis=1).astype(F32)
    lists = make_lists(flags, BATCHES)
    for t in range(8):
        for half in range(2):
            lists_out[2 * t + half:2 * t + half + 1, :] = lists[t:t + 1, half * 128:(half + 1) * 128]
    chip, core = me["row"] // 2, lax.rem(me["row"], 2)
    for away in (0, 1, 3, 2):
        for other in ((1,) if away == 0 else (0, 1)):
            peer = lax.rem(chip + away, N_ROW // 2) * 2 + lax.rem(core + other, 2)
            row_swap.copy(peer, peer).wait_recv()
            spread(rowall[rows_of(peer), :], peer)
    for swap in (col_swap, flag_swap, row_swap):
        swap.drain()


def project(modes_ref, vertex, acc_ref):
    total = None
    for comp in range(6):
        for k in range(4):
            lanes = slice(k * 128, (k + 1) * 128)
            term = modes_ref[comp, :, lanes] * vertex[comp:comp + 1, lanes]
            total = term if total is None else total + term
    acc_ref[...] = jnp.zeros(acc_ref.shape, F32)
    acc_ref[0:total.shape[0], :] = total
    ones = jnp.ones((8, 128), BF16)
    return sum(dot_nt(ones, p) for p in split3(acc_ref[...]))


def finish_kernel(col_ref, racc_ref, codes_ref, modes_hbm, vertex_out, grad_out,
                  modes, row_ref, part8, sumrow, part16, send, mid, stage, recv, acc, grad, grad8, mid_grad, grad16,
                  msem, a0, a1, b0, b1, c0, c1, d0, d1, e0, e1, f0, f1):
    me = {"row": lax.axis_index("row"), "col": lax.axis_index("col")}
    r, c = me["row"], me["col"]
    barrier = greet(me)
    fetch = pltpu.make_async_copy(modes_hbm, modes, msem)
    fetch.start()

    def halves(ref, i):
        return ref.at[:, pl.ds(pl.multiple_of(i * N_COL, N_COL), N_COL), :]

    swap_a = Swap(me, "row", N_ROW, lambda peer: row_ref, lambda slot: part8.at[slot], (a0, a1))
    swap_b = Swap(me, "col", N_COL, lambda peer: sumrow, lambda slot: part16.at[slot], (b0, b1))
    swap_c = Swap(me, "row", N_ROW, lambda peer: halves(send, peer), lambda slot: halves(mid, slot), (c0, c1))
    swap_d = Swap(me, "col", N_COL, lambda peer: stage.at[peer], lambda slot: recv.at[slot], (d0, d1))
    swap_e = Swap(me, "row", N_ROW, lambda peer: grad, lambda slot: grad8.at[slot], (e0, e1))
    swap_f = Swap(me, "col", N_COL, lambda peer: mid_grad, lambda slot: grad16.at[slot], (f0, f1))

    width = 256
    third = 1.0 / 3.0
    total = jnp.zeros((128, 192), F32)
    for n in range(3):
        for cb in range(col_ref.shape[1] // width):
            cols = slice(cb * width, (cb + 1) * width)
            code = codes_ref[n:n + 1, cols]
            slots = code >> 5
            element = jnp.minimum(iota((1, width), 1) + cb * width, SLAB_DEV).astype(F32)
            eight = jnp.concatenate([col_ref[:, cols] * third, (slots & 511).astype(F32), element], axis=0)
            total = total + bucket_terms(eight, slots, code & 31)
    send[0] = total[:, 0:128]
    send[1] = jnp.concatenate([total[:, 128:192], jnp.zeros((128, 64), F32)], axis=1)
    pl.semaphore_wait(barrier, N_ROW + N_COL - 2)
    swap_c.start()
    lane = iota((8, 128), 1)
    outs = [jnp.zeros((8, 128), F32) for _ in range(3)]
    for g in range(128):
        for q in range(3):
            outs[q] = jnp.where(lane == g, jnp.sum(racc_ref[g, q], axis=1, keepdims=True), outs[q])
    for q in range(3):
        row_ref[q * 8:(q + 1) * 8, :] = outs[q]
    swap_a.start()
    part8[r] = row_ref[...]
    halves(mid, r)[...] = halves(send, r)[...]
    swap_c.receive()
    for i in range(N_COL):
        for half in range(2):
            stage[i, :, half * 128:(half + 1) * 128] = mid[half, pl.ds(i, N_ROW, stride=N_COL), :]
    swap_d.start()
    recv[c] = stage[c]
    swap_a.receive()
    sumrow[...] = sum(part8[i] for i in range(N_ROW)) * third
    swap_b.start()
    part16[c] = sumrow[...]
    swap_b.receive()
    rows = sum(part16[i] for i in range(N_COL))
    swap_d.receive()
    vertex = add_up(recv[...].reshape(128, 256), rows)
    vertex_out[...] = vertex[0:6]
    fetch.wait()
    grad[...] = project(modes, vertex, acc)[0:1]
    swap_e.start()
    grad8[r] = grad[...]
    swap_e.receive()
    mid_grad[...] = sum(grad8[i] for i in range(N_ROW))
    swap_f.start()
    grad16[c] = mid_grad[...]
    swap_f.receive()
    grad_out[...] = sum(grad16[i] for i in range(N_COL))
    for swap in (swap_a, swap_b, swap_c, swap_d, swap_e, swap_f):
        swap.drain()


def emit_kernel(vertex_ref, grad_ref, vertex_out, grad_out):
    vertex_out[...] = vertex_ref[...]
    grad_out[...] = grad_ref[...].reshape(grad_ref.shape[1])[0:grad_out.shape[0]]


def body(centroid, normals, tangent, element_area, forward_field, adjoint_field, corners, slot_map, quad_order, morph_modes):
    el = centroid.shape[1]
    modes_t = jnp.transpose(morph_modes, (1, 0, 2))
    flags = jnp.transpose(quad_order[:, :, 0, :], (1, 2, 0))
    table = slot_map.reshape(512, 128)
    area = element_area[None, :]
    centroid, normals, tangent, area, forward_field, adjoint_field, corners, table, flags, modes_t = [
        pltpu.with_memory_space_constraint(x, pltpu.HBM)
        for x in (centroid, normals, tangent, area, forward_field, adjoint_field, corners, table, flags, modes_t)]
    rowtab, lists, codes, ctab = pl.pallas_call(
        gather_kernel,
        out_shape=(S((129, 5, 8, 128), F32), S((16, 128), I32), S((3, el), I32), S((24, el), F32)),
        in_specs=[HB] * 9, out_specs=(VM,) * 4,
        scratch_shapes=[pltpu.VMEM((3, el), F32), pltpu.VMEM((2, el), F32), pltpu.VMEM((8, 8, 16), I32),
                        pltpu.VMEM((512, 128), I32), pltpu.VMEM((3, el), I32), pltpu.VMEM((3, el), F32), pltpu.VMEM((3, el), F32),
                        pltpu.VMEM((1, el), F32), pltpu.VMEM((2, el), F32), DMA((9,)), pltpu.VMEM((1, 128), F32),
                        pltpu.VMEM((16, 128), F32), pltpu.VMEM((128, 128), F32),
                        pltpu.VMEM((8, 8, 16), I32)] + swap_sems(8) + swap_sems(16) + swap_sems(8),
        compiler_params=pltpu.CompilerParams(collective_id=0, has_side_effects=True, vmem_limit_bytes=16 << 20), name="gather",
    )(centroid, adjoint_field, flags, table, corners, normals, tangent, area, forward_field)
    col_part, row_part = pair_call(lists.reshape(2048), rowtab, ctab, BATCHES)
    vertex, grad = pl.pallas_call(
        finish_kernel,
        out_shape=(S((6, 512), F32), S((1, 384), F32)),
        in_specs=[VM] * 3 + [HB], out_specs=(VM, VM),
        scratch_shapes=[pltpu.VMEM((6, 300, 512), F32), pltpu.VMEM((24, 128), F32), pltpu.VMEM((8, 24, 128), F32), pltpu.VMEM((24, 128), F32),
                        pltpu.VMEM((16, 24, 128), F32), pltpu.VMEM((2, 128, 128), F32), pltpu.VMEM((2, 128, 128), F32),
                        pltpu.VMEM((16, 8, 256), F32), pltpu.VMEM((16, 8, 256), F32), pltpu.VMEM((384, 128), F32),
                        pltpu.VMEM((1, 384), F32), pltpu.VMEM((8, 1, 384), F32), pltpu.VMEM((1, 384), F32),
                        pltpu.VMEM((16, 1, 384), F32), DMA] + (swap_sems(8) + swap_sems(16)) * 3,
        compiler_params=pltpu.CompilerParams(collective_id=1, has_side_effects=True, vmem_limit_bytes=16 << 20), name="finish",
    )(col_part, row_part, codes, modes_t)
    return pl.pallas_call(emit_kernel, out_shape=(S((6, 512), F32), S((300,), F32)), in_specs=[VM] * 2, out_specs=(VM, VM),
                          compiler_params=pltpu.CompilerParams(vmem_limit_bytes=16 << 20), name="emit")(vertex, grad)


def solution(mesh):
    from jax.sharding import PartitionSpec as P
    every = ("row", "col")
    return jax.shard_map(
        body, mesh=mesh,
        in_specs=(P(None, every), P(None, every), P(None, every), P(every), P(None, every), P(None, every), P(None, every),
                  P(), P("row", None, "col", None), P(None, None, every)),
        out_specs=(P(None, every), P()), check_vma=False)
```

```python
import math, functools
import jax, jax.numpy as jnp
from jax import lax
from jax.experimental import pallas as pl
from jax.experimental.pallas import tpu as pltpu

F32 = jnp.float32
MAGIC = 12582912.0
INV_TURN = 1.0 / (2.0 * math.pi)
SIN_C = (4.442883014678955, -7.308245658874512, 3.6063544750213623, -0.8461129069328308, 0.10982698947191238)
COS_C = (1.4142135381698608, -6.978850841522217, 5.7394609451293945, -1.8835630416870117, 0.31069818139076233)


def horner(coeffs, z):
    total = z * coeffs[-1] + coeffs[-2]
    for value in coeffs[-3::-1]:
        total = total * z + value
    return total


def green(r2, cr, ci):
    inv = lax.rsqrt(r2)
    phi = r2 * inv
    turn = phi * INV_TURN
    frac = turn - jnp.round(turn)
    z = frac * frac
    hs = frac * horner(SIN_C, z)
    hc = horner(COS_C, z)
    cosine = 1.0 - hs * hs
    sine = hs * hc
    er = cr * cosine - ci * sine
    ei = cr * sine + ci * cosine
    i2 = inv * inv
    i3 = i2 * inv
    g = er + phi * ei
    h = ei - phi * er
    k = g * (3.0 * i2) - er
    return g, h, k, i3


def tile_terms(kind, row, col, cr_scale, ci_scale):
    x, y, z, ar, ai = row
    dx, dy, dz = x - col["y"][0], y - col["y"][1], z - col["y"][2]
    d = (dx, dy, dz)
    nx, ny, nz = col["n"]
    mn = dx * nx + dy * ny + dz * nz
    sq = dx * dx + dy * dy + dz * dz
    cr = ar * cr_scale + ai * ci_scale
    ci = ar * ci_scale - ai * cr_scale
    out = {}
    sa = sb = None
    if kind != 0:
        ex, ey, ez = col["t2"]
        e = dx * ex + dy * ey + dz * ez
        b = sq + col["at"]
        pts = []
        for sign in (-1, 1):
            if sign > 0:
                r2, m = b - e, mn - col["tn"]
            else:
                r2, m = b + e, mn + col["tn"]
            g, h, k, i3 = green(r2, cr, ci)
            pts.append((i3 * g, i3 * (h - m * k)))
        (a0, b0), (a2, b2) = pts
        sa, sb, da, db = a0 + a2, b0 + b2, a2 - a0, b2 - b0
    if kind != 1:
        g, h, k, i3 = green(sq + col["a"], cr, ci)
        a1, b1 = i3 * g, i3 * (h - mn * k)
        sa, sb = (a1, b1) if sa is None else (sa + a1, sb + b1)
    bd = [sb * v for v in d]
    ad = [sa * v for v in d]
    an = [sa * v for v in (nx, ny, nz)]
    pos = [p + q for p, q in zip(bd, an)]
    if kind == 0:
        return pos, pos, ad, None
    ts = col["ts"]
    pos = [p - db * t for p, t in zip(pos, ts)]
    return pos, pos, ad, da


def pair_kernel(batches, lists_ref, table, ctab, col_out, racc, colv, cacc):
    tiles = lists_ref.shape[0] // 256
    racc[...] = jnp.zeros(racc.shape, F32)

    def tile_body(t, _):
        lanes = pl.ds(pl.multiple_of(t * 128, 128), 128)
        for i in range(15):
            colv[i] = jnp.broadcast_to(ctab[i:i + 1, lanes], (8, 128))
        for kind, weight in enumerate((1.0, 0.5, 1.0 / 3.0)):
            for part in range(2):
                colv[15 + 2 * kind + part] = jnp.broadcast_to(ctab[15 + part:16 + part, lanes] * weight, (8, 128))

        def getcol():
            return dict(y=[colv[0], colv[1], colv[2]], n=[colv[3], colv[4], colv[5]], ts=[colv[6], colv[7], colv[8]],
                        t2=[colv[9], colv[10], colv[11]], a=colv[12], at=colv[13], tn=colv[14])
        zero = jnp.zeros((8, 128), F32)

        def make(kind, size):
            def body(it, state):
                pos, ids = state
                col = getcol()
                frs, fis = colv[15 + 2 * kind], colv[16 + 2 * kind]
                acc = [None] * 7
                news = []
                for j in range(size):
                    row = [table[ids[j], q] for q in range(5)]
                    gain, _, ad, da = tile_terms(kind, row, col, frs, fis)
                    for q, v in enumerate(gain + ad + [da]):
                        if v is not None:
                            acc[q] = v if acc[q] is None else acc[q] + v
                    news.append(gain)
                olds = [[racc[ids[j], q] for q in range(3)] for j in range(size)]
                for j in range(size):
                    for q in range(3):
                        racc[ids[j], q] = olds[j][q] + news[j][q]
                for q, v in enumerate(acc):
                    if v is not None:
                        cacc[q] = cacc[q] + v
                pos = pos + size
                return pos, tuple(lists_ref[pos + j] for j in range(most))
            return body
        most = max(batches)
        start = t * 256
        state = (start, tuple(lists_ref[start + j] for j in range(most)))
        cacc[...] = jnp.zeros(cacc.shape, F32)
        for kind in range(3):
            state = lax.fori_loop(0, lists_ref[start + 253 + kind], make(kind, batches[kind]), state)
        sums = [jnp.sum(cacc[q], axis=0, keepdims=True) for q in range(7)]
        for q in range(3):
            col_out[q:q + 1, lanes] = -sums[q]
            tsr = ctab[6 + q:7 + q, lanes]
            col_out[3 + q:4 + q, lanes] = 4.0 * (sums[3 + q] - sums[6] * tsr)
        return 0

    lax.fori_loop(0, tiles, tile_body, 0)

def pair_call(lists, table, ctab, batches):
    el = ctab.shape[1]
    vm = pl.BlockSpec(memory_space=pltpu.VMEM)
    return pl.pallas_call(
        functools.partial(pair_kernel, batches),
        out_shape=(jax.ShapeDtypeStruct((6, el), F32), jax.ShapeDtypeStruct((table.shape[0], 3, 8, 128), F32)),
        in_specs=[pl.BlockSpec(memory_space=pltpu.SMEM), vm, vm], out_specs=(vm, vm),
        scratch_shapes=[pltpu.VMEM((21, 8, 128), F32), pltpu.VMEM((7, 8, 128), F32)],
        compiler_params=pltpu.CompilerParams(vmem_limit_bytes=16 << 20), name="pairs",
    )(lists, table, ctab)


def dot_nn(a, b):
    return lax.dot_general(a, b, (((1,), (0,)), ((), ())), preferred_element_type=F32)


def dot_nt(a, b):
    return lax.dot_general(a, b, (((1,), (1,)), ((), ())), preferred_element_type=F32)


def iota(shape, dim):
    return lax.broadcasted_iota(jnp.int32, shape, dim)


BF16 = jnp.bfloat16


def split3(v):
    hi = v.astype(BF16)
    rest = v - hi.astype(F32)
    mid = rest.astype(BF16)
    low = (rest - mid.astype(F32)).astype(BF16)
    return hi, mid, low


def ones_where(mask):
    return jnp.where(mask, 1.0, 0.0)


def make_lists(flags, batches):
    before = ones_where(iota((128, 128), 0) < iota((128, 128), 1)).astype(BF16)
    tile = iota((8, 128), 0)
    lane = iota((8, 128), 1)
    pos = jnp.zeros((8, 128), F32)
    base = jnp.zeros((8, 1), F32)
    counts = []
    for kind in range(3):
        mask = ones_where(flags == float(kind))
        inside = dot_nn(mask.astype(BF16), before)
        total = jnp.sum(mask, axis=1, keepdims=True)
        pos = pos + mask * (inside + base)
        nb = jnp.floor((total + (batches[kind] - 0.5)) * (1.0 / batches[kind]))
        base = base + nb * float(batches[kind])
        counts.append(nb)
    posi = pos.astype(jnp.int32)
    slot = iota((256, 128), 0)
    out = jnp.zeros((8, 256), F32)
    for t in range(8):
        hit = ones_where(slot == posi[t:t + 1, :]).astype(BF16)
        value = jnp.where(tile == t, (((lane & 15) << 3) + (lane >> 4) - 128).astype(F32), 0.0).astype(BF16)
        out = out + dot_nt(value, hit)
    out = out + 128.0
    wide = iota((8, 256), 1)
    for kind in range(3):
        out = jnp.where(wide == 253 + kind, counts[kind], out)
    return out.astype(jnp.int32)


def lookup_slots(table, corners):
    parts = jnp.concatenate([(table >> 8).astype(F32).astype(BF16), (table & 255).astype(F32).astype(BF16)], axis=1)
    width = 256
    lo_iota = iota((128, width), 0)
    hi_iota = iota((512, width), 0)
    rows = []
    for n in range(corners.shape[0]):
        pieces = []
        for cb in range(corners.shape[1] // width):
            v = corners[n:n + 1, cb * width:(cb + 1) * width]
            hit = lo_iota == (v & 127)
            rhs = jnp.concatenate([jnp.where(hit, 256.0, 0.0), jnp.where(hit, 1.0, 0.0)], axis=0).astype(BF16)
            sel = dot_nn(parts, rhs)
            pieces.append(jnp.sum(jnp.where(hi_iota == (v >> 7), sel, 0.0), axis=0, keepdims=True))
        rows.append(jnp.concatenate(pieces, axis=1))
    return jnp.concatenate(rows, axis=0).astype(jnp.int32)


def patch_ranks(patches):
    width = 256
    before = ones_where(iota((width, width), 0) < iota((width, width), 1)).astype(BF16)
    sub = iota((128, width), 0)
    carry = jnp.zeros((128, 1), F32)
    rows = []
    for n in range(patches.shape[0]):
        pieces = []
        for cb in range(patches.shape[1] // width):
            hit = ones_where(sub == patches[n:n + 1, cb * width:(cb + 1) * width])
            earlier = dot_nn(hit.astype(BF16), before) + carry
            pieces.append(jnp.sum(hit * earlier, axis=0, keepdims=True))
            carry = carry + jnp.sum(hit, axis=1, keepdims=True)
        rows.append(jnp.concatenate(pieces, axis=1))
    return jnp.concatenate(rows, axis=0)


def bucket_terms(values, slots, ranks):
    width = values.shape[1]
    hit = ones_where(iota((128, width), 0) == (slots >> 9)).astype(BF16)
    mine = (iota((192, width), 0) >> 3) == ranks
    total = None
    for part in split3(values):
        rhs = jnp.where(mine, jnp.concatenate([part.astype(F32)] * 24, axis=0), 0.0).astype(BF16)
        term = dot_nt(hit, rhs)
        total = term if total is None else total + term
    return total


def add_up(recv, rows):
    turned = jnp.transpose(recv)
    sub = iota((512, 128), 0).astype(F32)
    row8 = iota((8, 128), 0)
    row8f = row8.astype(F32)
    total = jnp.zeros((24, 512), F32)
    for pair in range(12):
        parts, hits = [], []
        for q in (2 * pair, 2 * pair + 1):
            eight = turned[q * 8:(q + 1) * 8, :]
            mine = ones_where(row8f == eight[7:8, :])
            for comp in range(3):
                gain = jnp.sum(mine * rows[comp * 8:(comp + 1) * 8], axis=0, keepdims=True)
                eight = eight + jnp.where(row8 == comp, gain, 0.0)
            hits.append(ones_where(sub == eight[6:7, :]).astype(BF16))
            parts.append(jnp.concatenate([p.astype(F32) for p in split3(eight)], axis=0))
        lhs = jnp.concatenate(parts, axis=1).astype(BF16)
        total = total + dot_nt(lhs, jnp.concatenate(hits, axis=1))
    return total[0:8] + total[8:16] + total[16:24]


VM = pl.BlockSpec(memory_space=pltpu.VMEM)
HB = pl.BlockSpec(memory_space=pltpu.HBM)
SLAB_DEV = 8
BATCHES = (8, 5, 5)
N_ROW, N_COL = 8, 16
S = jax.ShapeDtypeStruct
I32 = jnp.int32
DMA = pltpu.SemaphoreType.DMA
MESH = pl.DeviceIdType.MESH


SIDE = 4


def far_first(inner):
    def hops(step, ring):
        return min(step, ring - step)
    steps = [(i, j) for i in range(SIDE) for j in range(inner) if (i, j) != (0, 0)]
    return sorted(steps, key=lambda s: -(hops(s[0], SIDE) * 2 + hops(s[1], inner) * (2 if inner == SIDE else 1)))


def whereabouts():
    me, peers = {}, {}
    for axis, inner in (("row", 2), ("col", SIDE)):
        here = lax.axis_index(axis)
        outer, low = here // inner, lax.rem(here, inner)
        me[axis] = here
        peers[axis] = [lax.rem(outer + i, SIDE) * inner + lax.rem(low + j, inner) for i, j in far_first(inner)]
    return me, peers


def greet(peers):
    barrier = pltpu.get_barrier_semaphore()
    for axis in ("col", "row"):
        for peer in peers[axis]:
            pl.semaphore_signal(barrier, inc=1, device_id={axis: peer}, device_id_type=MESH)
    return barrier


class Swap:
    def __init__(self, me, peers, axis, piece, slot, sems):
        self.me, self.peers, self.axis = me[axis], peers[axis], axis
        self.piece, self.slot = piece, slot
        self.send_sem, self.recv_sem = sems

    def copy(self, peer, slot):
        return pltpu.make_async_remote_copy(
            src_ref=self.piece(peer), dst_ref=self.slot(slot), send_sem=self.send_sem.at[peer], recv_sem=self.recv_sem.at[slot],
            device_id={self.axis: peer}, device_id_type=MESH)

    def start(self):
        for peer in self.peers:
            self.copy(peer, self.me).start()

    def receive(self):
        for peer in self.peers:
            self.copy(peer, peer).wait_recv()

    def drain(self):
        for peer in self.peers:
            self.copy(peer, peer).wait_send()


def swap_sems(n):
    return [DMA((n,)), DMA((n,))]


def fetch_all(sources, targets, sems):
    copies = [pltpu.make_async_copy(src, dst, sems.at[i]) for i, (src, dst) in enumerate(zip(sources, targets))]
    for copy in copies:
        copy.start()
    return copies


def column_rows(cen, nor, tan, area, fwd):
    ts = jnp.sqrt(area) * 2.4 * tan
    n16 = 16.0 * nor
    a16 = 16.0 * area
    at = a16 + jnp.sum(ts * ts, axis=0, keepdims=True)
    tn = jnp.sum(ts * n16, axis=0, keepdims=True)
    return [4.0 * cen, n16, ts, 2.0 * ts, a16, at, tn, fwd * (area * (1.0 / math.pi))]


def gather_kernel(cen_hbm, adj_hbm, flags_hbm, table_hbm, corners_hbm, nor_hbm, tan_hbm, area_hbm, fwd_hbm,
                  rowtab, lists_out, codes_out, ctab,
                  cen_ref, adj_ref, flags_ref, table_ref, corners_ref, nor_ref, tan_ref, area_ref, fwd_ref, insem,
                  own, rowblk, rowall, flagall, fs, fr, cs, cr, rs, rr):
    me, peers = whereabouts()
    copies = fetch_all((cen_hbm, adj_hbm, flags_hbm, table_hbm, corners_hbm, nor_hbm, tan_hbm, area_hbm, fwd_hbm),
                       (cen_ref, adj_ref, flags_ref, table_ref, corners_ref, nor_ref, tan_ref, area_ref, fwd_ref), insem)
    barrier = greet(peers)
    lane = iota((1, 128), 1)
    packed = jnp.zeros((1, 128), F32)
    for copy in copies[:3]:
        copy.wait()
    for q in range(5):
        line = cen_ref[q:q + 1, 0:128] * 4.0 if q < 3 else adj_ref[q - 3:q - 2, 0:128]
        if q:
            line = pltpu.roll(line, 8 * q, 1)
        packed = jnp.where((lane >> 3) == q, line, packed)
    own[...] = packed
    rowblk[pl.ds(me["col"], 1), :] = packed
    flagall[me["row"]] = flags_ref[me["row"]]
    for copy in copies[3:]:
        copy.wait()
    slots = lookup_slots(table_ref[...], corners_ref[...])
    rowtab[128] = jnp.concatenate([jnp.full((3, 8, 128), 1.0, F32), jnp.zeros((2, 8, 128), F32)], axis=0)
    pl.semaphore_wait(barrier, N_ROW + N_COL - 2)

    def rows_of(slot):
        return pl.ds(pl.multiple_of(slot * N_COL, N_COL), N_COL)

    flag_swap = Swap(me, peers, "row", lambda peer: flags_ref.at[peer], lambda slot: flagall.at[slot], (fs, fr))
    col_swap = Swap(me, peers, "col", lambda peer: own, lambda slot: rowblk.at[pl.ds(slot, 1), :], (cs, cr))
    row_swap = Swap(me, peers, "row", lambda peer: rowblk, lambda slot: rowall.at[rows_of(slot), :], (rs, rr))

    def spread(block, slot):
        turned = jnp.transpose(block)[0:40]
        for c in range(N_COL):
            for q in range(5):
                rowtab[c * N_ROW + slot, q] = jnp.broadcast_to(turned[q * 8:(q + 1) * 8, c:c + 1], (8, 128))

    col_swap.start()
    flag_swap.start()
    codes_out[...] = slots * 32 + patch_ranks(slots >> 9).astype(I32)
    at = 0
    for line in column_rows(cen_ref[...], nor_ref[...], tan_ref[...], area_ref[...], fwd_ref[...]):
        ctab[at:at + line.shape[0], :] = line
        at += line.shape[0]
    ctab[at:, :] = jnp.zeros((ctab.shape[0] - at, ctab.shape[1]), F32)
    col_swap.receive()
    row_swap.start()
    spread(rowblk[...], me["row"])
    flag_swap.receive()
    flags = jnp.concatenate([flagall[r] for r in range(N_ROW)], axis=1).astype(F32)
    lists = make_lists(flags, BATCHES)
    for t in range(8):
        for half in range(2):
            lists_out[2 * t + half:2 * t + half + 1, :] = lists[t:t + 1, half * 128:(half + 1) * 128]
    for peer in reversed(peers["row"]):
        row_swap.copy(peer, peer).wait_recv()
        spread(rowall[rows_of(peer), :], peer)
    for swap in (col_swap, flag_swap, row_swap):
        swap.drain()


def project(modes_ref, vertex, acc_ref):
    total = None
    for comp in range(6):
        for k in range(4):
            lanes = slice(k * 128, (k + 1) * 128)
            term = modes_ref[comp, :, lanes] * vertex[comp:comp + 1, lanes]
            total = term if total is None else total + term
    acc_ref[...] = jnp.zeros(acc_ref.shape, F32)
    acc_ref[0:total.shape[0], :] = total
    ones = jnp.ones((8, 128), BF16)
    return sum(dot_nt(ones, p) for p in split3(acc_ref[...]))


def finish_kernel(col_ref, racc_ref, codes_ref, modes_hbm, vertex_out, grad_out,
                  modes, row_ref, part8, sumrow, part16, send, mid, stage, recv, acc, grad, grad8, mid_grad, grad16,
                  msem, a0, a1, b0, b1, c0, c1, d0, d1, e0, e1, f0, f1):
    me, peers = whereabouts()
    r, c = me["row"], me["col"]
    barrier = greet(peers)
    fetch = pltpu.make_async_copy(modes_hbm, modes, msem)
    fetch.start()

    def halves(ref, i):
        return ref.at[:, pl.ds(pl.multiple_of(i * N_COL, N_COL), N_COL), :]

    swap_a = Swap(me, peers, "row", lambda peer: row_ref, lambda slot: part8.at[slot], (a0, a1))
    swap_b = Swap(me, peers, "col", lambda peer: sumrow, lambda slot: part16.at[slot], (b0, b1))
    swap_c = Swap(me, peers, "row", lambda peer: halves(send, peer), lambda slot: halves(mid, slot), (c0, c1))
    swap_d = Swap(me, peers, "col", lambda peer: stage.at[peer], lambda slot: recv.at[slot], (d0, d1))
    swap_e = Swap(me, peers, "row", lambda peer: grad, lambda slot: grad8.at[slot], (e0, e1))
    swap_f = Swap(me, peers, "col", lambda peer: mid_grad, lambda slot: grad16.at[slot], (f0, f1))

    width = 256
    third = 1.0 / 3.0
    total = jnp.zeros((128, 192), F32)
    for n in range(3):
        for cb in range(col_ref.shape[1] // width):
            cols = slice(cb * width, (cb + 1) * width)
            code = codes_ref[n:n + 1, cols]
            slots = code >> 5
            element = jnp.minimum(iota((1, width), 1) + cb * width, SLAB_DEV).astype(F32)
            eight = jnp.concatenate([col_ref[:, cols] * third, (slots & 511).astype(F32), element], axis=0)
            total = total + bucket_terms(eight, slots, code & 31)
    send[0] = total[:, 0:128]
    send[1] = jnp.concatenate([total[:, 128:192], jnp.zeros((128, 64), F32)], axis=1)
    pl.semaphore_wait(barrier, N_ROW + N_COL - 2)
    swap_c.start()
    lane = iota((8, 128), 1)
    outs = [jnp.zeros((8, 128), F32) for _ in range(3)]
    for g in range(128):
        for q in range(3):
            outs[q] = jnp.where(lane == g, jnp.sum(racc_ref[g, q], axis=1, keepdims=True), outs[q])
    for q in range(3):
        row_ref[q * 8:(q + 1) * 8, :] = outs[q]
    swap_a.start()
    part8[r] = row_ref[...]
    halves(mid, r)[...] = halves(send, r)[...]
    swap_c.receive()
    for i in range(N_COL):
        for half in range(2):
            stage[i, :, half * 128:(half + 1) * 128] = mid[half, pl.ds(i, N_ROW, stride=N_COL), :]
    swap_d.start()
    recv[c] = stage[c]
    swap_a.receive()
    sumrow[...] = sum(part8[i] for i in range(N_ROW)) * third
    swap_b.start()
    part16[c] = sumrow[...]
    swap_b.receive()
    rows = sum(part16[i] for i in range(N_COL))
    swap_d.receive()
    vertex = add_up(recv[...].reshape(128, 256), rows)
    vertex_out[...] = vertex[0:6]
    fetch.wait()
    grad[...] = project(modes, vertex, acc)[0:1]
    swap_e.start()
    grad8[r] = grad[...]
    swap_e.receive()
    mid_grad[...] = sum(grad8[i] for i in range(N_ROW))
    swap_f.start()
    grad16[c] = mid_grad[...]
    swap_f.receive()
    grad_out[...] = sum(grad16[i] for i in range(N_COL))
    for swap in (swap_a, swap_b, swap_c, swap_d, swap_e, swap_f):
        swap.drain()


def emit_kernel(vertex_ref, grad_ref, vertex_out, grad_out):
    vertex_out[...] = vertex_ref[...]
    grad_out[...] = grad_ref[...].reshape(grad_ref.shape[1])[0:grad_out.shape[0]]


def body(centroid, normals, tangent, element_area, forward_field, adjoint_field, corners, slot_map, quad_order, morph_modes):
    el = centroid.shape[1]
    modes_t = jnp.transpose(morph_modes, (1, 0, 2))
    flags = jnp.transpose(quad_order[:, :, 0, :], (1, 2, 0))
    table = slot_map.reshape(512, 128)
    area = element_area[None, :]
    centroid, normals, tangent, area, forward_field, adjoint_field, corners, table, flags, modes_t = [
        pltpu.with_memory_space_constraint(x, pltpu.HBM)
        for x in (centroid, normals, tangent, area, forward_field, adjoint_field, corners, table, flags, modes_t)]
    rowtab, lists, codes, ctab = pl.pallas_call(
        gather_kernel,
        out_shape=(S((129, 5, 8, 128), F32), S((16, 128), I32), S((3, el), I32), S((24, el), F32)),
        in_specs=[HB] * 9, out_specs=(VM,) * 4,
        scratch_shapes=[pltpu.VMEM((3, el), F32), pltpu.VMEM((2, el), F32), pltpu.VMEM((8, 8, 16), I32),
                        pltpu.VMEM((512, 128), I32), pltpu.VMEM((3, el), I32), pltpu.VMEM((3, el), F32), pltpu.VMEM((3, el), F32),
                        pltpu.VMEM((1, el), F32), pltpu.VMEM((2, el), F32), DMA((9,)), pltpu.VMEM((1, 128), F32),
                        pltpu.VMEM((16, 128), F32), pltpu.VMEM((128, 128), F32),
                        pltpu.VMEM((8, 8, 16), I32)] + swap_sems(8) + swap_sems(16) + swap_sems(8),
        compiler_params=pltpu.CompilerParams(collective_id=0, has_side_effects=True, vmem_limit_bytes=16 << 20), name="gather",
    )(centroid, adjoint_field, flags, table, corners, normals, tangent, area, forward_field)
    col_part, row_part = pair_call(lists.reshape(2048), rowtab, ctab, BATCHES)
    vertex, grad = pl.pallas_call(
        finish_kernel,
        out_shape=(S((6, 512), F32), S((1, 384), F32)),
        in_specs=[VM] * 3 + [HB], out_specs=(VM, VM),
        scratch_shapes=[pltpu.VMEM((6, 300, 512), F32), pltpu.VMEM((24, 128), F32), pltpu.VMEM((8, 24, 128), F32), pltpu.VMEM((24, 128), F32),
                        pltpu.VMEM((16, 24, 128), F32), pltpu.VMEM((2, 128, 128), F32), pltpu.VMEM((2, 128, 128), F32),
                        pltpu.VMEM((16, 8, 256), F32), pltpu.VMEM((16, 8, 256), F32), pltpu.VMEM((384, 128), F32),
                        pltpu.VMEM((1, 384), F32), pltpu.VMEM((8, 1, 384), F32), pltpu.VMEM((1, 384), F32),
                        pltpu.VMEM((16, 1, 384), F32), DMA] + (swap_sems(8) + swap_sems(16)) * 3,
        compiler_params=pltpu.CompilerParams(collective_id=1, has_side_effects=True, vmem_limit_bytes=16 << 20), name="finish",
    )(col_part, row_part, codes, modes_t)
    return pl.pallas_call(emit_kernel, out_shape=(S((6, 512), F32), S((300,), F32)), in_specs=[VM] * 2, out_specs=(VM, VM),
                          compiler_params=pltpu.CompilerParams(vmem_limit_bytes=16 << 20), name="emit")(vertex, grad)


def solution(mesh):
    from jax.sharding import PartitionSpec as P
    every = ("row", "col")
    return jax.shard_map(
        body, mesh=mesh,
        in_specs=(P(None, every), P(None, every), P(None, every), P(every), P(None, every), P(None, every), P(None, every),
                  P(), P("row", None, "col", None), P(None, None, every)),
        out_specs=(P(None, every), P()), check_vma=False)
```

```python
import math, functools
import jax, jax.numpy as jnp
from jax import lax
from jax.experimental import pallas as pl
from jax.experimental.pallas import tpu as pltpu

F32 = jnp.float32
MAGIC = 12582912.0
INV_TURN = 1.0 / (2.0 * math.pi)
SIN_C = (4.442883014678955, -7.308245658874512, 3.6063544750213623, -0.8461129069328308, 0.10982698947191238)
COS_C = (1.4142135381698608, -6.978850841522217, 5.7394609451293945, -1.8835630416870117, 0.31069818139076233)


def horner(coeffs, z):
    total = z * coeffs[-1] + coeffs[-2]
    for value in coeffs[-3::-1]:
        total = total * z + value
    return total


def green(r2, cr, ci):
    inv = lax.rsqrt(r2)
    phi = r2 * inv
    turn = phi * INV_TURN
    frac = turn - jnp.round(turn)
    z = frac * frac
    hs = frac * horner(SIN_C, z)
    hc = horner(COS_C, z)
    cosine = 1.0 - hs * hs
    sine = hs * hc
    er = cr * cosine - ci * sine
    ei = cr * sine + ci * cosine
    i2 = inv * inv
    i3 = i2 * inv
    g = er + phi * ei
    h = ei - phi * er
    k = g * (3.0 * i2) - er
    return g, h, k, i3


def tile_terms(kind, row, col, cr_scale, ci_scale):
    x, y, z, ar, ai = row
    dx, dy, dz = x - col["y"][0], y - col["y"][1], z - col["y"][2]
    d = (dx, dy, dz)
    nx, ny, nz = col["n"]
    mn = dx * nx + dy * ny + dz * nz
    sq = dx * dx + dy * dy + dz * dz
    cr = ar * cr_scale + ai * ci_scale
    ci = ar * ci_scale - ai * cr_scale
    out = {}
    sa = sb = None
    if kind != 0:
        ex, ey, ez = col["t2"]
        e = dx * ex + dy * ey + dz * ez
        b = sq + col["at"]
        pts = []
        for sign in (-1, 1):
            if sign > 0:
                r2, m = b - e, mn - col["tn"]
            else:
                r2, m = b + e, mn + col["tn"]
            g, h, k, i3 = green(r2, cr, ci)
            pts.append((i3 * g, i3 * (h - m * k)))
        (a0, b0), (a2, b2) = pts
        sa, sb, da, db = a0 + a2, b0 + b2, a2 - a0, b2 - b0
    if kind != 1:
        g, h, k, i3 = green(sq + col["a"], cr, ci)
        a1, b1 = i3 * g, i3 * (h - mn * k)
        sa, sb = (a1, b1) if sa is None else (sa + a1, sb + b1)
    bd = [sb * v for v in d]
    ad = [sa * v for v in d]
    an = [sa * v for v in (nx, ny, nz)]
    pos = [p + q for p, q in zip(bd, an)]
    if kind == 0:
        return pos, pos, ad, None
    ts = col["ts"]
    pos = [p - db * t for p, t in zip(pos, ts)]
    return pos, pos, ad, da


def pair_kernel(batches, lists_ref, table, ctab, col_out, racc, colv, cacc):
    tiles = lists_ref.shape[0] // 256
    racc[...] = jnp.zeros(racc.shape, F32)

    def tile_body(t, _):
        lanes = pl.ds(pl.multiple_of(t * 128, 128), 128)
        for i in range(15):
            colv[i] = jnp.broadcast_to(ctab[i:i + 1, lanes], (8, 128))
        for kind, weight in enumerate((1.0, 0.5, 1.0 / 3.0)):
            for part in range(2):
                colv[15 + 2 * kind + part] = jnp.broadcast_to(ctab[15 + part:16 + part, lanes] * weight, (8, 128))

        def getcol():
            return dict(y=[colv[0], colv[1], colv[2]], n=[colv[3], colv[4], colv[5]], ts=[colv[6], colv[7], colv[8]],
                        t2=[colv[9], colv[10], colv[11]], a=colv[12], at=colv[13], tn=colv[14])
        zero = jnp.zeros((8, 128), F32)

        def make(kind, size):
            def body(it, state):
                pos, ids = state
                col = getcol()
                frs, fis = colv[15 + 2 * kind], colv[16 + 2 * kind]
                acc = [None] * 7
                news = []
                for j in range(size):
                    row = [table[ids[j], q] for q in range(5)]
                    gain, _, ad, da = tile_terms(kind, row, col, frs, fis)
                    for q, v in enumerate(gain + ad + [da]):
                        if v is not None:
                            acc[q] = v if acc[q] is None else acc[q] + v
                    news.append(gain)
                olds = [[racc[ids[j], q] for q in range(3)] for j in range(size)]
                for j in range(size):
                    for q in range(3):
                        racc[ids[j], q] = olds[j][q] + news[j][q]
                for q, v in enumerate(acc):
                    if v is not None:
                        cacc[q] = cacc[q] + v
                pos = pos + size
                return pos, tuple(lists_ref[pos + j] for j in range(most))
            return body
        most = max(batches)
        start = t * 256
        state = (start, tuple(lists_ref[start + j] for j in range(most)))
        cacc[...] = jnp.zeros(cacc.shape, F32)
        for kind in range(3):
            state = lax.fori_loop(0, lists_ref[start + 253 + kind], make(kind, batches[kind]), state)
        sums = [jnp.sum(cacc[q], axis=0, keepdims=True) for q in range(7)]
        for q in range(3):
            col_out[q:q + 1, lanes] = -sums[q]
            tsr = ctab[6 + q:7 + q, lanes]
            col_out[3 + q:4 + q, lanes] = 4.0 * (sums[3 + q] - sums[6] * tsr)
        return 0

    lax.fori_loop(0, tiles, tile_body, 0)

def pair_call(lists, table, ctab, batches):
    el = ctab.shape[1]
    vm = pl.BlockSpec(memory_space=pltpu.VMEM)
    return pl.pallas_call(
        functools.partial(pair_kernel, batches),
        out_shape=(jax.ShapeDtypeStruct((6, el), F32), jax.ShapeDtypeStruct((table.shape[0], 3, 8, 128), F32)),
        in_specs=[pl.BlockSpec(memory_space=pltpu.SMEM), vm, vm], out_specs=(vm, vm),
        scratch_shapes=[pltpu.VMEM((21, 8, 128), F32), pltpu.VMEM((7, 8, 128), F32)],
        compiler_params=pltpu.CompilerParams(vmem_limit_bytes=16 << 20), name="pairs",
    )(lists, table, ctab)


def dot_nn(a, b):
    return lax.dot_general(a, b, (((1,), (0,)), ((), ())), preferred_element_type=F32)


def dot_nt(a, b):
    return lax.dot_general(a, b, (((1,), (1,)), ((), ())), preferred_element_type=F32)


def iota(shape, dim):
    return lax.broadcasted_iota(jnp.int32, shape, dim)


BF16 = jnp.bfloat16


def split3(v):
    hi = v.astype(BF16)
    rest = v - hi.astype(F32)
    mid = rest.astype(BF16)
    low = (rest - mid.astype(F32)).astype(BF16)
    return hi, mid, low


def ones_where(mask):
    return jnp.where(mask, 1.0, 0.0)


def make_lists(flags, batches):
    before = ones_where(iota((128, 128), 0) < iota((128, 128), 1)).astype(BF16)
    tile = iota((8, 128), 0)
    lane = iota((8, 128), 1)
    pos = jnp.zeros((8, 128), F32)
    base = jnp.zeros((8, 1), F32)
    counts = []
    for kind in range(3):
        mask = ones_where(flags == float(kind))
        inside = dot_nn(mask.astype(BF16), before)
        total = jnp.sum(mask, axis=1, keepdims=True)
        pos = pos + mask * (inside + base)
        nb = jnp.floor((total + (batches[kind] - 0.5)) * (1.0 / batches[kind]))
        base = base + nb * float(batches[kind])
        counts.append(nb)
    posi = pos.astype(jnp.int32)
    slot = iota((256, 128), 0)
    out = jnp.zeros((8, 256), F32)
    for t in range(8):
        hit = ones_where(slot == posi[t:t + 1, :]).astype(BF16)
        value = jnp.where(tile == t, (((lane & 15) << 3) + (lane >> 4) - 128).astype(F32), 0.0).astype(BF16)
        out = out + dot_nt(value, hit)
    out = out + 128.0
    wide = iota((8, 256), 1)
    for kind in range(3):
        out = jnp.where(wide == 253 + kind, counts[kind], out)
    return out.astype(jnp.int32)


def lookup_slots(table, corners):
    parts = jnp.concatenate([(table >> 8).astype(F32).astype(BF16), (table & 255).astype(F32).astype(BF16)], axis=1)
    width = 256
    lo_iota = iota((128, width), 0)
    hi_iota = iota((512, width), 0)
    rows = []
    for n in range(corners.shape[0]):
        pieces = []
        for cb in range(corners.shape[1] // width):
            v = corners[n:n + 1, cb * width:(cb + 1) * width]
            hit = lo_iota == (v & 127)
            rhs = jnp.concatenate([jnp.where(hit, 256.0, 0.0), jnp.where(hit, 1.0, 0.0)], axis=0).astype(BF16)
            sel = dot_nn(parts, rhs)
            pieces.append(jnp.sum(jnp.where(hi_iota == (v >> 7), sel, 0.0), axis=0, keepdims=True))
        rows.append(jnp.concatenate(pieces, axis=1))
    return jnp.concatenate(rows, axis=0).astype(jnp.int32)


def patch_ranks(patches):
    width = 256
    before = ones_where(iota((width, width), 0) < iota((width, width), 1)).astype(BF16)
    sub = iota((128, width), 0)
    carry = jnp.zeros((128, 1), F32)
    rows = []
    for n in range(patches.shape[0]):
        pieces = []
        for cb in range(patches.shape[1] // width):
            hit = ones_where(sub == patches[n:n + 1, cb * width:(cb + 1) * width])
            earlier = dot_nn(hit.astype(BF16), before) + carry
            pieces.append(jnp.sum(hit * earlier, axis=0, keepdims=True))
            carry = carry + jnp.sum(hit, axis=1, keepdims=True)
        rows.append(jnp.concatenate(pieces, axis=1))
    return jnp.concatenate(rows, axis=0)


def bucket_terms(values, slots, ranks):
    width = values.shape[1]
    hit = ones_where(iota((128, width), 0) == (slots >> 9)).astype(BF16)
    mine = (iota((192, width), 0) >> 3) == ranks
    total = None
    for part in split3(values):
        rhs = jnp.where(mine, jnp.concatenate([part.astype(F32)] * 24, axis=0), 0.0).astype(BF16)
        term = dot_nt(hit, rhs)
        total = term if total is None else total + term
    return total


def add_up(recv, rows):
    turned = jnp.transpose(recv)
    sub = iota((128, 128), 0)
    row8 = iota((8, 128), 0)
    total = jnp.zeros((96, 128), F32)
    for pair in range(12):
        parts, hits = [], []
        for q in (2 * pair, 2 * pair + 1):
            eight = turned[q * 8:(q + 1) * 8, :]
            slot = eight[6:7, :].astype(jnp.int32)
            mine = ones_where(row8 == eight[7:8, :].astype(jnp.int32))
            for comp in range(3):
                gain = jnp.sum(mine * rows[comp * 8:(comp + 1) * 8], axis=0, keepdims=True)
                eight = eight + jnp.where(row8 == comp, gain, 0.0)
            hits.append(ones_where(sub == (slot & 127)).astype(BF16))
            quarter = slot >> 7
            parts.append(jnp.concatenate([jnp.where(quarter == k, p.astype(F32), 0.0) for p in split3(eight) for k in range(4)], axis=0))
        total = total + dot_nt(jnp.concatenate(parts, axis=1).astype(BF16), jnp.concatenate(hits, axis=1))
    total = total[0:32] + total[32:64] + total[64:96]
    return jnp.concatenate([total[8 * k:8 * k + 8] for k in range(4)], axis=1)


VM = pl.BlockSpec(memory_space=pltpu.VMEM)
HB = pl.BlockSpec(memory_space=pltpu.HBM)
SLAB_DEV = 8
BATCHES = (8, 5, 5)
N_ROW, N_COL = 8, 16
S = jax.ShapeDtypeStruct
I32 = jnp.int32
DMA = pltpu.SemaphoreType.DMA
MESH = pl.DeviceIdType.MESH


SIDE = 4


def far_first(inner):
    def hops(step, ring):
        return min(step, ring - step)
    steps = [(i, j) for i in range(SIDE) for j in range(inner) if (i, j) != (0, 0)]
    return sorted(steps, key=lambda s: -(hops(s[0], SIDE) * 2 + hops(s[1], inner) * (2 if inner == SIDE else 1)))


def whereabouts():
    me, peers = {}, {}
    for axis, inner in (("row", 2), ("col", SIDE)):
        here = lax.axis_index(axis)
        outer, low = here // inner, lax.rem(here, inner)
        me[axis] = here
        peers[axis] = [lax.rem(outer + i, SIDE) * inner + lax.rem(low + j, inner) for i, j in far_first(inner)]
    return me, peers


def greet(peers):
    barrier = pltpu.get_barrier_semaphore()
    for axis in ("col", "row"):
        for peer in peers[axis]:
            pl.semaphore_signal(barrier, inc=1, device_id={axis: peer}, device_id_type=MESH)
    return barrier


class Swap:
    def __init__(self, me, peers, axis, piece, slot, sems):
        self.me, self.peers, self.axis = me[axis], peers[axis], axis
        self.piece, self.slot = piece, slot
        self.send_sem, self.recv_sem = sems

    def copy(self, peer, slot):
        return pltpu.make_async_remote_copy(
            src_ref=self.piece(peer), dst_ref=self.slot(slot), send_sem=self.send_sem.at[peer], recv_sem=self.recv_sem.at[slot],
            device_id={self.axis: peer}, device_id_type=MESH)

    def start(self):
        for peer in self.peers:
            self.copy(peer, self.me).start()

    def receive(self):
        for peer in self.peers:
            self.copy(peer, peer).wait_recv()

    def drain(self):
        for peer in self.peers:
            self.copy(peer, peer).wait_send()


def swap_sems(n):
    return [DMA((n,)), DMA((n,))]


def fetch_all(sources, targets, sems):
    copies = [pltpu.make_async_copy(src, dst, sems.at[i]) for i, (src, dst) in enumerate(zip(sources, targets))]
    for copy in copies:
        copy.start()
    return copies


def column_rows(cen, nor, tan, area, fwd):
    ts = jnp.sqrt(area) * 2.4 * tan
    n16 = 16.0 * nor
    a16 = 16.0 * area
    at = a16 + jnp.sum(ts * ts, axis=0, keepdims=True)
    tn = jnp.sum(ts * n16, axis=0, keepdims=True)
    return [4.0 * cen, n16, ts, 2.0 * ts, a16, at, tn, fwd * (area * (1.0 / math.pi))]


def gather_kernel(cen_hbm, adj_hbm, flags_hbm, table_hbm, corners_hbm, nor_hbm, tan_hbm, area_hbm, fwd_hbm,
                  rowtab, lists_out, codes_out, ctab,
                  cen_ref, adj_ref, flags_ref, table_ref, corners_ref, nor_ref, tan_ref, area_ref, fwd_ref, insem,
                  own, rowblk, rowall, flagall, fs, fr, cs, cr, rs, rr):
    me, peers = whereabouts()
    barrier = greet(peers)
    copies = fetch_all((cen_hbm, adj_hbm, flags_hbm, table_hbm, corners_hbm, nor_hbm, tan_hbm, area_hbm, fwd_hbm),
                       (cen_ref, adj_ref, flags_ref, table_ref, corners_ref, nor_ref, tan_ref, area_ref, fwd_ref), insem)
    lane = iota((1, 128), 1)
    packed = jnp.zeros((1, 128), F32)
    for copy in copies[:3]:
        copy.wait()
    for q in range(5):
        line = cen_ref[q:q + 1, 0:128] * 4.0 if q < 3 else adj_ref[q - 3:q - 2, 0:128]
        if q:
            line = pltpu.roll(line, 8 * q, 1)
        packed = jnp.where((lane >> 3) == q, line, packed)
    own[...] = packed
    rowblk[pl.ds(me["col"], 1), :] = packed
    flagall[me["row"]] = flags_ref[me["row"]]
    rowtab[128] = jnp.concatenate([jnp.full((3, 8, 128), 1.0, F32), jnp.zeros((2, 8, 128), F32)], axis=0)
    pl.semaphore_wait(barrier, N_ROW + N_COL - 2)

    def rows_of(slot):
        return pl.ds(pl.multiple_of(slot * N_COL, N_COL), N_COL)

    flag_swap = Swap(me, peers, "row", lambda peer: flags_ref.at[peer], lambda slot: flagall.at[slot], (fs, fr))
    col_swap = Swap(me, peers, "col", lambda peer: own, lambda slot: rowblk.at[pl.ds(slot, 1), :], (cs, cr))
    row_swap = Swap(me, peers, "row", lambda peer: rowblk, lambda slot: rowall.at[rows_of(slot), :], (rs, rr))

    def spread(block, slot):
        turned = jnp.transpose(block)[0:40]
        for c in range(N_COL):
            for q in range(5):
                rowtab[c * N_ROW + slot, q] = jnp.broadcast_to(turned[q * 8:(q + 1) * 8, c:c + 1], (8, 128))

    col_swap.start()
    flag_swap.start()
    for copy in copies[3:]:
        copy.wait()
    slots = lookup_slots(table_ref[...], corners_ref[...])
    codes_out[...] = slots * 32 + patch_ranks(slots >> 9).astype(I32)
    at = 0
    for line in column_rows(cen_ref[...], nor_ref[...], tan_ref[...], area_ref[...], fwd_ref[...]):
        ctab[at:at + line.shape[0], :] = line
        at += line.shape[0]
    ctab[at:, :] = jnp.zeros((ctab.shape[0] - at, ctab.shape[1]), F32)
    col_swap.receive()
    row_swap.start()
    spread(rowblk[...], me["row"])
    flag_swap.receive()
    flags = jnp.concatenate([flagall[r] for r in range(N_ROW)], axis=1).astype(F32)
    lists = make_lists(flags, BATCHES)
    for t in range(8):
        for half in range(2):
            lists_out[2 * t + half:2 * t + half + 1, :] = lists[t:t + 1, half * 128:(half + 1) * 128]
    for peer in reversed(peers["row"]):
        row_swap.copy(peer, peer).wait_recv()
        spread(rowall[rows_of(peer), :], peer)
    for swap in (col_swap, flag_swap, row_swap):
        swap.drain()


def project(modes_ref, vertex, acc_ref):
    total = None
    for comp in range(6):
        for k in range(4):
            lanes = slice(k * 128, (k + 1) * 128)
            term = modes_ref[comp, :, lanes] * vertex[comp:comp + 1, lanes]
            total = term if total is None else total + term
    acc_ref[...] = jnp.zeros(acc_ref.shape, F32)
    acc_ref[0:total.shape[0], :] = total
    ones = jnp.ones((8, 128), BF16)
    return sum(dot_nt(ones, p) for p in split3(acc_ref[...]))


def finish_kernel(col_ref, racc_ref, codes_ref, modes_hbm, vertex_out, grad_out,
                  modes, row_ref, part8, sumrow, part16, send, mid, stage, recv, acc, grad, grad8, mid_grad, grad16,
                  msem, a0, a1, b0, b1, c0, c1, d0, d1, e0, e1, f0, f1):
    me, peers = whereabouts()
    r, c = me["row"], me["col"]
    barrier = greet(peers)
    fetch = pltpu.make_async_copy(modes_hbm, modes, msem)
    fetch.start()

    def halves(ref, i):
        return ref.at[:, pl.ds(pl.multiple_of(i * N_COL, N_COL), N_COL), :]

    swap_a = Swap(me, peers, "row", lambda peer: row_ref, lambda slot: part8.at[slot], (a0, a1))
    swap_b = Swap(me, peers, "col", lambda peer: sumrow, lambda slot: part16.at[slot], (b0, b1))
    swap_c = Swap(me, peers, "row", lambda peer: halves(send, peer), lambda slot: halves(mid, slot), (c0, c1))
    swap_d = Swap(me, peers, "col", lambda peer: stage.at[peer], lambda slot: recv.at[slot], (d0, d1))
    swap_e = Swap(me, peers, "row", lambda peer: grad, lambda slot: grad8.at[slot], (e0, e1))
    swap_f = Swap(me, peers, "col", lambda peer: mid_grad, lambda slot: grad16.at[slot], (f0, f1))

    width = 256
    third = 1.0 / 3.0
    total = jnp.zeros((128, 192), F32)
    for n in range(3):
        for cb in range(col_ref.shape[1] // width):
            cols = slice(cb * width, (cb + 1) * width)
            code = codes_ref[n:n + 1, cols]
            slots = code >> 5
            element = jnp.minimum(iota((1, width), 1) + cb * width, SLAB_DEV).astype(F32)
            eight = jnp.concatenate([col_ref[:, cols] * third, (slots & 511).astype(F32), element], axis=0)
            total = total + bucket_terms(eight, slots, code & 31)
    send[0] = total[:, 0:128]
    send[1] = jnp.concatenate([total[:, 128:192], jnp.zeros((128, 64), F32)], axis=1)
    pl.semaphore_wait(barrier, N_ROW + N_COL - 2)
    swap_c.start()
    lane = iota((8, 128), 1)
    outs = [jnp.zeros((8, 128), F32) for _ in range(3)]
    for g in range(128):
        for q in range(3):
            outs[q] = jnp.where(lane == g, jnp.sum(racc_ref[g, q], axis=1, keepdims=True), outs[q])
    for q in range(3):
        row_ref[q * 8:(q + 1) * 8, :] = outs[q]
    swap_a.start()
    part8[r] = row_ref[...]
    halves(mid, r)[...] = halves(send, r)[...]
    swap_c.receive()
    for i in range(N_COL):
        for half in range(2):
            stage[i, :, half * 128:(half + 1) * 128] = mid[half, pl.ds(i, N_ROW, stride=N_COL), :]
    swap_d.start()
    recv[c] = stage[c]
    swap_a.receive()
    sumrow[...] = sum(part8[i] for i in range(N_ROW)) * third
    swap_b.start()
    part16[c] = sumrow[...]
    swap_b.receive()
    rows = sum(part16[i] for i in range(N_COL))
    swap_d.receive()
    vertex = add_up(recv[...].reshape(128, 256), rows)
    vertex_out[...] = vertex[0:6]
    fetch.wait()
    grad[...] = project(modes, vertex, acc)[0:1]
    swap_e.start()
    grad8[r] = grad[...]
    swap_e.receive()
    mid_grad[...] = sum(grad8[i] for i in range(N_ROW))
    swap_f.start()
    grad16[c] = mid_grad[...]
    swap_f.receive()
    grad_out[...] = sum(grad16[i] for i in range(N_COL))
    for swap in (swap_a, swap_b, swap_c, swap_d, swap_e, swap_f):
        swap.drain()


def emit_kernel(vertex_ref, grad_ref, vertex_out, grad_out):
    vertex_out[...] = vertex_ref[...]
    grad_out[...] = grad_ref[...].reshape(grad_ref.shape[1])[0:grad_out.shape[0]]


def body(centroid, normals, tangent, element_area, forward_field, adjoint_field, corners, slot_map, quad_order, morph_modes):
    el = centroid.shape[1]
    modes_t = jnp.transpose(morph_modes, (1, 0, 2))
    flags = jnp.transpose(quad_order[:, :, 0, :], (1, 2, 0))
    table = slot_map.reshape(512, 128)
    area = element_area[None, :]
    centroid, normals, tangent, area, forward_field, adjoint_field, corners, table, flags, modes_t = [
        pltpu.with_memory_space_constraint(x, pltpu.HBM)
        for x in (centroid, normals, tangent, area, forward_field, adjoint_field, corners, table, flags, modes_t)]
    rowtab, lists, codes, ctab = pl.pallas_call(
        gather_kernel,
        out_shape=(S((129, 5, 8, 128), F32), S((16, 128), I32), S((3, el), I32), S((24, el), F32)),
        in_specs=[HB] * 9, out_specs=(VM,) * 4,
        scratch_shapes=[pltpu.VMEM((3, el), F32), pltpu.VMEM((2, el), F32), pltpu.VMEM((8, 8, 16), I32),
                        pltpu.VMEM((512, 128), I32), pltpu.VMEM((3, el), I32), pltpu.VMEM((3, el), F32), pltpu.VMEM((3, el), F32),
                        pltpu.VMEM((1, el), F32), pltpu.VMEM((2, el), F32), DMA((9,)), pltpu.VMEM((1, 128), F32),
                        pltpu.VMEM((16, 128), F32), pltpu.VMEM((128, 128), F32),
                        pltpu.VMEM((8, 8, 16), I32)] + swap_sems(8) + swap_sems(16) + swap_sems(8),
        compiler_params=pltpu.CompilerParams(collective_id=0, has_side_effects=True, vmem_limit_bytes=16 << 20), name="gather",
    )(centroid, adjoint_field, flags, table, corners, normals, tangent, area, forward_field)
    col_part, row_part = pair_call(lists.reshape(2048), rowtab, ctab, BATCHES)
    vertex, grad = pl.pallas_call(
        finish_kernel,
        out_shape=(S((6, 512), F32), S((1, 384), F32)),
        in_specs=[VM] * 3 + [HB], out_specs=(VM, VM),
        scratch_shapes=[pltpu.VMEM((6, 300, 512), F32), pltpu.VMEM((24, 128), F32), pltpu.VMEM((8, 24, 128), F32), pltpu.VMEM((24, 128), F32),
                        pltpu.VMEM((16, 24, 128), F32), pltpu.VMEM((2, 128, 128), F32), pltpu.VMEM((2, 128, 128), F32),
                        pltpu.VMEM((16, 8, 256), F32), pltpu.VMEM((16, 8, 256), F32), pltpu.VMEM((384, 128), F32),
                        pltpu.VMEM((1, 384), F32), pltpu.VMEM((8, 1, 384), F32), pltpu.VMEM((1, 384), F32),
                        pltpu.VMEM((16, 1, 384), F32), DMA] + (swap_sems(8) + swap_sems(16)) * 3,
        compiler_params=pltpu.CompilerParams(collective_id=1, has_side_effects=True, vmem_limit_bytes=16 << 20), name="finish",
    )(col_part, row_part, codes, modes_t)
    return pl.pallas_call(emit_kernel, out_shape=(S((6, 512), F32), S((300,), F32)), in_specs=[VM] * 2, out_specs=(VM, VM),
                          compiler_params=pltpu.CompilerParams(vmem_limit_bytes=16 << 20), name="emit")(vertex, grad)


def solution(mesh):
    from jax.sharding import PartitionSpec as P
    every = ("row", "col")
    return jax.shard_map(
        body, mesh=mesh,
        in_specs=(P(None, every), P(None, every), P(None, every), P(every), P(None, every), P(None, every), P(None, every),
                  P(), P("row", None, "col", None), P(None, None, every)),
        out_specs=(P(None, every), P()), check_vma=False)
```

```python
import math, functools
import jax, jax.numpy as jnp
from jax import lax
from jax.experimental import pallas as pl
from jax.experimental.pallas import tpu as pltpu

F32 = jnp.float32
MAGIC = 12582912.0
INV_TURN = 1.0 / (2.0 * math.pi)
SIN_C = (4.442883014678955, -7.308245658874512, 3.6063544750213623, -0.8461129069328308, 0.10982698947191238)
COS_C = (1.4142135381698608, -6.978850841522217, 5.7394609451293945, -1.8835630416870117, 0.31069818139076233)


def horner(coeffs, z):
    total = z * coeffs[-1] + coeffs[-2]
    for value in coeffs[-3::-1]:
        total = total * z + value
    return total


def green(r2, cr, ci):
    inv = lax.rsqrt(r2)
    phi = r2 * inv
    turn = phi * INV_TURN
    frac = turn - jnp.round(turn)
    z = frac * frac
    hs = frac * horner(SIN_C, z)
    hc = horner(COS_C, z)
    cosine = 1.0 - hs * hs
    sine = hs * hc
    er = cr * cosine - ci * sine
    ei = cr * sine + ci * cosine
    i2 = inv * inv
    i3 = i2 * inv
    g = er + phi * ei
    h = ei - phi * er
    k = g * (3.0 * i2) - er
    return g, h, k, i3


def tile_terms(kind, row, col, cr_scale, ci_scale):
    x, y, z, ar, ai = row
    dx, dy, dz = x - col["y"][0], y - col["y"][1], z - col["y"][2]
    d = (dx, dy, dz)
    nx, ny, nz = col["n"]
    mn = dx * nx + dy * ny + dz * nz
    sq = dx * dx + dy * dy + dz * dz
    cr = ar * cr_scale + ai * ci_scale
    ci = ar * ci_scale - ai * cr_scale
    out = {}
    sa = sb = None
    if kind != 0:
        ex, ey, ez = col["t2"]
        e = dx * ex + dy * ey + dz * ez
        b = sq + col["at"]
        pts = []
        for sign in (-1, 1):
            if sign > 0:
                r2, m = b - e, mn - col["tn"]
            else:
                r2, m = b + e, mn + col["tn"]
            g, h, k, i3 = green(r2, cr, ci)
            pts.append((i3 * g, i3 * (h - m * k)))
        (a0, b0), (a2, b2) = pts
        sa, sb, da, db = a0 + a2, b0 + b2, a2 - a0, b2 - b0
    if kind != 1:
        g, h, k, i3 = green(sq + col["a"], cr, ci)
        a1, b1 = i3 * g, i3 * (h - mn * k)
        sa, sb = (a1, b1) if sa is None else (sa + a1, sb + b1)
    bd = [sb * v for v in d]
    ad = [sa * v for v in d]
    an = [sa * v for v in (nx, ny, nz)]
    pos = [p + q for p, q in zip(bd, an)]
    if kind == 0:
        return pos, pos, ad, None
    ts = col["ts"]
    pos = [p - db * t for p, t in zip(pos, ts)]
    return pos, pos, ad, da


def pair_kernel(batches, lists_ref, table, ctab, col_out, racc, colv, cacc):
    tiles = lists_ref.shape[0] // 256
    racc[...] = jnp.zeros(racc.shape, F32)

    def tile_body(t, _):
        lanes = pl.ds(pl.multiple_of(t * 128, 128), 128)
        for i in range(15):
            colv[i] = jnp.broadcast_to(ctab[i:i + 1, lanes], (8, 128))
        for kind, weight in enumerate((1.0, 0.5, 1.0 / 3.0)):
            for part in range(2):
                colv[15 + 2 * kind + part] = jnp.broadcast_to(ctab[15 + part:16 + part, lanes] * weight, (8, 128))

        def getcol():
            return dict(y=[colv[0], colv[1], colv[2]], n=[colv[3], colv[4], colv[5]], ts=[colv[6], colv[7], colv[8]],
                        t2=[colv[9], colv[10], colv[11]], a=colv[12], at=colv[13], tn=colv[14])
        zero = jnp.zeros((8, 128), F32)

        def make(kind, size):
            def body(it, state):
                pos, ids = state
                col = getcol()
                frs, fis = colv[15 + 2 * kind], colv[16 + 2 * kind]
                acc = [None] * 7
                news = []
                for j in range(size):
                    row = [table[ids[j], q] for q in range(5)]
                    gain, _, ad, da = tile_terms(kind, row, col, frs, fis)
                    for q, v in enumerate(gain + ad + [da]):
                        if v is not None:
                            acc[q] = v if acc[q] is None else acc[q] + v
                    news.append(gain)
                olds = [[racc[ids[j], q] for q in range(3)] for j in range(size)]
                for j in range(size):
                    for q in range(3):
                        racc[ids[j], q] = olds[j][q] + news[j][q]
                for q, v in enumerate(acc):
                    if v is not None:
                        cacc[q] = cacc[q] + v
                pos = pos + size
                return pos, tuple(lists_ref[pos + j] for j in range(most))
            return body
        most = max(max(sizes) for sizes in batches)
        start = t * 256
        state = (start, tuple(lists_ref[start + j] for j in range(most)))
        cacc[...] = jnp.zeros(cacc.shape, F32)
        for kind, sizes in enumerate(batches):
            for i, size in enumerate(sizes):
                state = lax.fori_loop(0, lists_ref[start + 250 + 2 * kind + i], make(kind, size), state)
        sums = [jnp.sum(cacc[q], axis=0, keepdims=True) for q in range(7)]
        for q in range(3):
            col_out[q:q + 1, lanes] = -sums[q]
            tsr = ctab[6 + q:7 + q, lanes]
            col_out[3 + q:4 + q, lanes] = 4.0 * (sums[3 + q] - sums[6] * tsr)
        return 0

    lax.fori_loop(0, tiles, tile_body, 0)

def pair_call(lists, table, ctab, batches):
    el = ctab.shape[1]
    vm = pl.BlockSpec(memory_space=pltpu.VMEM)
    return pl.pallas_call(
        functools.partial(pair_kernel, batches),
        out_shape=(jax.ShapeDtypeStruct((6, el), F32), jax.ShapeDtypeStruct((table.shape[0], 3, 8, 128), F32)),
        in_specs=[pl.BlockSpec(memory_space=pltpu.SMEM), vm, vm], out_specs=(vm, vm),
        scratch_shapes=[pltpu.VMEM((21, 8, 128), F32), pltpu.VMEM((7, 8, 128), F32)],
        compiler_params=pltpu.CompilerParams(vmem_limit_bytes=16 << 20), name="pairs",
    )(lists, table, ctab)


def dot_nn(a, b):
    return lax.dot_general(a, b, (((1,), (0,)), ((), ())), preferred_element_type=F32)


def dot_nt(a, b):
    return lax.dot_general(a, b, (((1,), (1,)), ((), ())), preferred_element_type=F32)


def iota(shape, dim):
    return lax.broadcasted_iota(jnp.int32, shape, dim)


BF16 = jnp.bfloat16


def split3(v):
    hi = v.astype(BF16)
    rest = v - hi.astype(F32)
    mid = rest.astype(BF16)
    low = (rest - mid.astype(F32)).astype(BF16)
    return hi, mid, low


def ones_where(mask):
    return jnp.where(mask, 1.0, 0.0)


def make_lists(flags, batches):
    before = ones_where(iota((128, 128), 0) < iota((128, 128), 1)).astype(BF16)
    tile = iota((8, 128), 0)
    lane = iota((8, 128), 1)
    pos = jnp.zeros((8, 128), F32)
    base = jnp.zeros((8, 1), F32)
    counts = []
    for kind in range(3):
        mask = ones_where(flags == float(kind))
        inside = dot_nn(mask.astype(BF16), before)
        total = jnp.sum(mask, axis=1, keepdims=True)
        pos = pos + mask * (inside + base)
        large, small = batches[kind]
        full = jnp.floor((total + (large - small - 0.5)) * (1.0 / large))
        tail = jnp.minimum(jnp.maximum(total - full * float(large), 0.0), 1.0)
        base = base + full * float(large) + tail * float(small)
        counts += [full, tail]
    posi = pos.astype(jnp.int32)
    slot = iota((256, 128), 0)
    out = jnp.zeros((8, 256), F32)
    for t in range(8):
        hit = ones_where(slot == posi[t:t + 1, :]).astype(BF16)
        value = jnp.where(tile == t, (((lane & 15) << 3) + (lane >> 4) - 128).astype(F32), 0.0).astype(BF16)
        out = out + dot_nt(value, hit)
    out = out + 128.0
    wide = iota((8, 256), 1)
    for i, count in enumerate(counts):
        out = jnp.where(wide == 250 + i, count, out)
    return out.astype(jnp.int32)


def lookup_slots(table, corners):
    parts = jnp.concatenate([(table >> 8).astype(F32).astype(BF16), (table & 255).astype(F32).astype(BF16)], axis=1)
    width = 256
    lo_iota = iota((128, width), 0)
    hi_iota = iota((512, width), 0)
    rows = []
    for n in range(corners.shape[0]):
        pieces = []
        for cb in range(corners.shape[1] // width):
            v = corners[n:n + 1, cb * width:(cb + 1) * width]
            hit = lo_iota == (v & 127)
            rhs = jnp.concatenate([jnp.where(hit, 256.0, 0.0), jnp.where(hit, 1.0, 0.0)], axis=0).astype(BF16)
            sel = dot_nn(parts, rhs)
            pieces.append(jnp.sum(jnp.where(hi_iota == (v >> 7), sel, 0.0), axis=0, keepdims=True))
        rows.append(jnp.concatenate(pieces, axis=1))
    return jnp.concatenate(rows, axis=0).astype(jnp.int32)


def patch_ranks(patches):
    width = 256
    before = ones_where(iota((width, width), 0) < iota((width, width), 1)).astype(BF16)
    sub = iota((128, width), 0)
    carry = jnp.zeros((128, 1), F32)
    rows = []
    for n in range(patches.shape[0]):
        pieces = []
        for cb in range(patches.shape[1] // width):
            hit = ones_where(sub == patches[n:n + 1, cb * width:(cb + 1) * width])
            earlier = dot_nn(hit.astype(BF16), before) + carry
            pieces.append(jnp.sum(hit * earlier, axis=0, keepdims=True))
            carry = carry + jnp.sum(hit, axis=1, keepdims=True)
        rows.append(jnp.concatenate(pieces, axis=1))
    return jnp.concatenate(rows, axis=0)


def bucket_terms(values, slots, ranks):
    width = values.shape[1]
    hit = ones_where(iota((128, width), 0) == (slots >> 9)).astype(BF16)
    mine = (iota((192, width), 0) >> 3) == ranks
    total = None
    for part in split3(values):
        rhs = jnp.where(mine, jnp.concatenate([part.astype(F32)] * 24, axis=0), 0.0).astype(BF16)
        term = dot_nt(hit, rhs)
        total = term if total is None else total + term
    return total


def add_up(recv, rows):
    turned = jnp.transpose(recv)
    sub = iota((128, 128), 0)
    row8 = iota((8, 128), 0)
    total = jnp.zeros((96, 128), F32)
    for pair in range(12):
        parts, hits = [], []
        for q in (2 * pair, 2 * pair + 1):
            eight = turned[q * 8:(q + 1) * 8, :]
            slot = eight[6:7, :].astype(jnp.int32)
            mine = ones_where(row8 == eight[7:8, :].astype(jnp.int32))
            for comp in range(3):
                gain = jnp.sum(mine * rows[comp * 8:(comp + 1) * 8], axis=0, keepdims=True)
                eight = eight + jnp.where(row8 == comp, gain, 0.0)
            hits.append(ones_where(sub == (slot & 127)).astype(BF16))
            quarter = slot >> 7
            parts.append(jnp.concatenate([jnp.where(quarter == k, p.astype(F32), 0.0) for p in split3(eight) for k in range(4)], axis=0))
        total = total + dot_nt(jnp.concatenate(parts, axis=1).astype(BF16), jnp.concatenate(hits, axis=1))
    total = total[0:32] + total[32:64] + total[64:96]
    return jnp.concatenate([total[8 * k:8 * k + 8] for k in range(4)], axis=1)


VM = pl.BlockSpec(memory_space=pltpu.VMEM)
HB = pl.BlockSpec(memory_space=pltpu.HBM)
SLAB_DEV = 8
BATCHES = ((8, 4), (5, 2), (5, 2))
N_ROW, N_COL = 8, 16
S = jax.ShapeDtypeStruct
I32 = jnp.int32
DMA = pltpu.SemaphoreType.DMA
MESH = pl.DeviceIdType.MESH


SIDE = 4


def far_first(inner):
    def hops(step, ring):
        return min(step, ring - step)
    steps = [(i, j) for i in range(SIDE) for j in range(inner) if (i, j) != (0, 0)]
    return sorted(steps, key=lambda s: -(hops(s[0], SIDE) * 2 + hops(s[1], inner) * (2 if inner == SIDE else 1)))


def whereabouts():
    me, peers = {}, {}
    for axis, inner in (("row", 2), ("col", SIDE)):
        here = lax.axis_index(axis)
        outer, low = here // inner, lax.rem(here, inner)
        me[axis] = here
        peers[axis] = [lax.rem(outer + i, SIDE) * inner + lax.rem(low + j, inner) for i, j in far_first(inner)]
    return me, peers


def greet(peers):
    barrier = pltpu.get_barrier_semaphore()
    for axis in ("col", "row"):
        for peer in peers[axis]:
            pl.semaphore_signal(barrier, inc=1, device_id={axis: peer}, device_id_type=MESH)
    return barrier


class Swap:
    def __init__(self, me, peers, axis, piece, slot, sems):
        self.me, self.peers, self.axis = me[axis], peers[axis], axis
        self.piece, self.slot = piece, slot
        self.send_sem, self.recv_sem = sems

    def copy(self, peer, slot):
        return pltpu.make_async_remote_copy(
            src_ref=self.piece(peer), dst_ref=self.slot(slot), send_sem=self.send_sem.at[peer], recv_sem=self.recv_sem.at[slot],
            device_id={self.axis: peer}, device_id_type=MESH)

    def start(self):
        for peer in self.peers:
            self.copy(peer, self.me).start()

    def receive(self):
        for peer in self.peers:
            self.copy(peer, peer).wait_recv()

    def drain(self):
        for peer in self.peers:
            self.copy(peer, peer).wait_send()


def swap_sems(n):
    return [DMA((n,)), DMA((n,))]


def fetch_all(sources, targets, sems):
    copies = [pltpu.make_async_copy(src, dst, sems.at[i]) for i, (src, dst) in enumerate(zip(sources, targets))]
    for copy in copies:
        copy.start()
    return copies


def column_rows(cen, nor, tan, area, fwd):
    ts = jnp.sqrt(area) * 2.4 * tan
    n16 = 16.0 * nor
    a16 = 16.0 * area
    at = a16 + jnp.sum(ts * ts, axis=0, keepdims=True)
    tn = jnp.sum(ts * n16, axis=0, keepdims=True)
    return [4.0 * cen, n16, ts, 2.0 * ts, a16, at, tn, fwd * (area * (1.0 / math.pi))]


def gather_kernel(cen_hbm, adj_hbm, flags_hbm, table_hbm, corners_hbm, nor_hbm, tan_hbm, area_hbm, fwd_hbm,
                  rowtab, lists_out, codes_out, ctab,
                  cen_ref, adj_ref, flags_ref, table_ref, corners_ref, nor_ref, tan_ref, area_ref, fwd_ref, insem,
                  own, rowblk, rowall, flagall, fs, fr, cs, cr, rs, rr):
    me, peers = whereabouts()
    barrier = greet(peers)
    copies = fetch_all((cen_hbm, adj_hbm, flags_hbm, table_hbm, corners_hbm, nor_hbm, tan_hbm, area_hbm, fwd_hbm),
                       (cen_ref, adj_ref, flags_ref, table_ref, corners_ref, nor_ref, tan_ref, area_ref, fwd_ref), insem)
    lane = iota((1, 128), 1)
    packed = jnp.zeros((1, 128), F32)
    for copy in copies[:3]:
        copy.wait()
    for q in range(5):
        line = cen_ref[q:q + 1, 0:128] * 4.0 if q < 3 else adj_ref[q - 3:q - 2, 0:128]
        if q:
            line = pltpu.roll(line, 8 * q, 1)
        packed = jnp.where((lane >> 3) == q, line, packed)
    own[...] = packed
    rowblk[pl.ds(me["col"], 1), :] = packed
    flagall[me["row"]] = flags_ref[me["row"]]
    rowtab[128] = jnp.concatenate([jnp.full((3, 8, 128), 1.0, F32), jnp.zeros((2, 8, 128), F32)], axis=0)
    pl.semaphore_wait(barrier, N_ROW + N_COL - 2)

    def rows_of(slot):
        return pl.ds(pl.multiple_of(slot * N_COL, N_COL), N_COL)

    flag_swap = Swap(me, peers, "row", lambda peer: flags_ref.at[peer], lambda slot: flagall.at[slot], (fs, fr))
    col_swap = Swap(me, peers, "col", lambda peer: own, lambda slot: rowblk.at[pl.ds(slot, 1), :], (cs, cr))
    row_swap = Swap(me, peers, "row", lambda peer: rowblk, lambda slot: rowall.at[rows_of(slot), :], (rs, rr))

    def spread(block, slot):
        turned = jnp.transpose(block)[0:40]
        for c in range(N_COL):
            for q in range(5):
                rowtab[c * N_ROW + slot, q] = jnp.broadcast_to(turned[q * 8:(q + 1) * 8, c:c + 1], (8, 128))

    col_swap.start()
    flag_swap.start()
    for copy in copies[3:]:
        copy.wait()
    slots = lookup_slots(table_ref[...], corners_ref[...])
    codes_out[...] = slots * 32 + patch_ranks(slots >> 9).astype(I32)
    at = 0
    for line in column_rows(cen_ref[...], nor_ref[...], tan_ref[...], area_ref[...], fwd_ref[...]):
        ctab[at:at + line.shape[0], :] = line
        at += line.shape[0]
    ctab[at:, :] = jnp.zeros((ctab.shape[0] - at, ctab.shape[1]), F32)
    col_swap.receive()
    row_swap.start()
    spread(rowblk[...], me["row"])
    flag_swap.receive()
    flags = jnp.concatenate([flagall[r] for r in range(N_ROW)], axis=1).astype(F32)
    lists = make_lists(flags, BATCHES)
    for t in range(8):
        for half in range(2):
            lists_out[2 * t + half:2 * t + half + 1, :] = lists[t:t + 1, half * 128:(half + 1) * 128]
    for peer in reversed(peers["row"]):
        row_swap.copy(peer, peer).wait_recv()
        spread(rowall[rows_of(peer), :], peer)
    for swap in (col_swap, flag_swap, row_swap):
        swap.drain()


def project(modes_ref, vertex, acc_ref):
    total = None
    for comp in range(6):
        for k in range(4):
            lanes = slice(k * 128, (k + 1) * 128)
            term = modes_ref[comp, :, lanes] * vertex[comp:comp + 1, lanes]
            total = term if total is None else total + term
    acc_ref[...] = jnp.zeros(acc_ref.shape, F32)
    acc_ref[0:total.shape[0], :] = total
    ones = jnp.ones((8, 128), BF16)
    return sum(dot_nt(ones, p) for p in split3(acc_ref[...]))


def finish_kernel(col_ref, racc_ref, codes_ref, modes_hbm, vertex_out, grad_out,
                  modes, row_ref, part8, sumrow, part16, send, mid, stage, recv, acc, grad, grad8, mid_grad, grad16,
                  msem, a0, a1, b0, b1, c0, c1, d0, d1, e0, e1, f0, f1):
    me, peers = whereabouts()
    r, c = me["row"], me["col"]
    barrier = greet(peers)
    fetch = pltpu.make_async_copy(modes_hbm, modes, msem)
    fetch.start()

    def halves(ref, i):
        return ref.at[:, pl.ds(pl.multiple_of(i * N_COL, N_COL), N_COL), :]

    swap_a = Swap(me, peers, "row", lambda peer: row_ref, lambda slot: part8.at[slot], (a0, a1))
    swap_b = Swap(me, peers, "col", lambda peer: sumrow, lambda slot: part16.at[slot], (b0, b1))
    swap_c = Swap(me, peers, "row", lambda peer: halves(send, peer), lambda slot: halves(mid, slot), (c0, c1))
    swap_d = Swap(me, peers, "col", lambda peer: stage.at[peer], lambda slot: recv.at[slot], (d0, d1))
    swap_e = Swap(me, peers, "row", lambda peer: grad, lambda slot: grad8.at[slot], (e0, e1))
    swap_f = Swap(me, peers, "col", lambda peer: mid_grad, lambda slot: grad16.at[slot], (f0, f1))

    lane = iota((8, 128), 1)
    outs = [jnp.zeros((8, 128), F32) for _ in range(3)]
    for g in range(128):
        for q in range(3):
            outs[q] = jnp.where(lane == g, jnp.sum(racc_ref[g, q], axis=1, keepdims=True), outs[q])
    for q in range(3):
        row_ref[q * 8:(q + 1) * 8, :] = outs[q]
    width = 256
    third = 1.0 / 3.0
    total = jnp.zeros((128, 192), F32)
    for n in range(3):
        for cb in range(col_ref.shape[1] // width):
            cols = slice(cb * width, (cb + 1) * width)
            code = codes_ref[n:n + 1, cols]
            slots = code >> 5
            element = jnp.minimum(iota((1, width), 1) + cb * width, SLAB_DEV).astype(F32)
            eight = jnp.concatenate([col_ref[:, cols] * third, (slots & 511).astype(F32), element], axis=0)
            total = total + bucket_terms(eight, slots, code & 31)
    send[0] = total[:, 0:128]
    send[1] = jnp.concatenate([total[:, 128:192], jnp.zeros((128, 64), F32)], axis=1)
    pl.semaphore_wait(barrier, N_ROW + N_COL - 2)
    swap_a.start()
    swap_c.start()
    part8[r] = row_ref[...]
    halves(mid, r)[...] = halves(send, r)[...]
    swap_a.receive()
    sumrow[...] = sum(part8[i] for i in range(N_ROW)) * third
    swap_b.start()
    part16[c] = sumrow[...]
    swap_c.receive()
    for i in range(N_COL):
        for half in range(2):
            stage[i, :, half * 128:(half + 1) * 128] = mid[half, pl.ds(i, N_ROW, stride=N_COL), :]
    swap_d.start()
    recv[c] = stage[c]
    swap_b.receive()
    rows = sum(part16[i] for i in range(N_COL))
    swap_d.receive()
    vertex = add_up(recv[...].reshape(128, 256), rows)
    vertex_out[...] = vertex[0:6]
    fetch.wait()
    grad[...] = project(modes, vertex, acc)[0:1]
    swap_e.start()
    grad8[r] = grad[...]
    swap_e.receive()
    mid_grad[...] = sum(grad8[i] for i in range(N_ROW))
    swap_f.start()
    grad16[c] = mid_grad[...]
    swap_f.receive()
    grad_out[...] = sum(grad16[i] for i in range(N_COL))
    for swap in (swap_a, swap_b, swap_c, swap_d, swap_e, swap_f):
        swap.drain()


def emit_kernel(vertex_ref, grad_ref, vertex_out, grad_out):
    vertex_out[...] = vertex_ref[...]
    grad_out[...] = grad_ref[...].reshape(grad_ref.shape[1])[0:grad_out.shape[0]]


def body(centroid, normals, tangent, element_area, forward_field, adjoint_field, corners, slot_map, quad_order, morph_modes):
    el = centroid.shape[1]
    modes_t = jnp.transpose(morph_modes, (1, 0, 2))
    flags = jnp.transpose(quad_order[:, :, 0, :], (1, 2, 0))
    table = slot_map.reshape(512, 128)
    area = element_area[None, :]
    centroid, normals, tangent, area, forward_field, adjoint_field, corners, table, flags, modes_t = [
        pltpu.with_memory_space_constraint(x, pltpu.HBM)
        for x in (centroid, normals, tangent, area, forward_field, adjoint_field, corners, table, flags, modes_t)]
    rowtab, lists, codes, ctab = pl.pallas_call(
        gather_kernel,
        out_shape=(S((129, 5, 8, 128), F32), S((16, 128), I32), S((3, el), I32), S((24, el), F32)),
        in_specs=[HB] * 9, out_specs=(VM,) * 4,
        scratch_shapes=[pltpu.VMEM((3, el), F32), pltpu.VMEM((2, el), F32), pltpu.VMEM((8, 8, 16), I32),
                        pltpu.VMEM((512, 128), I32), pltpu.VMEM((3, el), I32), pltpu.VMEM((3, el), F32), pltpu.VMEM((3, el), F32),
                        pltpu.VMEM((1, el), F32), pltpu.VMEM((2, el), F32), DMA((9,)), pltpu.VMEM((1, 128), F32),
                        pltpu.VMEM((16, 128), F32), pltpu.VMEM((128, 128), F32),
                        pltpu.VMEM((8, 8, 16), I32)] + swap_sems(8) + swap_sems(16) + swap_sems(8),
        compiler_params=pltpu.CompilerParams(collective_id=0, has_side_effects=True, vmem_limit_bytes=16 << 20), name="gather",
    )(centroid, adjoint_field, flags, table, corners, normals, tangent, area, forward_field)
    col_part, row_part = pair_call(lists.reshape(2048), rowtab, ctab, BATCHES)
    vertex, grad = pl.pallas_call(
        finish_kernel,
        out_shape=(S((6, 512), F32), S((1, 384), F32)),
        in_specs=[VM] * 3 + [HB], out_specs=(VM, VM),
        scratch_shapes=[pltpu.VMEM((6, 300, 512), F32), pltpu.VMEM((24, 128), F32), pltpu.VMEM((8, 24, 128), F32), pltpu.VMEM((24, 128), F32),
                        pltpu.VMEM((16, 24, 128), F32), pltpu.VMEM((2, 128, 128), F32), pltpu.VMEM((2, 128, 128), F32),
                        pltpu.VMEM((16, 8, 256), F32), pltpu.VMEM((16, 8, 256), F32), pltpu.VMEM((384, 128), F32),
                        pltpu.VMEM((1, 384), F32), pltpu.VMEM((8, 1, 384), F32), pltpu.VMEM((1, 384), F32),
                        pltpu.VMEM((16, 1, 384), F32), DMA] + (swap_sems(8) + swap_sems(16)) * 3,
        compiler_params=pltpu.CompilerParams(collective_id=1, has_side_effects=True, vmem_limit_bytes=16 << 20), name="finish",
    )(col_part, row_part, codes, modes_t)
    return pl.pallas_call(emit_kernel, out_shape=(S((6, 512), F32), S((300,), F32)), in_specs=[VM] * 2, out_specs=(VM, VM),
                          compiler_params=pltpu.CompilerParams(vmem_limit_bytes=16 << 20), name="emit")(vertex, grad)


def solution(mesh):
    from jax.sharding import PartitionSpec as P
    every = ("row", "col")
    return jax.shard_map(
        body, mesh=mesh,
        in_specs=(P(None, every), P(None, every), P(None, every), P(every), P(None, every), P(None, every), P(None, every),
                  P(), P("row", None, "col", None), P(None, None, every)),
        out_specs=(P(None, every), P()), check_vma=False)
```
